32 devices in a mesh: dp: 4 (over y, core), context: 2 (over x), tensor: 4 (over z).
Axes of the slice: x: 2, y: 2, z: 4, core: 2. Of those that a mesh axis runs over, the one named last changes fastest.
Arguments:
- frames: float32 [2, 4, 1024, 1536], P(None, 'dp', 'context'), may hold values from -6 to 6
- text_states: bfloat16 [2, 4, 64, 1536], P(None, 'dp'), may hold values from -6 to 6
- cotangent: float32 [2, 4, 1024, 1536], P(None, 'dp', 'context'), may hold values from -6 to 6
- clip_live: int32 [2, 4], P(None, 'dp'), may hold values 0 or 1
- first_gain: bfloat16 [1536], P(('dp', 'context')), may hold values from 0.5 to 1.5
- first_bias: bfloat16 [1536], P(('dp', 'context')), may hold values from -1 to 1
- second_gain: bfloat16 [1536], P(('dp', 'context')), may hold values from 0.5 to 1.5
- second_bias: bfloat16 [1536], P(('dp', 'context')), may hold values from -1 to 1
- third_gain: bfloat16 [1536], P(('dp', 'context')), may hold values from 0.5 to 1.5
- third_bias: bfloat16 [1536], P(('dp', 'context')), may hold values from -1 to 1
- self_query: bfloat16 [1536, 1536], P(('dp', 'context'), 'tensor'), may hold values from -0.21875 to 0.21875
- self_key: bfloat16 [1536, 1536], P(('dp', 'context'), 'tensor'), may hold values from -0.15625 to 0.15625
- self_value: bfloat16 [1536, 1536], P(('dp', 'context'), 'tensor'), may hold values from -0.15625 to 0.15625
- self_output: bfloat16 [1536, 1536], P('tensor', ('dp', 'context')), may hold values from -0.625 to 0.625
- cross_query: bfloat16 [1536, 1536], P(('dp', 'context'), 'tensor'), may hold values from -0.21875 to 0.21875
- cross_key: bfloat16 [1536, 1536], P(('dp', 'context'), 'tensor'), may hold values from -0.15625 to 0.15625
- cross_value: bfloat16 [1536, 1536], P(('dp', 'context'), 'tensor'), may hold values from -0.15625 to 0.15625
- cross_output: bfloat16 [1536, 1536], P('tensor', ('dp', 'context')), may hold values from -0.3125 to 0.3125
- hidden_up: bfloat16 [1536, 6144], P(('dp', 'context'), 'tensor'), may hold values from -0.15625 to 0.15625
- hidden_down: bfloat16 [6144, 1536], P('tensor', ('dp', 'context')), may hold values from -0.078125 to 0.078125
Outputs:
- out_frames: float32 [2, 4, 1024, 1536], P(None, 'dp', 'context')
- frames_grad: float32 [2, 4, 1024, 1536], P(None, 'dp', 'context')
- text_grad: float32 [2, 4, 64, 1536], P(None, 'dp', 'context', 'tensor')
- grad_first_gain: float32 [1536], P(('dp', 'context'))
- grad_first_bias: float32 [1536], P(('dp', 'context'))
- grad_second_gain: float32 [1536], P(('dp', 'context'))
- grad_second_bias: float32 [1536], P(('dp', 'context'))
- grad_third_gain: float32 [1536], P(('dp', 'context'))
- grad_third_bias: float32 [1536], P(('dp', 'context'))
- grad_self_query: float32 [1536, 1536], P(('dp', 'context'), 'tensor')
- grad_self_key: float32 [1536, 1536], P(('dp', 'context'), 'tensor')
- grad_self_value: float32 [1536, 1536], P(('dp', 'context'), 'tensor')
- grad_self_output: float32 [1536, 1536], P('tensor', ('dp', 'context'))
- grad_cross_query: float32 [1536, 1536], P(('dp', 'context'), 'tensor')
- grad_cross_key: float32 [1536, 1536], P(('dp', 'context'), 'tensor')
- grad_cross_value: float32 [1536, 1536], P(('dp', 'context'), 'tensor')
- grad_cross_output: float32 [1536, 1536], P('tensor', ('dp', 'context'))
- grad_hidden_up: float32 [1536, 6144], P(('dp', 'context'), 'tensor')
- grad_hidden_down: float32 [6144, 1536], P('tensor', ('dp', 'context'))
The draws below stay inside these ranges and needn't reach their ends.
All inputs are finite; a program needn't handle non-finite values. No bound on the sum of `clip_live` on one device may be relied on, other than what follows from the above.
Results may differ from the reference program's by a relative error of at most 0.03.
Values may be sent and summed in bfloat16 or wider, within the bound.
No kernel may reach another device: no remote copies, remote signals or barrier semaphores. Data moves between devices by JAX's collectives and lax.ppermute only.
A program may use at most 256 MiB of HBM per device.

```python
import jax
import jax.numpy as jnp
from jax import lax

D = 1536
HEADS = 24
HD = 64
FF = 6144
TXT = 64
MB = 2
LEN = 1024
CLIPS = 4


def plant(entries, rng, least, high):
    place = [jax.random.randint(jax.random.fold_in(rng, axis), (), 0, length) for axis, length in enumerate(entries.shape)]
    main_axis = entries.shape.index(max(entries.shape))
    neighbour = place[:main_axis] + [(place[main_axis] + 1) % entries.shape[main_axis]] + place[main_axis + 1:]
    return entries.at[tuple(place)].set(least).at[tuple(neighbour)].set(high)


def level_of(stream_key, extent, shards, low, largest):
    factor_of = 1.0
    for position, parts in shards:
        steps = jax.random.uniform(jax.random.fold_in(jax.random.fold_in(stream_key, 6), position), (parts,), jnp.float32, low / len(shards), largest / len(shards))
        factor_of = factor_of * jnp.repeat(jnp.exp(steps), extent[position] // parts).reshape((-1,) + (1,) * (len(extent) - 1 - position))
    return factor_of


def bell_draw(rng, shape, scale, most, cuts=(), dtype=jnp.bfloat16):
    result = jax.random.normal(rng, shape, jnp.float32) * scale
    if len(cuts) > 0:
        result = level_of(rng, shape, cuts, -0.22, 0.18) * result
    return jnp.clip(result, min=-most, max=most).astype(dtype)


def setup_inputs(seed: int = 0) -> dict:
    key_list = jax.random.split(jax.random.key(seed), 21)
    frames = bell_draw(key_list[0], (MB, CLIPS, LEN, D), 1.0, 6.0, ((1, 4), (2, 2)), jnp.float32)
    text_states = bell_draw(key_list[1], (MB, CLIPS, TXT, D), 1.0, 6.0, ((1, 4),))
    cotangent = bell_draw(key_list[2], (MB, CLIPS, LEN, D), 1.0, 6.0, ((1, 4), (2, 2)), jnp.float32)
    clip_live = plant((jax.random.randint(key_list[3], (MB, CLIPS), 0, 4) < 3).astype(jnp.int32), jax.random.fold_in(key_list[3], 1), 0, 1)
    first_gain = jnp.clip(1.0 + 0.1 * jax.random.normal(key_list[4], (D,), jnp.float32), 0.5, 1.5).astype(jnp.bfloat16)
    first_bias = bell_draw(key_list[5], (D,), 0.2, 1.0, ((0, 8),))
    second_gain = jnp.clip(1.0 + 0.1 * jax.random.normal(key_list[6], (D,), jnp.float32), 0.5, 1.5).astype(jnp.bfloat16)
    second_bias = bell_draw(key_list[7], (D,), 0.2, 1.0, ((0, 8),))
    third_gain = jnp.clip(1.0 + 0.1 * jax.random.normal(key_list[8], (D,), jnp.float32), 0.5, 1.5).astype(jnp.bfloat16)
    third_bias = bell_draw(key_list[9], (D,), 0.2, 1.0, ((0, 8),))
    self_query = bell_draw(key_list[10], (D, D), (D // 2) ** -0.5, 0.21875, ((0, 8), (1, 4)))
    self_key = bell_draw(key_list[11], (D, D), D ** -0.5, 0.15625, ((0, 8), (1, 4)))
    self_value = bell_draw(key_list[12], (D, D), D ** -0.5, 0.15625, ((0, 8), (1, 4)))
    self_output = bell_draw(key_list[13], (D, D), (D // 16) ** -0.5, 0.625, ((0, 4), (1, 8)))
    cross_query = bell_draw(key_list[14], (D, D), (D // 2) ** -0.5, 0.21875, ((0, 8), (1, 4)))
    cross_key = bell_draw(key_list[15], (D, D), D ** -0.5, 0.15625, ((0, 8), (1, 4)))
    cross_value = bell_draw(key_list[16], (D, D), D ** -0.5, 0.15625, ((0, 8), (1, 4)))
    cross_output = bell_draw(key_list[17], (D, D), (D // 4) ** -0.5, 0.3125, ((0, 4), (1, 8)))
    hidden_up = bell_draw(key_list[18], (D, FF), D ** -0.5, 0.15625, ((0, 8), (1, 4)))
    hidden_down = bell_draw(key_list[19], (FF, D), FF ** -0.5, 0.078125, ((0, 4), (1, 8)))
    return dict(frames=frames, text_states=text_states, cotangent=cotangent, clip_live=clip_live, first_gain=first_gain, first_bias=first_bias, second_gain=second_gain, second_bias=second_bias, third_gain=third_gain, third_bias=third_bias, self_query=self_query, self_key=self_key, self_value=self_value, self_output=self_output, cross_query=cross_query, cross_key=cross_key, cross_value=cross_value, cross_output=cross_output, hidden_up=hidden_up, hidden_down=hidden_down)


epsilon = 1e-05
masked_score = -1e+30
highest = lax.Precision.HIGHEST

@jax.custom_vjp
def low(v):
    return lax.optimization_barrier(v.astype(jnp.bfloat16)).astype(jnp.float32)

@jax.custom_vjp
def low_back(v):
    return v

def low_keep(v):
    return (low(v), None)

def low_pass(kept, grad):
    return (grad,)

def back_keep(v):
    return (v, None)

def back_low(kept, grad):
    return (low(grad),)
low.defvjp(low_keep, low_pass)
low_back.defvjp(back_keep, back_low)

def rounded(values):
    return low_back(low(values))

def product(former, latter):
    return jnp.dot(former, latter, precision=highest)

def layer_norm(values, norm_gain, norm_shift):
    centre = values - lax.optimization_barrier(jnp.mean(values, axis=-1, keepdims=True))
    spread = lax.optimization_barrier(jnp.mean(centre * centre, axis=-1, keepdims=True))
    return centre * lax.rsqrt(spread + epsilon) * norm_gain + norm_shift

def attend(queries, key_rows, value_rows, causal):
    query_heads = queries.reshape(queries.shape[0], HEADS, HD)
    key_heads = key_rows.reshape(key_rows.shape[0], HEADS, HD)
    value_heads = value_rows.reshape(value_rows.shape[0], HEADS, HD)
    scores = jnp.einsum('ihd,jhd->hij', query_heads, key_heads, precision=highest) * HD ** (-0.5)
    if causal:
        shape_ij = (queries.shape[0], key_rows.shape[0])
        query_pos = lax.broadcasted_iota(jnp.int32, shape_ij, 0)
        key_pos = lax.broadcasted_iota(jnp.int32, shape_ij, 1)
        scores = jnp.where(key_pos <= query_pos, scores, masked_score)
    weights = jax.nn.softmax(low_back(scores), axis=-1)
    mixed = jnp.einsum('hij,jhd->ihd', low(weights), value_heads, precision=highest)
    return mixed.reshape(queries.shape[0], HEADS * HD)

def clip_layer(params, frame_rows, text_rows):
    first_gain, first_bias, second_gain, second_bias, third_gain, third_bias, self_query, self_key, self_value, self_output, cross_query, cross_key, cross_value, cross_output, hidden_up, hidden_down = params
    normed = low(layer_norm(frame_rows, first_gain, first_bias))
    mixed = rounded(attend(rounded(product(normed, self_query)), rounded(product(normed, self_key)), rounded(product(normed, self_value)), True))
    after_self = frame_rows + low_back(product(mixed, self_output))
    normed = low(layer_norm(after_self, second_gain, second_bias))
    crossed = rounded(attend(rounded(product(normed, cross_query)), rounded(product(text_rows, cross_key)), rounded(product(text_rows, cross_value)), False))
    after_cross = after_self + low_back(product(crossed, cross_output))
    normed = low(layer_norm(after_cross, third_gain, third_bias))
    activated = low(jax.nn.gelu(low_back(product(normed, hidden_up)), approximate=False))
    return after_cross + low_back(product(activated, hidden_down))

def reference(frames, text_states, cotangent, clip_live, first_gain, first_bias, second_gain, second_bias, third_gain, third_bias, self_query, self_key, self_value, self_output, cross_query, cross_key, cross_value, cross_output, hidden_up, hidden_down):
    weights_in = (first_gain, first_bias, second_gain, second_bias, third_gain, third_bias, self_query, self_key, self_value, self_output, cross_query, cross_key, cross_value, cross_output, hidden_up, hidden_down)
    params = tuple((member.astype(jnp.float32) for member in weights_in))

    def forward(layer_params, frame_values, text_values):
        flat_frames = frame_values.reshape(MB * CLIPS, LEN, D)
        flat_text = text_values.reshape(MB * CLIPS, TXT, D)

        def one_clip(clip_pair):
            return clip_layer(layer_params, clip_pair[0], clip_pair[1])
        results = lax.map(jax.checkpoint(one_clip), (flat_frames, flat_text))
        return results.reshape(MB, CLIPS, LEN, D)
    out_frames, pullback = jax.vjp(forward, params, frames, text_states.astype(jnp.float32))
    live_weight = clip_live.astype(jnp.float32)[:, :, None, None]
    param_grads, frames_grad, text_grad = pullback(cotangent * live_weight)
    return (out_frames, frames_grad, text_grad, param_grads[0], param_grads[1], param_grads[2], param_grads[3], param_grads[4], param_grads[5], param_grads[6], param_grads[7], param_grads[8], param_grads[9], param_grads[10], param_grads[11], param_grads[12], param_grads[13], param_grads[14], param_grads[15])
```

```python
import jax
import jax.numpy as jnp
from jax import lax
from jax.sharding import PartitionSpec as P

HD = 64


epsilon = 1e-05
masked_score = -1e30


def layer_norm(values, norm_gain, norm_shift):
    centre = values - jnp.mean(values, axis=-1, keepdims=True)
    spread = jnp.mean(centre * centre, axis=-1, keepdims=True)
    return centre * lax.rsqrt(spread + epsilon) * norm_gain + norm_shift


def exact_gelu(values):
    return jax.nn.gelu(values, approximate=False)


def matmul(former, latter):
    return jnp.dot(former, latter, preferred_element_type=jnp.float32)


def against(former, latter):
    return lax.dot_general(
        former, latter, (((former.ndim - 1,), (1,)), ((), ())), preferred_element_type=jnp.float32
    )


def outer_sum(former, latter):
    flat_former = former.reshape(-1, former.shape[-1])
    flat_latter = latter.reshape(-1, latter.shape[-1])
    return lax.dot_general(
        flat_former, flat_latter, (((0,), (0,)), ((), ())), preferred_element_type=jnp.float32
    )


def split_heads(values):
    return values.reshape(values.shape[0], values.shape[1], values.shape[2] // HD, HD)


def join_heads(values):
    return values.reshape(values.shape[0], values.shape[1], values.shape[2] * values.shape[3])


def head_scores(queries, key_rows, offset, causal, key_offset=0):
    scores = jnp.einsum(
        "cihd,cjhd->chij",
        split_heads(queries),
        split_heads(key_rows),
        preferred_element_type=jnp.float32,
    ) * HD ** (-0.5)
    if causal:
        shape_ij = (queries.shape[1], key_rows.shape[1])
        query_pos = offset + lax.broadcasted_iota(jnp.int32, shape_ij, 0)
        key_pos = key_offset + lax.broadcasted_iota(jnp.int32, shape_ij, 1)
        scores = jnp.where(key_pos <= query_pos, scores, masked_score)
    return scores


def softmax_parts(scores):
    top_score = jnp.max(scores, axis=-1, keepdims=True)
    scaled = jnp.exp(scores - top_score)
    row_total = jnp.sum(scaled, axis=-1, keepdims=True)
    return (scaled / row_total, top_score + jnp.log(row_total))


def mix_heads(weights, value_rows):
    return join_heads(
        jnp.einsum(
            "chij,cjhd->cihd", weights, split_heads(value_rows), preferred_element_type=jnp.float32
        )
    )


def attention_back(queries, key_rows, value_rows, grad_mixed, log_total, offset, causal):
    probability = jnp.exp(head_scores(queries, key_rows, offset, causal) - log_total)
    grad_probs = jnp.einsum(
        "cihd,cjhd->chij",
        split_heads(grad_mixed),
        split_heads(value_rows),
        preferred_element_type=jnp.float32,
    )
    inner_sum = jnp.sum(grad_probs * probability, axis=-1, keepdims=True)
    grad_scores = (probability * (grad_probs - inner_sum)).astype(jnp.bfloat16)
    score_scale = HD ** (-0.5)
    grad_queries = join_heads(
        jnp.einsum(
            "chij,cjhd->cihd",
            grad_scores,
            split_heads(key_rows),
            preferred_element_type=jnp.float32,
        )
        * score_scale
    )
    grad_keys = join_heads(
        jnp.einsum(
            "chij,cihd->cjhd", grad_scores, split_heads(queries), preferred_element_type=jnp.float32
        )
        * score_scale
    )
    grad_values = join_heads(
        jnp.einsum(
            "chij,cihd->cjhd",
            probability.astype(jnp.bfloat16),
            split_heads(grad_mixed),
            preferred_element_type=jnp.float32,
        )
    )
    return (grad_queries.astype(jnp.bfloat16), inner_sum, grad_keys, grad_values)


def branch_sum(values):
    return lax.psum(values, "tensor")


def back_sum(values):
    return lax.psum(values.astype(jnp.bfloat16), "tensor").astype(jnp.float32)


def reduce_grads(row_terms, col_terms):
    row_sums = (
        lax.psum_scatter(
            row_terms[0].astype(jnp.bfloat16), ("dp", "context"), scatter_dimension=0, tiled=True
        ).astype(jnp.float32),
        lax.psum_scatter(
            row_terms[1].astype(jnp.bfloat16), ("dp", "context"), scatter_dimension=0, tiled=True
        ).astype(jnp.float32),
        lax.psum_scatter(
            row_terms[2].astype(jnp.bfloat16), ("dp", "context"), scatter_dimension=0, tiled=True
        ).astype(jnp.float32),
        lax.psum_scatter(
            row_terms[3].astype(jnp.bfloat16), ("dp", "context"), scatter_dimension=0, tiled=True
        ).astype(jnp.float32),
        lax.psum_scatter(
            row_terms[4].astype(jnp.bfloat16), ("dp", "context"), scatter_dimension=0, tiled=True
        ).astype(jnp.float32),
        lax.psum_scatter(
            row_terms[5].astype(jnp.bfloat16), ("dp", "context"), scatter_dimension=0, tiled=True
        ).astype(jnp.float32),
        lax.psum_scatter(
            row_terms[6].astype(jnp.bfloat16), ("dp", "context"), scatter_dimension=0, tiled=True
        ).astype(jnp.float32),
        lax.psum_scatter(
            row_terms[7].astype(jnp.bfloat16), ("dp", "context"), scatter_dimension=0, tiled=True
        ).astype(jnp.float32),
        lax.psum_scatter(
            row_terms[8].astype(jnp.bfloat16), ("dp", "context"), scatter_dimension=0, tiled=True
        ).astype(jnp.float32),
        lax.psum_scatter(
            row_terms[9].astype(jnp.bfloat16), ("dp", "context"), scatter_dimension=0, tiled=True
        ).astype(jnp.float32),
        lax.psum_scatter(
            row_terms[10].astype(jnp.bfloat16), ("dp", "context"), scatter_dimension=0, tiled=True
        ).astype(jnp.float32),
        lax.psum_scatter(
            row_terms[11].astype(jnp.bfloat16), ("dp", "context"), scatter_dimension=0, tiled=True
        ).astype(jnp.float32),
        lax.psum_scatter(
            row_terms[12].astype(jnp.bfloat16), ("dp", "context"), scatter_dimension=0, tiled=True
        ).astype(jnp.float32),
    )
    col_sums = (
        lax.psum_scatter(
            col_terms[0].astype(jnp.bfloat16), ("dp", "context"), scatter_dimension=1, tiled=True
        ).astype(jnp.float32),
        lax.psum_scatter(
            col_terms[1].astype(jnp.bfloat16), ("dp", "context"), scatter_dimension=1, tiled=True
        ).astype(jnp.float32),
        lax.psum_scatter(
            col_terms[2].astype(jnp.bfloat16), ("dp", "context"), scatter_dimension=1, tiled=True
        ).astype(jnp.float32),
    )
    return (row_sums, col_sums)


def general_shards(
    frames,
    text_states,
    cotangent,
    clip_live,
    first_gain,
    first_bias,
    second_gain,
    second_bias,
    third_gain,
    third_bias,
    self_query,
    self_key,
    self_value,
    self_output,
    cross_query,
    cross_key,
    cross_value,
    cross_output,
    hidden_up,
    hidden_down,
):
    row_weights = (
        lax.all_gather(first_gain, ("dp", "context"), axis=0, tiled=True),
        lax.all_gather(first_bias, ("dp", "context"), axis=0, tiled=True),
        lax.all_gather(second_gain, ("dp", "context"), axis=0, tiled=True),
        lax.all_gather(second_bias, ("dp", "context"), axis=0, tiled=True),
        lax.all_gather(third_gain, ("dp", "context"), axis=0, tiled=True),
        lax.all_gather(third_bias, ("dp", "context"), axis=0, tiled=True),
        lax.all_gather(self_query, ("dp", "context"), axis=0, tiled=True),
        lax.all_gather(self_key, ("dp", "context"), axis=0, tiled=True),
        lax.all_gather(self_value, ("dp", "context"), axis=0, tiled=True),
        lax.all_gather(cross_query, ("dp", "context"), axis=0, tiled=True),
        lax.all_gather(cross_key, ("dp", "context"), axis=0, tiled=True),
        lax.all_gather(cross_value, ("dp", "context"), axis=0, tiled=True),
        lax.all_gather(hidden_up, ("dp", "context"), axis=0, tiled=True),
    )
    col_weights = (
        lax.all_gather(self_output, ("dp", "context"), axis=1, tiled=True),
        lax.all_gather(cross_output, ("dp", "context"), axis=1, tiled=True),
        lax.all_gather(hidden_down, ("dp", "context"), axis=1, tiled=True),
    )
    norm_params = [member.astype(jnp.float32) for member in row_weights[:6]]
    query_full, key_full, value_full = (row_weights[6], row_weights[7], row_weights[8])
    cross_query_full, cross_key_full, cross_value_full = (
        row_weights[9],
        row_weights[10],
        row_weights[11],
    )
    up_full = row_weights[12]
    output_full, cross_output_full, down_full = col_weights
    context_index = lax.axis_index("context")
    offset = context_index * frames.shape[2]
    text_share = text_states.shape[2] // lax.axis_size("context")
    row_total = None
    col_total = None
    outputs = []
    input_grads = []
    text_grads = []
    for micro_batch in range(frames.shape[0]):
        block = frames[micro_batch]
        text_block = text_states[micro_batch]
        normed_first, first_back = jax.vjp(layer_norm, block, norm_params[0], norm_params[1])
        normed_one = normed_first.astype(jnp.bfloat16)
        queries = matmul(normed_one, query_full).astype(jnp.bfloat16)
        key_local = matmul(normed_one, key_full).astype(jnp.bfloat16)
        value_local = matmul(normed_one, value_full).astype(jnp.bfloat16)
        key_rows, value_rows = (
            lax.all_gather(key_local, "context", axis=1, tiled=True),
            lax.all_gather(value_local, "context", axis=1, tiled=True),
        )
        probability, log_total = softmax_parts(head_scores(queries, key_rows, offset, True))
        mixed = mix_heads(probability.astype(jnp.bfloat16), value_rows).astype(jnp.bfloat16)
        after_self = block + branch_sum(matmul(mixed, output_full))
        normed_second, second_back = jax.vjp(layer_norm, after_self, norm_params[2], norm_params[3])
        normed_two = normed_second.astype(jnp.bfloat16)
        cross_queries = matmul(normed_two, cross_query_full).astype(jnp.bfloat16)
        text_keys = matmul(text_block, cross_key_full).astype(jnp.bfloat16)
        text_values = matmul(text_block, cross_value_full).astype(jnp.bfloat16)
        cross_probs, cross_total = softmax_parts(head_scores(cross_queries, text_keys, 0, False))
        crossed = mix_heads(cross_probs.astype(jnp.bfloat16), text_values).astype(jnp.bfloat16)
        after_cross = after_self + branch_sum(matmul(crossed, cross_output_full))
        normed_third, third_back = jax.vjp(layer_norm, after_cross, norm_params[4], norm_params[5])
        normed_three = normed_third.astype(jnp.bfloat16)
        inner = matmul(normed_three, up_full)
        gelu_value, gelu_back = jax.vjp(exact_gelu, inner)
        activated = gelu_value.astype(jnp.bfloat16)
        outputs.append(after_cross + branch_sum(matmul(activated, down_full)))
        live_weight = clip_live[micro_batch].astype(jnp.float32)[:, None, None]
        grad_result = cotangent[micro_batch] * live_weight
        grad_branch = grad_result.astype(jnp.bfloat16)
        grad_down = outer_sum(activated, grad_branch)
        grad_inner = gelu_back(against(grad_branch, down_full))[0].astype(jnp.bfloat16)
        grad_up = outer_sum(normed_three, grad_inner)
        grad_cross_in, grad_gain_three, grad_bias_three = third_back(
            back_sum(against(grad_inner, up_full))
        )
        grad_after_cross = grad_result + grad_cross_in
        grad_branch = grad_after_cross.astype(jnp.bfloat16)
        grad_cross_output = outer_sum(crossed, grad_branch)
        grad_crossed = against(grad_branch, cross_output_full).astype(jnp.bfloat16)
        grad_cross_act, cross_inner, text_key_part, text_value_part = attention_back(
            cross_queries, text_keys, text_values, grad_crossed, cross_total, 0, False
        )
        text_key_sum, text_value_sum = (
            lax.psum_scatter(
                text_key_part.astype(jnp.bfloat16), "context", scatter_dimension=1, tiled=True
            ).astype(jnp.float32),
            lax.psum_scatter(
                text_value_part.astype(jnp.bfloat16), "context", scatter_dimension=1, tiled=True
            ).astype(jnp.float32),
        )
        text_key_grad = text_key_sum.astype(jnp.bfloat16)
        text_value_grad = text_value_sum.astype(jnp.bfloat16)
        text_slice = lax.dynamic_slice_in_dim(text_block, context_index * text_share, text_share, 1)
        grad_cross_query = outer_sum(normed_two, grad_cross_act)
        grad_cross_key = outer_sum(text_slice, text_key_grad)
        grad_cross_value = outer_sum(text_slice, text_value_grad)
        text_part = against(text_key_grad, cross_key_full) + against(
            text_value_grad, cross_value_full
        )
        text_grads.append(
            lax.psum_scatter(
                text_part.astype(jnp.bfloat16), "tensor", scatter_dimension=2, tiled=True
            ).astype(jnp.float32)
        )
        grad_self_in, grad_gain_two, grad_bias_two = second_back(
            back_sum(against(grad_cross_act, cross_query_full))
        )
        grad_after_self = grad_after_cross + grad_self_in
        grad_branch = grad_after_self.astype(jnp.bfloat16)
        grad_self_output = outer_sum(mixed, grad_branch)
        grad_mixed = against(grad_branch, output_full).astype(jnp.bfloat16)
        back_keys, back_values = (key_rows, value_rows)
        grad_query_act, self_inner, key_part, value_part = attention_back(
            queries, back_keys, back_values, grad_mixed, log_total, offset, True
        )
        key_sum, value_sum = (
            lax.psum_scatter(
                key_part.astype(jnp.bfloat16), "context", scatter_dimension=1, tiled=True
            ).astype(jnp.float32),
            lax.psum_scatter(
                value_part.astype(jnp.bfloat16), "context", scatter_dimension=1, tiled=True
            ).astype(jnp.float32),
        )
        key_grad = key_sum.astype(jnp.bfloat16)
        value_grad = value_sum.astype(jnp.bfloat16)
        grad_self_query = outer_sum(normed_one, grad_query_act)
        grad_self_key = outer_sum(normed_one, key_grad)
        grad_self_value = outer_sum(normed_one, value_grad)
        normed_grad = back_sum(
            against(grad_query_act, query_full)
            + against(key_grad, key_full)
            + against(value_grad, value_full)
        )
        grad_frames_in, grad_gain_one, grad_bias_one = first_back(normed_grad)
        input_grads.append(grad_after_self + grad_frames_in)
        row_terms = (
            grad_gain_one,
            grad_bias_one,
            grad_gain_two,
            grad_bias_two,
            grad_gain_three,
            grad_bias_three,
            grad_self_query,
            grad_self_key,
            grad_self_value,
            grad_cross_query,
            grad_cross_key,
            grad_cross_value,
            grad_up,
        )
        col_terms = (grad_self_output, grad_cross_output, grad_down)
        if row_total is None:
            row_total, col_total = (row_terms, col_terms)
        else:
            row_total = jax.tree.map(jnp.add, row_total, row_terms)
            col_total = jax.tree.map(jnp.add, col_total, col_terms)
    row_total, col_total = reduce_grads(row_total, col_total)
    return (
        jnp.stack(outputs),
        jnp.stack(input_grads),
        jnp.stack(text_grads),
        row_total[0],
        row_total[1],
        row_total[2],
        row_total[3],
        row_total[4],
        row_total[5],
        row_total[6],
        row_total[7],
        row_total[8],
        col_total[0],
        row_total[9],
        row_total[10],
        row_total[11],
        col_total[1],
        row_total[12],
        col_total[2],
    )


def norm_stats(values):
    centre = values - jnp.mean(values, axis=-1, keepdims=True)
    rate = lax.rsqrt(jnp.mean(centre * centre, axis=-1, keepdims=True) + epsilon)
    return centre * rate, rate


def norm_back(grads, gain, normed, rate):
    scaled = grads * gain
    first = jnp.mean(scaled, axis=-1, keepdims=True)
    second = jnp.mean(scaled * normed, axis=-1, keepdims=True)
    return rate * (scaled - first - normed * second)


def low(values):
    return values.astype(jnp.bfloat16)


def wide(values):
    return values.astype(jnp.float32)


def plane_perm(sizes, core, row, col):
    dp, ctx = sizes
    return [
        (d * ctx + x, ((d ^ core) ^ (2 * row)) * ctx + (x ^ col)) for d in range(dp) for x in range(ctx)
    ]


def plane_move(values, core, row, col):
    sizes = (lax.axis_size("dp"), lax.axis_size("context"))
    return lax.ppermute(values, ("dp", "context"), plane_perm(sizes, core, row, col))


def z_move(values, step):
    size = lax.axis_size("tensor")
    return lax.ppermute(values, "tensor", [(k, (k + step) % size) for k in range(size)])


def grid_move(values, col, step):
    size, ctx = lax.axis_size("tensor"), lax.axis_size("context")
    return lax.ppermute(
        values,
        ("context", "tensor"),
        [
            (x * size + z, (x ^ col) * size + (z + step) % size)
            for x in range(ctx)
            for z in range(size)
        ],
    )


def side_swap(values):
    return lax.ppermute(values, "context", [(0, 1), (1, 0)])


OFFSETS = [(c, y, x) for c in range(2) for y in range(2) for x in range(2)]
BITS = [y * 4 + c * 2 + x for c, y, x in OFFSETS]


def plane_gather(shard):
    near = [shard] + [plane_move(shard, 0, y, x) for y, x in ((0, 1), (1, 0), (1, 1))]
    far = [plane_move(piece, 1, 0, 0) for piece in near]
    return near + far


def plane_reduce(near, far):
    total = wide(near) + wide(plane_move(far, 1, 0, 0))
    result = total[0]
    for place, (y, x) in enumerate(((0, 1), (1, 0), (1, 1))):
        result = result + wide(plane_move(low(total[place + 1]), 0, y, x))
    return result


def z_gather(piece):
    return [piece] + [z_move(piece, step) for step in range(1, lax.axis_size("tensor"))]


def block_order(index):
    inverse = [0] * 8
    for place, bits in enumerate(BITS):
        inverse[bits] = place
    return jnp.asarray(inverse)[jnp.arange(8) ^ index]


def assemble(pieces, index):
    stacked = jnp.stack(pieces)[block_order(index)]
    return stacked.reshape(-1, stacked.shape[-1])


def disassemble(whole, index):
    blocks = whole.reshape(8, whole.shape[0] // 8, whole.shape[1])
    blocks = blocks[jnp.asarray(BITS) ^ index]
    return blocks[:4], blocks[4:]


def pack_heads(q, k, v):
    return jnp.concatenate(
        [q[:, :128], k[:, :128], v[:, :128], q[:, 128:], v[:, 128:], k[:, 128:], jnp.zeros_like(q[:, :64])],
        axis=1,
    )


def unpack_heads(packed):
    q = jnp.concatenate([packed[:, 0:128], packed[:, 384:448]], axis=1)
    k = jnp.concatenate([packed[:, 128:256], packed[:, 512:576]], axis=1)
    v = jnp.concatenate([packed[:, 256:384], packed[:, 448:512]], axis=1)
    return q, k, v


def pack_mixed(o):
    return jnp.concatenate([o[:, :128], jnp.zeros_like(o[:, :64]), o[:, 128:]], axis=1)


def unpack_mixed(packed):
    return jnp.concatenate([packed[:, :128], packed[:, 192:256]], axis=1)


def heads_of(values):
    return values.reshape(values.shape[0], -1, HD).swapaxes(0, 1)


def unheads(values):
    return values.swapaxes(0, 1).reshape(values.shape[1], -1)


def bdot(former, latter, dims):
    return lax.dot_general(former, latter, (dims, ((0,), (0,))), preferred_element_type=jnp.float32)


def causal_scores(q, k):
    scores = bdot(q, k, ((2,), (2,))) * HD ** (-0.5)
    rows = lax.broadcasted_iota(jnp.int32, scores.shape, 1)
    cols = lax.broadcasted_iota(jnp.int32, scores.shape, 2)
    return jnp.where(cols <= rows, scores, masked_score)


def project(frames, gains, weights, side):
    normed, _ = norm_stats(frames)
    hidden = low(normed * gains[0] + gains[1])
    both = low(matmul(hidden, weights))
    keep = jnp.where(side == 0, both[:, :640], both[:, 640:])
    send = jnp.where(side == 0, both[:, 640:], both[:, :640])
    return hidden, keep, send


def ordered(keep, recv, side):
    return jnp.concatenate(
        [jnp.where(side == 0, keep, recv), jnp.where(side == 0, recv, keep)], axis=0
    )


def attend(packed):
    q, k, v = (heads_of(part) for part in unpack_heads(packed))
    weights, total = softmax_parts(causal_scores(q, k))
    mixed = low(bdot(low(weights), v, ((2,), (1,))))
    return pack_mixed(unheads(mixed)), total


def attend_back(packed, total, grad_mixed):
    q, k, v = (heads_of(part) for part in unpack_heads(packed))
    do = heads_of(unpack_mixed(grad_mixed))
    p = jnp.exp(causal_scores(q, k) - total)
    dp = bdot(do, v, ((2,), (2,)))
    ds = low(p * (dp - jnp.sum(dp * p, axis=-1, keepdims=True)))
    dq = low(bdot(ds, k, ((2,), (1,))) * HD ** (-0.5))
    dk = low(bdot(ds, q, ((1,), (1,))) * HD ** (-0.5))
    dv = low(bdot(low(p), do, ((1,), (1,))))
    return pack_heads(unheads(dq), unheads(dk), unheads(dv))


def grid_blocks(rows, side, level):
    size = lax.axis_size("tensor")
    share = rows.shape[0] // (2 * size)
    return [
        lax.dynamic_slice_in_dim(rows, ((side ^ col) * size + (level + step) % size) * share, share, 0)
        for col in (0, 1)
        for step in range(size)
    ]


def grid_unblocks(blocks, side, level):
    size = lax.axis_size("tensor")
    share = blocks[0].shape[0]
    result = jnp.zeros((2 * size * share, blocks[0].shape[1]), blocks[0].dtype)
    for place, block in enumerate(blocks):
        col, step = place // size, place % size
        result = lax.dynamic_update_slice_in_dim(
            result, block, ((side ^ col) * size + (level + step) % size) * share, 0
        )
    return result


def grid_exchange(blocks, sign):
    size = lax.axis_size("tensor")
    return [
        block if place == 0 else grid_move(block, place // size, sign * (place % size))
        for place, block in enumerate(blocks)
    ]


def middle_parts(weights):
    steps = weights.reshape(weights.shape[0], -1, 1280)
    return steps[:, :, :384], steps[:, :, 384:896], steps[:, :, 896:]


def middle_forward(mixed, rows, gains, weights, text, side):
    cq_w, so_w, co_w = middle_parts(weights)
    size = cq_w.shape[1]
    wide_in = cq_w.shape[0]
    absolute = [
        jnp.where(side == s, mixed[step], mixed[size + step]) for step in range(size) for s in (0, 1)
    ]
    mixed_row = jnp.concatenate(absolute, axis=1)
    after_self = rows + against(mixed_row, so_w.reshape(wide_in, -1))
    normed, _ = norm_stats(after_self)
    hidden = low(normed * gains[2] + gains[3])
    queries = low(matmul(hidden, cq_w.reshape(wide_in, -1)))
    keys = text[:, :, :384].swapaxes(0, 1).reshape(text.shape[1], -1)
    vals = text[:, :, 384:].swapaxes(0, 1).reshape(text.shape[1], -1)
    scores = bdot(heads_of(queries), heads_of(keys), ((2,), (2,))) * HD ** (-0.5)
    weights_p, _ = softmax_parts(scores)
    crossed = low(unheads(bdot(low(weights_p), heads_of(vals), ((2,), (1,)))))
    after_cross = after_self + against(crossed, co_w.reshape(wide_in, -1))
    normed, _ = norm_stats(after_cross)
    third = low(normed * gains[4] + gains[5])
    return mixed_row, after_self, hidden, queries, crossed, after_cross, third


def feed(third, grad_rows, weights):
    up, down = weights[:, : weights.shape[1] // 2], weights[:, weights.shape[1] // 2 :]
    inner = matmul(third, up)
    bell = (1.0 + lax.erf(inner * 0.5**0.5)) * 0.5
    activated = low(inner * bell)
    slope = bell + inner * jnp.exp(-0.5 * inner * inner) * (2.0 * jnp.pi) ** (-0.5)
    grad_inner = low(matmul(grad_rows, down) * slope)
    return activated, grad_inner, low(against(activated, down)), low(against(grad_inner, up))


def middle_back(third_grad, grad_rows, kept, gains, weights, text, side):
    mixed_row, after_self, hidden, queries, crossed, after_cross, third = kept
    cq_w, so_w, co_w = middle_parts(weights)
    size = cq_w.shape[1]
    wide_in = cq_w.shape[0]
    normed, rate = norm_stats(after_cross)
    gain_three = jnp.sum(third_grad * normed, axis=0)
    bias_three = jnp.sum(third_grad, axis=0)
    grad_cross = grad_rows + norm_back(third_grad, gains[4], normed, rate)
    d2 = low(grad_cross)
    grad_crossed = heads_of(low(matmul(d2, co_w.reshape(wide_in, -1))))
    keys = heads_of(text[:, :, :384].swapaxes(0, 1).reshape(text.shape[1], -1))
    vals = heads_of(text[:, :, 384:].swapaxes(0, 1).reshape(text.shape[1], -1))
    q = heads_of(queries)
    cp, _ = softmax_parts(bdot(q, keys, ((2,), (2,))) * HD ** (-0.5))
    dcp = bdot(grad_crossed, vals, ((2,), (2,)))
    dcs = low(cp * (dcp - jnp.sum(dcp * cp, axis=-1, keepdims=True)))
    dcq = low(unheads(bdot(dcs, keys, ((2,), (1,)))) * HD ** (-0.5))
    dck = unheads(bdot(dcs, q, ((1,), (1,)))) * HD ** (-0.5)
    dcv = unheads(bdot(low(cp), grad_crossed, ((1,), (1,))))
    second_grad = against(dcq, cq_w.reshape(wide_in, -1))
    normed, rate = norm_stats(after_self)
    gain_two = jnp.sum(second_grad * normed, axis=0)
    bias_two = jnp.sum(second_grad, axis=0)
    grad_self = grad_cross + norm_back(second_grad, gains[2], normed, rate)
    d1 = low(grad_self)
    grad_mixed = low(matmul(d1, so_w.reshape(wide_in, -1)))
    blocks = []
    for col in (0, 1):
        for step in range(size):
            first = grad_mixed[:, step * 512 : step * 512 + 256]
            other = grad_mixed[:, step * 512 + 256 : step * 512 + 512]
            blocks.append(jnp.where((side ^ col) == 0, first, other))
    text_grads = jnp.concatenate(
        [part[:, step * 384 : step * 384 + 384] for step in range(size) for part in (dck, dcv)], axis=1
    )
    return blocks, d1, d2, dcq, grad_self, low(text_grads), (gain_two, bias_two, gain_three, bias_three)


def z_rows(rows, level, step):
    size = lax.axis_size("tensor")
    share = rows.shape[0] // size
    return lax.dynamic_slice_in_dim(rows, ((level + step) % size) * share, share, 0)


def z_place(pieces, level):
    size = lax.axis_size("tensor")
    share = pieces[0].shape[0]
    result = jnp.zeros((size * share, pieces[0].shape[1]), pieces[0].dtype)
    for step, piece in enumerate(pieces):
        result = lax.dynamic_update_slice_in_dim(result, piece, ((level - step) % size) * share, 0)
    return result


def shards(
    frames,
    text_states,
    cotangent,
    clip_live,
    first_gain,
    first_bias,
    second_gain,
    second_bias,
    third_gain,
    third_bias,
    self_query,
    self_key,
    self_value,
    self_output,
    cross_query,
    cross_key,
    cross_value,
    cross_output,
    hidden_up,
    hidden_down,
):
    side = lax.axis_index("context")
    level = lax.axis_index("tensor")
    index = lax.axis_index("dp") * 2 + side
    size = lax.axis_size("tensor")
    batches = frames.shape[0]
    x = frames[:, 0]
    live = clip_live.astype(jnp.float32)[:, 0]
    dy = cotangent[:, 0] * live[:, None, None]
    text = text_states[:, 0]
    text_rows = text.reshape(-1, text.shape[-1])
    local_rows = x.shape[1]
    share = local_rows // size
    block = self_query.shape[0]

    half = self_query.shape[1] // 2
    norm_row = jnp.concatenate([first_gain, first_bias, second_gain, second_bias, third_gain, third_bias])
    norm_rows = jnp.zeros((16, 1280), jnp.bfloat16).at[0, : 6 * block].set(norm_row)
    qkv_local = jnp.concatenate(
        [
            pack_heads(self_query[:, h], self_key[:, h], self_value[:, h])
            for h in (slice(0, half), slice(half, None))
        ],
        axis=1,
    )
    qkv_pieces = plane_gather(jnp.concatenate([qkv_local, norm_rows], axis=0))
    qkv_full = assemble([piece[:block] for piece in qkv_pieces], index)
    norm_full = assemble([piece[block : block + 1] for piece in qkv_pieces], index)[:, : 6 * block]
    gains = wide(norm_full.reshape(8, 6, block).swapaxes(0, 1).reshape(6, -1))
    so_turned = self_output.T
    middle_local = jnp.concatenate(
        [
            cross_query,
            pack_mixed(so_turned[:, :half]),
            pack_mixed(so_turned[:, half:]),
            cross_output.T,
        ],
        axis=1,
    )
    middle_step = jnp.concatenate(z_gather(middle_local), axis=1)
    middle_full = assemble(plane_gather(middle_step), index)
    text_full = assemble(plane_gather(jnp.concatenate([cross_key, cross_value], axis=1)), index)
    feed_full = assemble(plane_gather(jnp.concatenate([hidden_up, hidden_down.T], axis=1)), index)

    text_kv = jnp.stack(z_gather(low(matmul(text_rows, text_full))))
    text_kv = text_kv.reshape(size, batches, -1, text_kv.shape[-1])

    saved = []
    for m in range(batches):
        hidden, keep, send = project(x[m], gains, qkv_full, side)
        packed = ordered(keep, side_swap(send), side)
        mixed, total = attend(packed)
        blocks = grid_exchange(grid_blocks(mixed, side, level), 1)
        own = z_rows(x[m], level, 0)
        kept = middle_forward(blocks, own, gains, middle_full, text_kv[:, m], side)
        third = jnp.concatenate(z_gather(kept[-1]), axis=0)
        d3 = low(jnp.concatenate([z_rows(dy[m], level, -step) for step in range(size)], axis=0))
        activated, grad_inner, out_part, grad_part = feed(third, d3, feed_full)
        saved.append((hidden, packed, total, kept, third, d3, activated, grad_inner, out_part, grad_part))

    outs = []
    later = []
    for m in range(batches):
        hidden, packed, total, kept, third, d3, activated, grad_inner, out_part, grad_part = saved[m]
        out_sum = wide(out_part[:share])
        grad_sum = wide(grad_part[:share])
        for step in range(1, size):
            rows = slice(step * share, step * share + share)
            pair = z_move(jnp.stack([out_part[rows], grad_part[rows]]), -step)
            out_sum = out_sum + wide(pair[0])
            grad_sum = grad_sum + wide(pair[1])
        after_cross = kept[5]
        branch = low(after_cross + out_sum - z_rows(x[m], level, 0))
        outs.append(x[m] + wide(z_place(z_gather(branch), level)))
        result = middle_back(
            grad_sum, z_rows(dy[m], level, 0), kept, gains, middle_full, text_kv[:, m], side
        )
        later.append(result)

    text_parts = jnp.concatenate([result[5] for result in later], axis=0)
    text_sum = wide(text_parts[:, :768])
    for step in range(1, size):
        text_sum = text_sum + wide(z_move(text_parts[:, step * 768 : step * 768 + 768], -step))
    text_sum = low(text_sum)
    text_sum = low(wide(text_sum) + wide(side_swap(text_sum)))
    count = text.shape[1]
    text_back = low(against(text_sum, text_full))
    col_share = text_back.shape[1] // size
    text_back = text_back.reshape(batches, count, -1)
    text_own = lax.dynamic_slice_in_dim(text_back, side * (count // 2), count // 2, 1)
    text_grad = wide(lax.dynamic_slice_in_dim(text_own, level * col_share, col_share, 2))
    for step in range(1, size):
        part = lax.dynamic_slice_in_dim(text_own, ((level + step) % size) * col_share, col_share, 2)
        text_grad = text_grad + wide(z_move(part, step))
    text_side = lax.dynamic_slice_in_dim(text, side * (count // 2), count // 2, 1)
    sum_side = lax.dynamic_slice_in_dim(
        text_sum.reshape(batches, count, -1), side * (count // 2), count // 2, 1
    )
    text_grads = disassemble(low(outer_sum(text_side, sum_side)), index)

    grads = []
    frame_grads = []
    first_sums = []
    for m in range(batches):
        hidden, packed, total, kept, third, d3, activated, grad_inner, out_part, grad_part = saved[m]
        blocks, d1, d2, dcq, grad_self, _, _ = later[m]
        grad_mixed = grid_unblocks(grid_exchange(blocks, -1), side, level)
        dqkv = attend_back(packed, total, grad_mixed)
        keep = lax.dynamic_slice_in_dim(dqkv, side * local_rows, local_rows, 0)
        recv = side_swap(lax.dynamic_slice_in_dim(dqkv, (1 - side) * local_rows, local_rows, 0))
        both = jnp.concatenate(
            [jnp.where(side == 0, keep, recv), jnp.where(side == 0, recv, keep)], axis=1
        )
        first_part = low(against(both, qkv_full))
        first_sum = wide(z_rows(first_part, level, 0))
        for step in range(1, size):
            first_sum = first_sum + wide(z_move(z_rows(first_part, level, step), step))
        own = z_rows(x[m], level, 0)
        normed, rate = norm_stats(own)
        first_sums.append((jnp.sum(first_sum * normed, axis=0), jnp.sum(first_sum, axis=0)))
        branch = low(grad_self + norm_back(first_sum, gains[0], normed, rate) - z_rows(dy[m], level, 0))
        frame_grads.append(dy[m] + wide(z_place(z_gather(branch), level)))
        grads.append(both)

    def joined(parts):
        return jnp.concatenate(parts, axis=0)

    feed_grad = jnp.concatenate(
        [
            outer_sum(joined([s[4] for s in saved]), joined([s[7] for s in saved])),
            outer_sum(joined([s[5] for s in saved]), joined([s[6] for s in saved])),
        ],
        axis=1,
    )
    feed_own = plane_reduce(*disassemble(low(feed_grad), index))
    qkv_grad = outer_sum(joined([s[0] for s in saved]), joined(grads))
    qkv_own = plane_reduce(*disassemble(low(qkv_grad), index))
    cq_grad = outer_sum(joined([s[3][2] for s in saved]), joined([r[3] for r in later]))
    so_grad = outer_sum(joined([r[1] for r in later]), joined([s[3][0] for s in saved]))
    co_grad = outer_sum(joined([r[2] for r in later]), joined([s[3][4] for s in saved]))
    middle_grad = jnp.concatenate(
        [
            part
            for step in range(size)
            for part in (
                cq_grad[:, step * 384 : step * 384 + 384],
                so_grad[:, step * 512 : step * 512 + 512],
                co_grad[:, step * 384 : step * 384 + 384],
            )
        ],
        axis=1,
    )
    middle_own = plane_reduce(*disassemble(low(middle_grad), index))
    middle_sum = middle_own[:, :1280]
    for step in range(1, size):
        middle_sum = middle_sum + wide(
            z_move(low(middle_own[:, step * 1280 : step * 1280 + 1280]), -step)
        )
    text_own_grad = plane_reduce(*text_grads)

    norm_sums = jnp.stack(
        [
            sum(s[0] for s in first_sums),
            sum(s[1] for s in first_sums),
        ]
        + [sum(r[6][k] for r in later) for k in range(4)]
    )
    norm_sums = norm_sums.reshape(6, 8, block).swapaxes(0, 1).reshape(8, 6 * block)
    norm_near, norm_far = disassemble(norm_sums, index)
    norm_own = norm_near[:, 0] + plane_move(norm_far[:, 0], 1, 0, 0)
    norm_total = norm_own[0]
    for place, (y, x_) in enumerate(((0, 1), (1, 0), (1, 1))):
        norm_total = norm_total + plane_move(norm_own[place + 1], 0, y, x_)
    norm_total = sum(z_gather(norm_total)).reshape(6, block)

    first = [unpack_heads(qkv_own[:, :640]), unpack_heads(qkv_own[:, 640:])]
    q_own, k_own, v_own = (jnp.concatenate([a, b], axis=1) for a, b in zip(*first))
    so_own = jnp.concatenate(
        [unpack_mixed(middle_sum[:, 384:640]), unpack_mixed(middle_sum[:, 640:896])], axis=1
    )
    ff = feed_own.shape[1] // 2
    return (
        jnp.stack(outs)[:, None],
        jnp.stack(frame_grads)[:, None],
        text_grad[:, None],
        norm_total[0],
        norm_total[1],
        norm_total[2],
        norm_total[3],
        norm_total[4],
        norm_total[5],
        q_own,
        k_own,
        v_own,
        so_own.T,
        middle_sum[:, :384],
        text_own_grad[:, :384],
        text_own_grad[:, 384:],
        middle_sum[:, 896:].T,
        feed_own[:, :ff],
        feed_own[:, ff:].T,
    )


def per_device(mesh):
    sizes = dict(mesh.shape)

    def dispatch(*args):
        frames, self_query, hidden_up = args[0], args[10], args[18]
        fits = (
            sizes["dp"] == 4
            and sizes["context"] == 2
            and frames.shape[1] == 1
            and frames.shape[2] % (16 * sizes["tensor"]) == 0
            and self_query.shape[1] == 6 * HD
            and self_query.shape[0] * 8 == frames.shape[3]
        )
        return (shards if fits else general_shards)(*args)

    return dispatch


def solution(mesh):
    return jax.shard_map(
        per_device(mesh),
        mesh=mesh,
        in_specs=(
            P(None, "dp", "context", None),
            P(None, "dp", None, None),
            P(None, "dp", "context", None),
            P(None, "dp"),
            P(("dp", "context")),
            P(("dp", "context")),
            P(("dp", "context")),
            P(("dp", "context")),
            P(("dp", "context")),
            P(("dp", "context")),
            P(("dp", "context"), "tensor"),
            P(("dp", "context"), "tensor"),
            P(("dp", "context"), "tensor"),
            P("tensor", ("dp", "context")),
            P(("dp", "context"), "tensor"),
            P(("dp", "context"), "tensor"),
            P(("dp", "context"), "tensor"),
            P("tensor", ("dp", "context")),
            P(("dp", "context"), "tensor"),
            P("tensor", ("dp", "context")),
        ),
        out_specs=(
            P(None, "dp", "context", None),
            P(None, "dp", "context", None),
            P(None, "dp", "context", "tensor"),
            P(("dp", "context")),
            P(("dp", "context")),
            P(("dp", "context")),
            P(("dp", "context")),
            P(("dp", "context")),
            P(("dp", "context")),
            P(("dp", "context"), "tensor"),
            P(("dp", "context"), "tensor"),
            P(("dp", "context"), "tensor"),
            P("tensor", ("dp", "context")),
            P(("dp", "context"), "tensor"),
            P(("dp", "context"), "tensor"),
            P(("dp", "context"), "tensor"),
            P("tensor", ("dp", "context")),
            P(("dp", "context"), "tensor"),
            P("tensor", ("dp", "context")),
        ),
        check_vma=False,
    )
```

```python
import functools

import jax
import jax.numpy as jnp
from jax import lax
from jax.experimental import pallas as pl
from jax.experimental.pallas import tpu as pltpu
from jax.sharding import PartitionSpec as P

HD = 64
PAIRS, MIXES, TURNED = "cihd,cjhd->chij", "chij,cjhd->cihd", "chij,cihd->cjhd"
DATA, SIDES, LEVELS = "dp", "context", "tensor"


epsilon = 1e-05
masked_score = -1e30


def layer_norm(values, norm_gain, norm_shift):
    centre = values - jnp.mean(values, axis=-1, keepdims=True)
    spread = jnp.mean(centre * centre, axis=-1, keepdims=True)
    return centre * lax.rsqrt(spread + epsilon) * norm_gain + norm_shift


def exact_gelu(values):
    return jax.nn.gelu(values, approximate=False)


def matmul(former, latter):
    return jnp.dot(former, latter, preferred_element_type=jnp.float32)


def against(former, latter):
    return lax.dot_general(
        former, latter, (((former.ndim - 1,), (1,)), ((), ())), preferred_element_type=jnp.float32
    )


def outer_sum(former, latter):
    flat_former = former.reshape(-1, former.shape[-1])
    flat_latter = latter.reshape(-1, latter.shape[-1])
    return lax.dot_general(
        flat_former, flat_latter, (((0,), (0,)), ((), ())), preferred_element_type=jnp.float32
    )


def split_heads(values):
    return values.reshape(values.shape[0], values.shape[1], values.shape[2] // HD, HD)


def join_heads(values):
    return values.reshape(values.shape[0], values.shape[1], values.shape[2] * values.shape[3])


def head_scores(queries, key_rows, offset, causal, key_offset=0):
    scores = jnp.einsum(
        PAIRS,
        split_heads(queries),
        split_heads(key_rows),
        preferred_element_type=jnp.float32,
    ) * HD ** (-0.5)
    if causal:
        shape_ij = (queries.shape[1], key_rows.shape[1])
        query_pos = offset + lax.broadcasted_iota(jnp.int32, shape_ij, 0)
        key_pos = key_offset + lax.broadcasted_iota(jnp.int32, shape_ij, 1)
        scores = jnp.where(key_pos <= query_pos, scores, masked_score)
    return scores


def softmax_parts(scores):
    top_score = jnp.max(scores, axis=-1, keepdims=True)
    scaled = jnp.exp(scores - top_score)
    row_total = jnp.sum(scaled, axis=-1, keepdims=True)
    return (scaled / row_total, top_score + jnp.log(row_total))


def mix_heads(weights, value_rows):
    return join_heads(
        jnp.einsum(
            MIXES, weights, split_heads(value_rows), preferred_element_type=jnp.float32
        )
    )


def attention_back(queries, key_rows, value_rows, grad_mixed, log_total, offset, causal):
    probability = jnp.exp(head_scores(queries, key_rows, offset, causal) - log_total)
    grad_probs = jnp.einsum(
        PAIRS,
        split_heads(grad_mixed),
        split_heads(value_rows),
        preferred_element_type=jnp.float32,
    )
    inner_sum = jnp.sum(grad_probs * probability, axis=-1, keepdims=True)
    grad_scores = (probability * (grad_probs - inner_sum)).astype(jnp.bfloat16)
    score_scale = HD ** (-0.5)
    grad_queries = join_heads(
        jnp.einsum(
            MIXES,
            grad_scores,
            split_heads(key_rows),
            preferred_element_type=jnp.float32,
        )
        * score_scale
    )
    grad_keys = join_heads(
        jnp.einsum(
            TURNED, grad_scores, split_heads(queries), preferred_element_type=jnp.float32
        )
        * score_scale
    )
    grad_values = join_heads(
        jnp.einsum(
            TURNED,
            probability.astype(jnp.bfloat16),
            split_heads(grad_mixed),
            preferred_element_type=jnp.float32,
        )
    )
    return (grad_queries.astype(jnp.bfloat16), inner_sum, grad_keys, grad_values)


def branch_sum(values):
    return lax.psum(values, LEVELS)


def back_sum(values):
    return lax.psum(values.astype(jnp.bfloat16), LEVELS).astype(jnp.float32)


def reduce_grads(row_terms, col_terms):
    row_sums = (
        lax.psum_scatter(
            row_terms[0].astype(jnp.bfloat16), (DATA, SIDES), scatter_dimension=0, tiled=True
        ).astype(jnp.float32),
        lax.psum_scatter(
            row_terms[1].astype(jnp.bfloat16), (DATA, SIDES), scatter_dimension=0, tiled=True
        ).astype(jnp.float32),
        lax.psum_scatter(
            row_terms[2].astype(jnp.bfloat16), (DATA, SIDES), scatter_dimension=0, tiled=True
        ).astype(jnp.float32),
        lax.psum_scatter(
            row_terms[3].astype(jnp.bfloat16), (DATA, SIDES), scatter_dimension=0, tiled=True
        ).astype(jnp.float32),
        lax.psum_scatter(
            row_terms[4].astype(jnp.bfloat16), (DATA, SIDES), scatter_dimension=0, tiled=True
        ).astype(jnp.float32),
        lax.psum_scatter(
            row_terms[5].astype(jnp.bfloat16), (DATA, SIDES), scatter_dimension=0, tiled=True
        ).astype(jnp.float32),
        lax.psum_scatter(
            row_terms[6].astype(jnp.bfloat16), (DATA, SIDES), scatter_dimension=0, tiled=True
        ).astype(jnp.float32),
        lax.psum_scatter(
            row_terms[7].astype(jnp.bfloat16), (DATA, SIDES), scatter_dimension=0, tiled=True
        ).astype(jnp.float32),
        lax.psum_scatter(
            row_terms[8].astype(jnp.bfloat16), (DATA, SIDES), scatter_dimension=0, tiled=True
        ).astype(jnp.float32),
        lax.psum_scatter(
            row_terms[9].astype(jnp.bfloat16), (DATA, SIDES), scatter_dimension=0, tiled=True
        ).astype(jnp.float32),
        lax.psum_scatter(
            row_terms[10].astype(jnp.bfloat16), (DATA, SIDES), scatter_dimension=0, tiled=True
        ).astype(jnp.float32),
        lax.psum_scatter(
            row_terms[11].astype(jnp.bfloat16), (DATA, SIDES), scatter_dimension=0, tiled=True
        ).astype(jnp.float32),
        lax.psum_scatter(
            row_terms[12].astype(jnp.bfloat16), (DATA, SIDES), scatter_dimension=0, tiled=True
        ).astype(jnp.float32),
    )
    col_sums = (
        lax.psum_scatter(
            col_terms[0].astype(jnp.bfloat16), (DATA, SIDES), scatter_dimension=1, tiled=True
        ).astype(jnp.float32),
        lax.psum_scatter(
            col_terms[1].astype(jnp.bfloat16), (DATA, SIDES), scatter_dimension=1, tiled=True
        ).astype(jnp.float32),
        lax.psum_scatter(
            col_terms[2].astype(jnp.bfloat16), (DATA, SIDES), scatter_dimension=1, tiled=True
        ).astype(jnp.float32),
    )
    return (row_sums, col_sums)


def general_shards(
    frames,
    text_states,
    cotangent,
    clip_live,
    first_gain,
    first_bias,
    second_gain,
    second_bias,
    third_gain,
    third_bias,
    self_query,
    self_key,
    self_value,
    self_output,
    cross_query,
    cross_key,
    cross_value,
    cross_output,
    hidden_up,
    hidden_down,
):
    row_weights = (
        lax.all_gather(first_gain, (DATA, SIDES), axis=0, tiled=True),
        lax.all_gather(first_bias, (DATA, SIDES), axis=0, tiled=True),
        lax.all_gather(second_gain, (DATA, SIDES), axis=0, tiled=True),
        lax.all_gather(second_bias, (DATA, SIDES), axis=0, tiled=True),
        lax.all_gather(third_gain, (DATA, SIDES), axis=0, tiled=True),
        lax.all_gather(third_bias, (DATA, SIDES), axis=0, tiled=True),
        lax.all_gather(self_query, (DATA, SIDES), axis=0, tiled=True),
        lax.all_gather(self_key, (DATA, SIDES), axis=0, tiled=True),
        lax.all_gather(self_value, (DATA, SIDES), axis=0, tiled=True),
        lax.all_gather(cross_query, (DATA, SIDES), axis=0, tiled=True),
        lax.all_gather(cross_key, (DATA, SIDES), axis=0, tiled=True),
        lax.all_gather(cross_value, (DATA, SIDES), axis=0, tiled=True),
        lax.all_gather(hidden_up, (DATA, SIDES), axis=0, tiled=True),
    )
    col_weights = (
        lax.all_gather(self_output, (DATA, SIDES), axis=1, tiled=True),
        lax.all_gather(cross_output, (DATA, SIDES), axis=1, tiled=True),
        lax.all_gather(hidden_down, (DATA, SIDES), axis=1, tiled=True),
    )
    norm_params = [member.astype(jnp.float32) for member in row_weights[:6]]
    query_full, key_full, value_full = (row_weights[6], row_weights[7], row_weights[8])
    cross_query_full, cross_key_full, cross_value_full = (
        row_weights[9],
        row_weights[10],
        row_weights[11],
    )
    up_full = row_weights[12]
    output_full, cross_output_full, down_full = col_weights
    context_index = lax.axis_index(SIDES)
    offset = context_index * frames.shape[2]
    text_share = text_states.shape[2] // lax.axis_size(SIDES)
    row_total = None
    col_total = None
    outputs = []
    input_grads = []
    text_grads = []
    for micro_batch in range(frames.shape[0]):
        block = frames[micro_batch]
        text_block = text_states[micro_batch]
        normed_first, first_back = jax.vjp(layer_norm, block, norm_params[0], norm_params[1])
        normed_one = normed_first.astype(jnp.bfloat16)
        queries = matmul(normed_one, query_full).astype(jnp.bfloat16)
        key_local = matmul(normed_one, key_full).astype(jnp.bfloat16)
        value_local = matmul(normed_one, value_full).astype(jnp.bfloat16)
        key_rows, value_rows = (
            lax.all_gather(key_local, SIDES, axis=1, tiled=True),
            lax.all_gather(value_local, SIDES, axis=1, tiled=True),
        )
        probability, log_total = softmax_parts(head_scores(queries, key_rows, offset, True))
        mixed = mix_heads(probability.astype(jnp.bfloat16), value_rows).astype(jnp.bfloat16)
        after_self = block + branch_sum(matmul(mixed, output_full))
        normed_second, second_back = jax.vjp(layer_norm, after_self, norm_params[2], norm_params[3])
        normed_two = normed_second.astype(jnp.bfloat16)
        cross_queries = matmul(normed_two, cross_query_full).astype(jnp.bfloat16)
        text_keys = matmul(text_block, cross_key_full).astype(jnp.bfloat16)
        text_values = matmul(text_block, cross_value_full).astype(jnp.bfloat16)
        cross_probs, cross_total = softmax_parts(head_scores(cross_queries, text_keys, 0, False))
        crossed = mix_heads(cross_probs.astype(jnp.bfloat16), text_values).astype(jnp.bfloat16)
        after_cross = after_self + branch_sum(matmul(crossed, cross_output_full))
        normed_third, third_back = jax.vjp(layer_norm, after_cross, norm_params[4], norm_params[5])
        normed_three = normed_third.astype(jnp.bfloat16)
        inner = matmul(normed_three, up_full)
        gelu_value, gelu_back = jax.vjp(exact_gelu, inner)
        activated = gelu_value.astype(jnp.bfloat16)
        outputs.append(after_cross + branch_sum(matmul(activated, down_full)))
        live_weight = clip_live[micro_batch].astype(jnp.float32)[:, None, None]
        grad_result = cotangent[micro_batch] * live_weight
        grad_branch = grad_result.astype(jnp.bfloat16)
        grad_down = outer_sum(activated, grad_branch)
        grad_inner = gelu_back(against(grad_branch, down_full))[0].astype(jnp.bfloat16)
        grad_up = outer_sum(normed_three, grad_inner)
        grad_cross_in, grad_gain_three, grad_bias_three = third_back(
            back_sum(against(grad_inner, up_full))
        )
        grad_after_cross = grad_result + grad_cross_in
        grad_branch = grad_after_cross.astype(jnp.bfloat16)
        grad_cross_output = outer_sum(crossed, grad_branch)
        grad_crossed = against(grad_branch, cross_output_full).astype(jnp.bfloat16)
        grad_cross_act, cross_inner, text_key_part, text_value_part = attention_back(
            cross_queries, text_keys, text_values, grad_crossed, cross_total, 0, False
        )
        text_key_sum, text_value_sum = (
            lax.psum_scatter(
                text_key_part.astype(jnp.bfloat16), SIDES, scatter_dimension=1, tiled=True
            ).astype(jnp.float32),
            lax.psum_scatter(
                text_value_part.astype(jnp.bfloat16), SIDES, scatter_dimension=1, tiled=True
            ).astype(jnp.float32),
        )
        text_key_grad = text_key_sum.astype(jnp.bfloat16)
        text_value_grad = text_value_sum.astype(jnp.bfloat16)
        text_slice = lax.dynamic_slice_in_dim(text_block, context_index * text_share, text_share, 1)
        grad_cross_query = outer_sum(normed_two, grad_cross_act)
        grad_cross_key = outer_sum(text_slice, text_key_grad)
        grad_cross_value = outer_sum(text_slice, text_value_grad)
        text_part = against(text_key_grad, cross_key_full) + against(
            text_value_grad, cross_value_full
        )
        text_grads.append(
            lax.psum_scatter(
                text_part.astype(jnp.bfloat16), LEVELS, scatter_dimension=2, tiled=True
            ).astype(jnp.float32)
        )
        grad_self_in, grad_gain_two, grad_bias_two = second_back(
            back_sum(against(grad_cross_act, cross_query_full))
        )
        grad_after_self = grad_after_cross + grad_self_in
        grad_branch = grad_after_self.astype(jnp.bfloat16)
        grad_self_output = outer_sum(mixed, grad_branch)
        grad_mixed = against(grad_branch, output_full).astype(jnp.bfloat16)
        back_keys, back_values = (key_rows, value_rows)
        grad_query_act, self_inner, key_part, value_part = attention_back(
            queries, back_keys, back_values, grad_mixed, log_total, offset, True
        )
        key_sum, value_sum = (
            lax.psum_scatter(
                key_part.astype(jnp.bfloat16), SIDES, scatter_dimension=1, tiled=True
            ).astype(jnp.float32),
            lax.psum_scatter(
                value_part.astype(jnp.bfloat16), SIDES, scatter_dimension=1, tiled=True
            ).astype(jnp.float32),
        )
        key_grad = key_sum.astype(jnp.bfloat16)
        value_grad = value_sum.astype(jnp.bfloat16)
        grad_self_query = outer_sum(normed_one, grad_query_act)
        grad_self_key = outer_sum(normed_one, key_grad)
        grad_self_value = outer_sum(normed_one, value_grad)
        normed_grad = back_sum(
            against(grad_query_act, query_full)
            + against(key_grad, key_full)
            + against(value_grad, value_full)
        )
        grad_frames_in, grad_gain_one, grad_bias_one = first_back(normed_grad)
        input_grads.append(grad_after_self + grad_frames_in)
        row_terms = (
            grad_gain_one,
            grad_bias_one,
            grad_gain_two,
            grad_bias_two,
            grad_gain_three,
            grad_bias_three,
            grad_self_query,
            grad_self_key,
            grad_self_value,
            grad_cross_query,
            grad_cross_key,
            grad_cross_value,
            grad_up,
        )
        col_terms = (grad_self_output, grad_cross_output, grad_down)
        if row_total is None:
            row_total, col_total = (row_terms, col_terms)
        else:
            row_total = jax.tree.map(jnp.add, row_total, row_terms)
            col_total = jax.tree.map(jnp.add, col_total, col_terms)
    row_total, col_total = reduce_grads(row_total, col_total)
    return (
        jnp.stack(outputs),
        jnp.stack(input_grads),
        jnp.stack(text_grads),
        row_total[0],
        row_total[1],
        row_total[2],
        row_total[3],
        row_total[4],
        row_total[5],
        row_total[6],
        row_total[7],
        row_total[8],
        col_total[0],
        row_total[9],
        row_total[10],
        row_total[11],
        col_total[1],
        row_total[12],
        col_total[2],
    )


def norm_stats(values):
    centre = values - jnp.mean(values, axis=-1, keepdims=True)
    rate = lax.rsqrt(jnp.mean(centre * centre, axis=-1, keepdims=True) + epsilon)
    return centre * rate, rate


def norm_back(grads, gain, normed, rate):
    scaled = grads * gain
    first = jnp.mean(scaled, axis=-1, keepdims=True)
    second = jnp.mean(scaled * normed, axis=-1, keepdims=True)
    return rate * (scaled - first - normed * second)


def low(values):
    return values.astype(jnp.bfloat16)


def wide(values):
    return values.astype(jnp.float32)


def plane_perm(sizes, core, row, col):
    dp, ctx = sizes
    return [
        (d * ctx + x, ((d ^ core) ^ (2 * row)) * ctx + (x ^ col)) for d in range(dp) for x in range(ctx)
    ]


def plane_move(values, core, row, col):
    sizes = (lax.axis_size(DATA), lax.axis_size(SIDES))
    return lax.ppermute(values, (DATA, SIDES), plane_perm(sizes, core, row, col))


def z_move(values, step):
    size = lax.axis_size(LEVELS)
    return lax.ppermute(values, LEVELS, [(k, (k + step) % size) for k in range(size)])


def grid_move(values, col, step):
    size, ctx = lax.axis_size(LEVELS), lax.axis_size(SIDES)
    return lax.ppermute(
        values,
        (SIDES, LEVELS),
        [
            (x * size + z, (x ^ col) * size + (z + step) % size)
            for x in range(ctx)
            for z in range(size)
        ],
    )


def side_swap(values):
    return lax.ppermute(values, SIDES, [(0, 1), (1, 0)])


OFFSETS = [(c, y, x) for c in range(2) for y in range(2) for x in range(2)]
BITS = [y * 4 + c * 2 + x for c, y, x in OFFSETS]


def plane_gather(shard):
    near = [shard] + [plane_move(shard, 0, y, x) for y, x in ((0, 1), (1, 0), (1, 1))]
    far = [plane_move(piece, 1, 0, 0) for piece in near]
    return near + far


def z_gather(piece):
    return [piece] + [z_move(piece, step) for step in range(1, lax.axis_size(LEVELS))]


def block_order(index):
    inverse = [0] * 8
    for place, bits in enumerate(BITS):
        inverse[bits] = place
    return jnp.asarray(inverse)[jnp.arange(8) ^ index]


def assemble(pieces, index):
    stacked = jnp.stack(pieces)[block_order(index)]
    return stacked.reshape(-1, stacked.shape[-1])


def disassemble(whole, index):
    blocks = whole.reshape(8, whole.shape[0] // 8, whole.shape[1])
    blocks = blocks[jnp.asarray(BITS) ^ index]
    return blocks[:4], blocks[4:]


def pack_heads(q, k, v):
    return jnp.concatenate(
        [q[:, :128], k[:, :128], v[:, :128], q[:, 128:], v[:, 128:], k[:, 128:], jnp.zeros_like(q[:, :64])],
        axis=1,
    )


def unpack_heads(packed):
    q = jnp.concatenate([packed[:, 0:128], packed[:, 384:448]], axis=1)
    k = jnp.concatenate([packed[:, 128:256], packed[:, 512:576]], axis=1)
    v = jnp.concatenate([packed[:, 256:384], packed[:, 448:512]], axis=1)
    return q, k, v


def pack_mixed(o):
    return jnp.concatenate([o[:, :128], jnp.zeros_like(o[:, :64]), o[:, 128:]], axis=1)


def unpack_mixed(packed):
    return jnp.concatenate([packed[:, :128], packed[:, 192:256]], axis=1)


def grid_exchange(blocks, sign):
    size = lax.axis_size(LEVELS)
    return [
        block if place == 0 else grid_move(block, place // size, sign * (place % size))
        for place, block in enumerate(blocks)
    ]


GRANT = 62 * 2**20
LANES = 128


def any_spec():
    return pl.BlockSpec(memory_space=pl.ANY)


def full_spec(shape):
    return pl.BlockSpec(shape, lambda *_: (0,) * len(shape))


def run_kernel(kernel, name, grid, place, operands, in_specs, outs, out_specs, scratch, flops=0, moved=0):
    return pl.pallas_call(
        kernel,
        out_shape=outs,
        grid_spec=pltpu.PrefetchScalarGridSpec(
            num_scalar_prefetch=1,
            grid=grid,
            in_specs=in_specs,
            out_specs=out_specs,
            scratch_shapes=scratch,
        ),
        compiler_params=pltpu.CompilerParams(vmem_limit_bytes=GRANT),
        cost_estimate=pl.CostEstimate(flops=int(flops), bytes_accessed=int(moved), transcendentals=0),
        name=name,
    )(place, *operands)


def shape_of(shape, dtype=jnp.bfloat16):
    return jax.ShapeDtypeStruct(tuple(shape), dtype)


def piece_copies(pieces, weights, sems, index, rows):
    copies = []
    for place, piece in enumerate(pieces):
        start = pl.multiple_of((index ^ BITS[place]) * rows, 64)
        copies.append(
            pltpu.make_async_copy(
                piece.at[pl.ds(0, rows), :], weights.at[pl.ds(start, rows), :], sems.at[place]
            )
        )
    return copies


def start_all(copies):
    for copy in copies:
        copy.start()


def wait_all(copies):
    for copy in copies:
        copy.wait()


def nn(former, latter):
    return lax.dot_general(former, latter, (((1,), (0,)), ((), ())), preferred_element_type=jnp.float32)


def nt(former, latter):
    return lax.dot_general(former, latter, (((1,), (1,)), ((), ())), preferred_element_type=jnp.float32)


def tn(former, latter):
    return lax.dot_general(former, latter, (((0,), (0,)), ((), ())), preferred_element_type=jnp.float32)


def low_half(shape):
    return lax.broadcasted_iota(jnp.int32, shape, len(shape) - 1) < HD


def masked_half(values, upper):
    mask = low_half(values.shape)
    zero = jnp.zeros_like(values)
    return jnp.where(mask, zero, values) if upper else jnp.where(mask, values, zero)


def project_kernel(place, x_ref, gains, *rest):
    pieces, (hidden, keep, send, weights, sems) = rest[:8], rest[8:]
    first = pl.program_id(0) == 0
    rows = weights.shape[0] // 8
    copies = piece_copies(pieces, weights, sems, place[2], rows)

    @pl.when(first)
    def _():
        start_all(copies)

    normed, _ = norm_stats(x_ref[0, 0])
    value = low(normed * gains[0:1] + gains[1:2])
    hidden[...] = value

    @pl.when(first)
    def _():
        wait_all(copies)

    both = low(nn(value, weights[...]))

    @pl.when(place[0] == 0)
    def _():
        keep[...] = both[:, :640]
        send[...] = both[:, 640:]

    @pl.when(place[0] != 0)
    def _():
        keep[...] = both[:, 640:]
        send[...] = both[:, :640]


def project(place, frames, batch, gains, pieces):
    rows, width = frames.shape[2:]
    tile = 256
    outs = (shape_of((rows, width)), shape_of((rows, 640)), shape_of((rows, 640)))
    return run_kernel(
        project_kernel,
        "project",
        (rows // tile,),
        place,
        (frames, gains, *pieces),
        [pl.BlockSpec((1, 1, tile, width), lambda i, _: (batch, 0, i, 0)), full_spec(gains.shape)]
        + [any_spec()] * 8,
        outs,
        [pl.BlockSpec((tile, out.shape[1]), lambda i, _: (i, 0)) for out in outs],
        [pltpu.VMEM((width, 1280), jnp.bfloat16), pltpu.SemaphoreType.DMA((8,))],
        2 * rows * width * 1280,
        rows * width * 6 + width * 2560 + rows * 2560,
    )


HEAD_TILES = ((0, 128, 256, False), (0, 128, 256, True))
QUERY_TILE = 256


def gather_rows(place, keep, recv, packed):
    count = keep.shape[0]
    own = pl.multiple_of(place[0] * count, 256)
    other = pl.multiple_of((1 - place[0]) * count, 256)
    packed[pl.ds(own, count), :] = keep[...]
    packed[pl.ds(other, count), :] = recv[...]


def block_start(place, share, col, step, size):
    return pl.multiple_of(((place[0] ^ col) * size + (place[1] + step) % size) * share, 64)


def attend_kernel(place, keep, recv, *rest):
    blocks, (packed, mixed) = rest[:-2], rest[-2:]
    gather_rows(place, keep, recv, packed)
    total = packed.shape[0]
    scale = HD ** (-0.5)
    tile = QUERY_TILE
    causal = lax.broadcasted_iota(jnp.int32, (tile, tile), 1) <= lax.broadcasted_iota(
        jnp.int32, (tile, tile), 0
    )
    k01 = packed[:, 128:256]
    keys = (masked_half(k01, False), masked_half(k01, True), packed[:, 512:640])
    vals = (packed[:, 256:384], packed[:, 256:384], packed[:, 384:512])
    for part in range(total // tile):
        start, stop = part * tile, part * tile + tile
        results = []
        for head in range(3):
            lanes = slice(0, 128) if head < 2 else slice(384, 512)
            q = packed[start:stop, lanes] * scale
            key, val = keys[head], vals[head]
            edge = jnp.where(causal, nt(q, key[start:stop]), masked_score)
            top = jnp.max(edge, axis=-1, keepdims=True)
            if part > 0:
                body = nt(q, key[:start])
                top = jnp.maximum(top, jnp.max(body, axis=-1, keepdims=True))
                body = jnp.exp(body - top)
            edge = jnp.exp(edge - top)
            weight = jnp.sum(edge, axis=-1, keepdims=True)
            value = nn(low(edge), val[start:stop])
            if part > 0:
                weight = weight + jnp.sum(body, axis=-1, keepdims=True)
                value = value + nn(low(body), val[:start])
            results.append(value / weight)
        mask = low_half((tile, 128))
        mixed[start:stop, 0:128] = low(jnp.where(mask, results[0], results[1]))
        mixed[start:stop, 128:256] = low(jnp.where(mask, 0.0, results[2]))
    size = len(blocks) // 2
    share = total // len(blocks)
    for spot, block in enumerate(blocks):
        block[...] = mixed[pl.ds(block_start(place, share, spot // size, spot % size, size), share), :]


def attend(place, keep, recv, size):
    count = keep.shape[0]
    share = count // size
    outs = [shape_of((share, 256))] * (2 * size)
    return run_kernel(
        attend_kernel,
        "attend",
        (1,),
        place,
        (keep, recv),
        [full_spec(keep.shape)] * 2,
        outs,
        [full_spec((share, 256))] * (2 * size),
        [pltpu.VMEM((2 * count, 640), jnp.bfloat16), pltpu.VMEM((2 * count, 256), jnp.bfloat16)],
        6e9,
        count * 8000,
    )


def attend_back_kernel(place, keep, recv, *rest):
    blocks, (keep_out, send_out, packed, mixed, grads) = rest[:-5], rest[-5:]
    gather_rows(place, keep, recv, packed)
    total = packed.shape[0]
    size = len(blocks) // 2
    share = total // len(blocks)
    for spot, block in enumerate(blocks):
        mixed[pl.ds(block_start(place, share, spot // size, spot % size, size), share), :] = block[...]
    scale = HD ** (-0.5)
    tile = QUERY_TILE
    causal = lax.broadcasted_iota(jnp.int32, (tile, tile), 0) <= lax.broadcasted_iota(
        jnp.int32, (tile, tile), 1
    )
    for pair in range(2):
        heads = (0, 1) if pair == 0 else (2,)
        grads_q, grads_k, grads_v = [], None, None
        sums_k = [None] * (total // tile)
        sums_v = [None] * (total // tile)
        for part in range(total // tile):
            start, stop = part * tile, part * tile + tile
            sum_q = None
            for head in heads:
                if pair == 0:
                    upper = head == 1
                    q = masked_half(packed[start:stop, 0:128], upper) * scale
                    do = masked_half(mixed[start:stop, 0:128], upper)
                    key = packed[:stop, 128:256]
                    val = packed[:stop, 256:384]
                else:
                    q = masked_half(packed[start:stop, 384:512], False) * scale
                    do = mixed[start:stop, 128:256]
                    key = packed[:stop, 512:640]
                    val = packed[:stop, 384:512]
                scores = nt(key, q)
                edge = jnp.where(causal, scores[start:stop], masked_score)
                if part > 0:
                    scores = jnp.concatenate([scores[:start], edge], axis=0)
                else:
                    scores = edge
                scores = jnp.exp(scores - jnp.max(scores, axis=0, keepdims=True))
                p = scores * (1.0 / jnp.sum(scores, axis=0, keepdims=True))
                dp = nt(val, do)
                ds = low(p * (dp - jnp.sum(dp * p, axis=0, keepdims=True)))
                p = low(p)
                new_k = nn(ds, q)
                new_v = nn(p, do)
                if pair == 0:
                    key = masked_half(key, upper)
                new_q = tn(ds, key) * scale
                sum_q = new_q if sum_q is None else sum_q + new_q
                for spot in range(part + 1):
                    rows = slice(spot * tile, spot * tile + tile)
                    sums_k[spot] = new_k[rows] if sums_k[spot] is None else sums_k[spot] + new_k[rows]
                    sums_v[spot] = new_v[rows] if sums_v[spot] is None else sums_v[spot] + new_v[rows]
            grads_q.append(sum_q)
        for part in range(total // tile):
            rows = slice(part * tile, part * tile + tile)
            if pair == 0:
                grads[rows, 0:128] = low(grads_q[part])
                grads[rows, 128:256] = low(sums_k[part])
                grads[rows, 256:384] = low(sums_v[part])
            else:
                mask = low_half((tile, 128))
                grads[rows, 384:512] = low(jnp.where(mask, grads_q[part], sums_v[part]))
                grads[rows, 512:640] = low(sums_k[part])
    count = keep.shape[0]
    keep_out[...] = grads[pl.ds(pl.multiple_of(place[0] * count, 256), count), :]
    send_out[...] = grads[pl.ds(pl.multiple_of((1 - place[0]) * count, 256), count), :]


def attend_back(place, keep, recv, blocks):
    count = keep.shape[0]
    share = blocks[0].shape[0]
    outs = [shape_of(keep.shape)] * 2
    return run_kernel(
        attend_back_kernel,
        "attend_back",
        (1,),
        place,
        (keep, recv, *blocks),
        [full_spec(keep.shape)] * 2 + [full_spec((share, 256))] * len(blocks),
        outs,
        [full_spec(keep.shape)] * 2,
        [
            pltpu.VMEM((2 * count, 640), jnp.bfloat16),
            pltpu.VMEM((2 * count, 256), jnp.bfloat16),
            pltpu.VMEM((2 * count, 640), jnp.bfloat16),
        ],
        12e9,
        count * 8000,
    )


def pair_keys(tile):
    return jnp.concatenate([masked_half(tile, False), masked_half(tile, True)], axis=0)


def pair_softmax(scores):
    mask = low_half(scores.shape)
    tops = [
        jnp.max(jnp.where(part, scores, masked_score), axis=-1, keepdims=True) for part in (mask, ~mask)
    ]
    scaled = jnp.exp(scores - jnp.where(mask, tops[0], tops[1]))
    sums = [jnp.sum(jnp.where(part, scaled, 0.0), axis=-1, keepdims=True) for part in (mask, ~mask)]
    return scaled * jnp.where(mask, 1.0 / sums[0], 1.0 / sums[1])


def middle_kernel(place, *rest):
    size = place_size(rest)
    mixed, rest = rest[: 2 * size], rest[2 * size :]
    x_ref, gains, text = rest[:3]
    pieces, rest = rest[3:11], rest[11:]
    mixed_row, after_self, hidden, queries, crossed, after_cross, third, weights, sems = rest
    copies = piece_copies(pieces, weights, sems, place[2], weights.shape[0] // 8)
    start_all(copies)
    for step in range(size):
        for spot in range(2):
            lanes = slice((step * 2 + spot) * 256, (step * 2 + spot) * 256 + 256)

            @pl.when(place[0] == spot)
            def _():
                mixed_row[:, lanes] = mixed[step][...]

            @pl.when(place[0] != spot)
            def _():
                mixed_row[:, lanes] = mixed[size + step][...]

    wait_all(copies)
    first = jnp.zeros(x_ref.shape[2:], jnp.float32)
    for step in range(size):
        first = first + nt(
            mixed_row[:, step * 512 : step * 512 + 512], weights[:, step * 1280 + 384 : step * 1280 + 896]
        )
    first = x_ref[0, 0] + first
    after_self[...] = first
    normed, _ = norm_stats(first)
    value = low(normed * gains[2:3] + gains[3:4])
    hidden[...] = value
    scale = HD ** (-0.5)
    second = jnp.zeros_like(first)
    for step in range(size):
        q = low(nn(value, weights[:, step * 1280 : step * 1280 + 384]))
        queries[:, step * 384 : step * 384 + 384] = q
        for tile in range(3):
            lanes = slice(tile * 128, tile * 128 + 128)
            keys = pair_keys(text[step, :, lanes])
            vals = pair_keys(text[step, :, tile * 128 + 384 : tile * 128 + 512])
            p = low(pair_softmax(nt(q[:, lanes], keys) * scale))
            crossed[:, step * 384 + tile * 128 : step * 384 + tile * 128 + 128] = low(nn(p, vals))
    for step in range(size):
        second = second + nt(
            crossed[:, step * 384 : step * 384 + 384], weights[:, step * 1280 + 896 : step * 1280 + 1280]
        )
    second = after_self[...] + second
    after_cross[...] = second
    normed, _ = norm_stats(second)
    third[...] = low(normed * gains[4:5] + gains[5:6])


def place_size(refs):
    return 4


def middle_forward(place, blocks, frames, batch, gains, pieces, text):
    size = len(blocks) // 2
    share = blocks[0].shape[0]
    width = frames.shape[3]
    outs = (
        shape_of((share, 512 * size)),
        shape_of((share, width), jnp.float32),
        shape_of((share, width)),
        shape_of((share, width)),
        shape_of((share, width)),
        shape_of((share, width), jnp.float32),
        shape_of((share, width)),
    )
    count = text.shape[2]
    return run_kernel(
        middle_kernel,
        "middle",
        (1,),
        place,
        (*blocks, frames, gains, text, *pieces),
        [full_spec((share, 256))] * (2 * size)
        + [
            pl.BlockSpec((1, 1, share, width), lambda i, at: (batch, 0, at[1], 0)),
            full_spec(gains.shape),
            pl.BlockSpec((size, None, count, text.shape[3]), lambda i, at: (0, batch, 0, 0)),
        ]
        + [any_spec()] * 8,
        outs,
        [full_spec(out.shape) for out in outs],
        [pltpu.VMEM((width, 1280 * size), jnp.bfloat16), pltpu.SemaphoreType.DMA((8,))],
        2 * share * width * 1280 * size,
        width * 2560 * size,
    )


def feed_kernel(place, third, dy_a, dy_b, live, *rest, batch):
    pieces, rest = rest[:8], rest[8:]
    activated, grad_inner, d3_out, parts, (weights, sems) = rest[0], rest[1], rest[2], rest[3:-2], rest[-2:]
    turn = pl.program_id(0)
    copies = piece_copies(pieces, weights, sems, place[2], weights.shape[0] // 8)

    @pl.when(turn == 0)
    def _():
        start_all(copies)
        wait_all(copies)

    half = weights.shape[1] // 2
    share, width = third.shape[1:]
    value = third[...].reshape(2 * share, width)
    factor = live[batch]
    d3 = jnp.concatenate([low(dy_a[0, 0] * factor), low(dy_b[0, 0] * factor)], axis=0)
    d3_out[...] = d3
    inner = nn(value, weights[:, :half])
    bell = (1.0 + lax.erf(inner * 0.5**0.5)) * 0.5
    act = low(inner * bell)
    activated[...] = act
    slope = bell + inner * jnp.exp(-0.5 * inner * inner) * (2.0 * jnp.pi) ** (-0.5)
    grad = low(nn(d3, weights[:, half:]) * slope)
    grad_inner[...] = grad
    y = low(nt(act, weights[:, half:]))
    e = low(nt(grad, weights[:, :half]))
    for spot in range(2):

        @pl.when(turn == spot)
        def _():
            for sub in range(2):
                parts[spot * 2 + sub][0] = y[sub * share : sub * share + share]
                parts[spot * 2 + sub][1] = e[sub * share : sub * share + share]


def feed(place, third, cotangent, live, batch, pieces):
    size, share, width = third.shape
    inner = pieces[0].shape[1] // 2
    rows = size * share
    outs = (
        shape_of((rows, inner)),
        shape_of((rows, inner)),
        shape_of((rows, width)),
        *[shape_of((2, share, width))] * size,
    )

    def dy_spec(step):
        return pl.BlockSpec(
            (1, 1, share, width), lambda i, at: (batch, 0, (at[1] + size - 2 * i - step) % size, 0)
        )

    return run_kernel(
        functools.partial(feed_kernel, batch=batch),
        "feed",
        (size // 2,),
        place,
        (third, cotangent, cotangent, live, *pieces),
        [
            pl.BlockSpec((2, share, width), lambda i, _: (i, 0, 0)),
            dy_spec(0),
            dy_spec(1),
            pl.BlockSpec(memory_space=pltpu.SMEM),
        ]
        + [any_spec()] * 8,
        outs,
        [pl.BlockSpec((2 * share, out.shape[1]), lambda i, _: (i, 0)) for out in outs[:3]]
        + [full_spec((2, share, width))] * size,
        [pltpu.VMEM((width, 2 * inner), jnp.bfloat16), pltpu.SemaphoreType.DMA((8,))],
        8 * rows * width * inner,
        rows * width * 20,
    )


def middle_back_kernel(place, *rest, batch):
    size = place_size(rest)
    parts, rest = rest[:size], rest[size:]
    x_ref, dy_ref, live, gains, text = rest[:5]
    mixed_row, after_self_ref, hidden, queries, crossed, after_cross_ref = rest[5:11]
    pieces, rest = rest[11:19], rest[19:]
    blocks, rest = rest[: 2 * size], rest[2 * size :]
    branch, d1_out, d2_out, dcq_out, grad_self_out, text_out, sums, weights, sems = rest
    copies = piece_copies(pieces, weights, sems, place[2], weights.shape[0] // 8)
    start_all(copies)
    out_sum = wide(parts[0][0])
    third_grad = wide(parts[0][1])
    for step in range(1, size):
        out_sum = out_sum + wide(parts[step][0])
        third_grad = third_grad + wide(parts[step][1])
    after_cross = after_cross_ref[...]
    branch[...] = low(after_cross + out_sum - x_ref[0, 0])
    normed, rate = norm_stats(after_cross)
    sums[2:3] = jnp.sum(third_grad * normed, axis=0, keepdims=True)
    sums[3:4] = jnp.sum(third_grad, axis=0, keepdims=True)
    grad_cross = dy_ref[0, 0] * live[batch] + norm_back(third_grad, gains[4:5], normed, rate)
    d2 = low(grad_cross)
    d2_out[...] = d2
    wait_all(copies)
    scale = HD ** (-0.5)
    half_mask = low_half((text.shape[1], 128))
    for step in range(size):
        grad_crossed = low(nn(d2, weights[:, step * 1280 + 896 : step * 1280 + 1280]))
        for tile in range(3):
            lanes = slice(tile * 128, tile * 128 + 128)
            q = queries[:, step * 384 + tile * 128 : step * 384 + tile * 128 + 128]
            do = grad_crossed[:, lanes]
            keys = pair_keys(text[step, :, lanes])
            vals = pair_keys(text[step, :, tile * 128 + 384 : tile * 128 + 512])
            p = pair_softmax(nt(q, keys) * scale)
            dp = nt(do, vals)
            both = dp * p
            mask = low_half(both.shape)
            inner = jnp.where(
                mask,
                jnp.sum(jnp.where(mask, both, 0.0), axis=-1, keepdims=True),
                jnp.sum(jnp.where(mask, 0.0, both), axis=-1, keepdims=True),
            )
            ds = low(p * (dp - inner))
            dcq_out[:, step * 384 + tile * 128 : step * 384 + tile * 128 + 128] = low(nn(ds, keys) * scale)
            count = text.shape[1]
            dk = tn(ds, q) * scale
            dv = tn(low(p), do)
            base = step * 768 + tile * 128
            text_out[:, base : base + 128] = low(jnp.where(half_mask, dk[:count], dk[count:]))
            text_out[:, base + 384 : base + 512] = low(jnp.where(half_mask, dv[:count], dv[count:]))
    second_grad = jnp.zeros(d2.shape, jnp.float32)
    for step in range(size):
        second_grad = second_grad + nt(
            dcq_out[:, step * 384 : step * 384 + 384], weights[:, step * 1280 : step * 1280 + 384]
        )
    normed, rate = norm_stats(after_self_ref[...])
    sums[0:1] = jnp.sum(second_grad * normed, axis=0, keepdims=True)
    sums[1:2] = jnp.sum(second_grad, axis=0, keepdims=True)
    grad_self = grad_cross + norm_back(second_grad, gains[2:3], normed, rate)
    grad_self_out[...] = grad_self
    d1 = low(grad_self)
    d1_out[...] = d1
    for step in range(size):
        for spot in range(2):
            lanes = step * 1280 + 384 + spot * 256
            value = low(nn(d1, weights[:, lanes : lanes + 256]))

            @pl.when(place[0] == spot)
            def _():
                blocks[step][...] = value

            @pl.when(place[0] != spot)
            def _():
                blocks[size + step][...] = value


def middle_back(place, parts, frames, cotangent, live, batch, kept, gains, pieces, text):
    size = len(parts)
    share, width = parts[0].shape[1:]
    count = text.shape[2]
    outs = (
        *[shape_of((share, 256))] * (2 * size),
        shape_of((share, width)),
        shape_of((share, width)),
        shape_of((share, width)),
        shape_of((share, width)),
        shape_of((share, width), jnp.float32),
        shape_of((count, 768 * size)),
        shape_of((4, width), jnp.float32),
    )
    row_spec = pl.BlockSpec((1, 1, share, width), lambda i, at: (batch, 0, at[1], 0))
    return run_kernel(
        functools.partial(middle_back_kernel, batch=batch),
        "middle_back",
        (1,),
        place,
        (*parts, frames, cotangent, live, gains, text, *kept, *pieces),
        [full_spec((2, share, width))] * size
        + [
            row_spec,
            row_spec,
            pl.BlockSpec(memory_space=pltpu.SMEM),
            full_spec(gains.shape),
            pl.BlockSpec((size, None, count, text.shape[3]), lambda i, at: (0, batch, 0, 0)),
        ]
        + [full_spec(part.shape) for part in kept]
        + [any_spec()] * 8,
        outs,
        [full_spec(out.shape) for out in outs],
        [pltpu.VMEM((width, 1280 * size), jnp.bfloat16), pltpu.SemaphoreType.DMA((8,))],
        2 * share * width * 1280 * size,
        width * 2560 * size,
    )


def first_kernel(place, keep, recv, *rest):
    pieces, rest = rest[:8], rest[8:]
    outs, (weights, sems, result) = rest[:-3], rest[-3:]
    copies = piece_copies(pieces, weights, sems, place[2], weights.shape[0] // 8)
    start_all(copies)
    wait_all(copies)

    @pl.when(place[0] == 0)
    def _():
        result[...] = low(nt(keep[...], weights[:, :640]) + nt(recv[...], weights[:, 640:]))

    @pl.when(place[0] != 0)
    def _():
        result[...] = low(nt(recv[...], weights[:, :640]) + nt(keep[...], weights[:, 640:]))

    size = len(outs)
    share = result.shape[0] // size
    for step, out in enumerate(outs):
        start = pl.multiple_of(((place[1] + step) % size) * share, 64)
        out[...] = result[pl.ds(start, share), :]


def first_part(place, keep, recv, pieces, size):
    rows = keep.shape[0]
    width = pieces[0].shape[0] - 16
    width = width * 8
    outs = [shape_of((rows // size, width))] * size
    return run_kernel(
        first_kernel,
        "first_part",
        (1,),
        place,
        (keep, recv, *pieces),
        [full_spec(keep.shape)] * 2 + [any_spec()] * 8,
        outs,
        [full_spec((rows // size, width))] * size,
        [
            pltpu.VMEM((width, 1280), jnp.bfloat16),
            pltpu.SemaphoreType.DMA((8,)),
            pltpu.VMEM((rows, width), jnp.bfloat16),
        ],
        2 * rows * width * 1280,
        width * 2560 + rows * width * 2,
    )


def last_kernel(place, *rest, batch):
    size = place_size(rest)
    parts, (grad_self, x_ref, dy_ref, live, gains, branch, sums) = rest[:size], rest[size:]
    total = wide(parts[0][...])
    for step in range(1, size):
        total = total + wide(parts[step][...])
    normed, rate = norm_stats(x_ref[0, 0])
    sums[0:1] = jnp.sum(total * normed, axis=0, keepdims=True)
    sums[1:2] = jnp.sum(total, axis=0, keepdims=True)
    branch[...] = low(
        grad_self[...] + norm_back(total, gains[0:1], normed, rate) - dy_ref[0, 0] * live[batch]
    )


def last_part(place, parts, grad_self, frames, cotangent, live, batch, gains):
    size = len(parts)
    share, width = parts[0].shape
    outs = (shape_of((share, width)), shape_of((2, width), jnp.float32))
    row_spec = pl.BlockSpec((1, 1, share, width), lambda i, at: (batch, 0, at[1], 0))
    return run_kernel(
        functools.partial(last_kernel, batch=batch),
        "last_part",
        (1,),
        place,
        (*parts, grad_self, frames, cotangent, live, gains),
        [full_spec((share, width))] * (size + 1)
        + [row_spec, row_spec, pl.BlockSpec(memory_space=pltpu.SMEM), full_spec(gains.shape)],
        outs,
        [full_spec(out.shape) for out in outs],
        [],
        share * width * 30,
        share * width * 20,
    )


def place_kernel(place, base, live, *rest):
    pieces, out = rest[:-1], rest[-1]
    batch, step = pl.program_id(0), pl.program_id(1)
    size = pl.num_programs(1)
    for spot, piece in enumerate(pieces):

        @pl.when(batch * size + step == spot)
        def _():
            out[0, 0] = base[0, 0] * live[batch] + wide(piece[...])


def place_rows(place, base, live, pieces):
    batches = base.shape[0]
    size = len(pieces) // batches
    share, width = pieces[0].shape
    spec = pl.BlockSpec((1, 1, share, width), lambda m, i, at: (m, 0, (at[1] + size - i) % size, 0))
    return run_kernel(
        place_kernel,
        "place_rows",
        (batches, size),
        place,
        (base, live, *pieces),
        [spec, pl.BlockSpec(memory_space=pltpu.SMEM)] + [full_spec((share, width))] * len(pieces),
        shape_of(base.shape, jnp.float32),
        spec,
        [],
        base.size,
        base.size * 10,
    )


def outer_blocks(place, terms, width):
    operands, specs = [], []
    full = terms[0][0][0][0].shape[1]
    block = full // 8
    for pairs, _ in terms:
        for lhs, rhs in pairs:
            operands += [lhs, rhs]
            specs += [
                pl.BlockSpec((lhs.shape[0], 2 * block), lambda g, at: (0, at[3] ^ (g // 2) ^ (2 * (g % 2)))),
                full_spec(rhs.shape),
            ]

    def kernel(at, *refs):
        near, far = refs[-2:]
        turn = pl.program_id(0)
        spot = 0
        for pairs, segments in terms:
            chosen = refs[spot : spot + 2 * len(pairs)]
            spot += 2 * len(pairs)
            for start, target, count in segments:
                total = None
                for pair in range(len(pairs)):
                    value = tn(chosen[2 * pair][...], chosen[2 * pair + 1][:, start : start + count])
                    total = value if total is None else total + value
                total = low(total)
                target = pl.multiple_of(target(at), LANES) if callable(target) else target
                for col in range(2):
                    rows = total[col * block : col * block + block]

                    @pl.when(turn < 2)
                    def _():
                        near[at[0] ^ col, :, pl.ds(target, count)] = rows

                    @pl.when(turn >= 2)
                    def _():
                        far[at[0] ^ col, :, pl.ds(target, count)] = rows

    out = shape_of((4, block, width))
    rows = sum(lhs.shape[0] for pairs, _ in terms for lhs, _ in pairs)
    return run_kernel(
        kernel,
        "outer_blocks",
        (4,),
        place,
        operands,
        specs,
        (out, out),
        [
            pl.BlockSpec((2, block, width), lambda g, at: (jnp.minimum(g, 1), 0, 0)),
            pl.BlockSpec((2, block, width), lambda g, at: (jnp.maximum(g - 2, 0), 0, 0)),
        ],
        [],
        2 * rows * full * width / len(terms),
        full * width * 2 + rows * full * 4,
    )


def join_kernel(place, near, far, *outs):
    total = wide(near[...]) + wide(far[...])
    for spot, out in enumerate(outs):
        out[...] = low(total[spot])


def plane_reduce(place, near, far):
    count, block, width = near.shape
    far = plane_move(far, 1, 0, 0)
    tile = 640 if width % 640 == 0 else 768
    sums = run_kernel(
        join_kernel,
        "join",
        (width // tile,),
        place,
        (near, far),
        [pl.BlockSpec((count, block, tile), lambda i, _: (0, 0, i))] * 2,
        [shape_of((block, width))] * count,
        [pl.BlockSpec((block, tile), lambda i, _: (0, i))] * count,
        [],
        near.size,
        near.size * 6,
    )
    result = wide(sums[0])
    for spot, (y, x) in enumerate(((0, 1), (1, 0), (1, 1))):
        result = result + wide(plane_move(sums[spot + 1], 0, y, x))
    return result


def apply_kernel(place, rows, *rest, turned):
    pieces, (out, weights, sems) = rest[:8], rest[8:]
    copies = piece_copies(pieces, weights, sems, place[2], weights.shape[0] // 8)
    start_all(copies)
    wait_all(copies)
    out[...] = low((nt if turned else nn)(rows[...], weights[...]))


def apply_pieces(place, rows, pieces, turned):
    block, width = pieces[0].shape
    out = shape_of((rows.shape[0], 8 * block if turned else width))
    return run_kernel(
        functools.partial(apply_kernel, turned=turned),
        "apply",
        (1,),
        place,
        (rows, *pieces),
        [full_spec(rows.shape)] + [any_spec()] * 8,
        out,
        full_spec(out.shape),
        [pltpu.VMEM((8 * block, width), jnp.bfloat16), pltpu.SemaphoreType.DMA((8,))],
        2 * rows.shape[0] * 8 * block * width,
        8 * block * width * 2,
    )


def own_rows(rows, level, size):
    share = rows.shape[0] // size
    return lax.dynamic_slice_in_dim(rows, level * share, share, 0)


def shards(
    frames,
    text_states,
    cotangent,
    clip_live,
    first_gain,
    first_bias,
    second_gain,
    second_bias,
    third_gain,
    third_bias,
    self_query,
    self_key,
    self_value,
    self_output,
    cross_query,
    cross_key,
    cross_value,
    cross_output,
    hidden_up,
    hidden_down,
):
    side = lax.axis_index(SIDES)
    level = lax.axis_index(LEVELS)
    dp = lax.axis_index(DATA)
    index = dp * 2 + side
    place = jnp.stack([side, level, index, dp]).astype(jnp.int32)
    size = lax.axis_size(LEVELS)
    batches = frames.shape[0]
    live = clip_live.astype(jnp.float32)[:, 0]
    ones = jnp.ones_like(live)
    text = text_states[:, 0]
    text_rows = text.reshape(-1, text.shape[-1])
    count = text.shape[1]
    block = self_query.shape[0]

    half = self_query.shape[1] // 2
    norm_row = jnp.concatenate([first_gain, first_bias, second_gain, second_bias, third_gain, third_bias])
    norm_rows = jnp.zeros((16, 1280), jnp.bfloat16).at[0, : 6 * block].set(norm_row)
    qkv_local = jnp.concatenate(
        [
            pack_heads(self_query[:, h], self_key[:, h], self_value[:, h])
            for h in (slice(0, half), slice(half, None))
        ],
        axis=1,
    )
    qkv_pieces = plane_gather(jnp.concatenate([qkv_local, norm_rows], axis=0))
    norm_full = assemble([piece[block : block + 1] for piece in qkv_pieces], index)[:, : 6 * block]
    gains = wide(norm_full.reshape(8, 6, block).swapaxes(0, 1).reshape(6, -1))
    so_turned = self_output.T
    middle_local = jnp.concatenate(
        [
            cross_query,
            pack_mixed(so_turned[:, :half]),
            pack_mixed(so_turned[:, half:]),
            cross_output.T,
        ],
        axis=1,
    )
    middle_pieces = plane_gather(jnp.concatenate(z_gather(middle_local), axis=1))
    text_pieces = plane_gather(jnp.concatenate([cross_key, cross_value], axis=1))
    feed_pieces = plane_gather(jnp.concatenate([hidden_up, hidden_down.T], axis=1))

    text_kv = jnp.stack(z_gather(apply_pieces(place, text_rows, text_pieces, False)))
    text_kv = text_kv.reshape(size, batches, count, text_kv.shape[-1])

    saved = []
    for m in range(batches):
        hidden, keep, send = project(place, frames, m, gains, qkv_pieces)
        recv = side_swap(send)
        blocks = grid_exchange(attend(place, keep, recv, size), 1)
        kept = middle_forward(place, blocks, frames, m, gains, middle_pieces, text_kv)
        third = jnp.stack(z_gather(kept[-1]))
        activated, grad_inner, d3, *parts = feed(place, third, cotangent, live, m, feed_pieces)
        saved.append((hidden, keep, recv, kept, third, activated, grad_inner, d3, parts))

    branches = []
    later = []
    for m in range(batches):
        hidden, keep, recv, kept, third, activated, grad_inner, d3, parts = saved[m]
        sums = [part if step == 0 else z_move(part, -step) for step, part in enumerate(parts)]
        result = middle_back(
            place, sums, frames, cotangent, live, m, kept[:-1], gains, middle_pieces, text_kv
        )
        branches += z_gather(result[2 * size])
        later.append((result[: 2 * size], *result[2 * size + 1 :]))
    out_frames = place_rows(place, frames, ones, branches)

    rows_of = [s[4].reshape(-1, s[4].shape[-1]) for s in saved]
    ff = hidden_up.shape[1]
    feed_grad = outer_blocks(
        place,
        [
            ([(rows_of[m], saved[m][6]) for m in range(batches)], [(0, 0, ff)]),
            ([(saved[m][7], saved[m][5]) for m in range(batches)], [(0, ff, ff)]),
        ],
        2 * ff,
    )
    feed_own = plane_reduce(place, *feed_grad)

    text_parts = jnp.concatenate([r[5] for r in later], axis=0)
    text_sum = wide(text_parts[:, :768])
    for step in range(1, size):
        text_sum = text_sum + wide(z_move(text_parts[:, step * 768 : step * 768 + 768], -step))
    text_sum = low(text_sum)
    text_sum = low(wide(text_sum) + wide(side_swap(text_sum)))
    text_back = apply_pieces(place, text_sum, text_pieces, True)
    col_share = text_back.shape[1] // size
    text_back = text_back.reshape(batches, count, -1)
    text_own = lax.dynamic_slice_in_dim(text_back, side * (count // 2), count // 2, 1)
    text_grad = wide(lax.dynamic_slice_in_dim(text_own, level * col_share, col_share, 2))
    for step in range(1, size):
        part = lax.dynamic_slice_in_dim(text_own, ((level + step) % size) * col_share, col_share, 2)
        text_grad = text_grad + wide(z_move(part, step))
    text_side = lax.dynamic_slice_in_dim(text, side * (count // 2), count // 2, 1)
    sum_side = lax.dynamic_slice_in_dim(
        text_sum.reshape(batches, count, -1), side * (count // 2), count // 2, 1
    )
    text_grads = outer_blocks(
        place,
        [
            (
                [(text_side.reshape(-1, text.shape[-1]), sum_side.reshape(-1, text_sum.shape[-1]))],
                [(0, 0, text_sum.shape[-1])],
            )
        ],
        text_sum.shape[-1],
    )
    text_own_grad = plane_reduce(place, *text_grads)

    grads = []
    frame_branches = []
    first_sums = []
    for m in range(batches):
        keep, recv = saved[m][1:3]
        blocks, d1, d2, dcq, grad_self = later[m][:5]
        grad_keep, grad_send = attend_back(place, keep, recv, grid_exchange(blocks, -1))
        grad_recv = side_swap(grad_send)
        parts = first_part(place, grad_keep, grad_recv, qkv_pieces, size)
        parts = [part if step == 0 else z_move(part, step) for step, part in enumerate(parts)]
        branch, sums = last_part(place, parts, grad_self, frames, cotangent, live, m, gains)
        first_sums.append(sums)
        frame_branches += z_gather(branch)
        grads.append((grad_keep, grad_recv))
    frame_grads = place_rows(place, cotangent, live, frame_branches)

    middle_grad = outer_blocks(
        place,
        [
            (
                [(saved[m][3][2], later[m][3]) for m in range(batches)],
                [(step * 384, step * 1280, 384) for step in range(size)],
            ),
            (
                [(later[m][1], saved[m][3][0]) for m in range(batches)],
                [(step * 512, step * 1280 + 384, 512) for step in range(size)],
            ),
            (
                [(later[m][2], saved[m][3][4]) for m in range(batches)],
                [(step * 384, step * 1280 + 896, 384) for step in range(size)],
            ),
        ],
        1280 * size,
    )
    middle_own = plane_reduce(place, *middle_grad)
    middle_sum = middle_own[:, :1280]
    for step in range(1, size):
        middle_sum = middle_sum + wide(
            z_move(low(middle_own[:, step * 1280 : step * 1280 + 1280]), -step)
        )
    qkv_grad = outer_blocks(
        place,
        [
            ([(saved[m][0], grads[m][0]) for m in range(batches)], [(0, lambda at: at[0] * 640, 640)]),
            ([(saved[m][0], grads[m][1]) for m in range(batches)], [(0, lambda at: (1 - at[0]) * 640, 640)]),
        ],
        1280,
    )
    qkv_own = plane_reduce(place, *qkv_grad)

    norm_sums = jnp.concatenate([sum(first_sums), sum(r[6] for r in later)], axis=0)
    norm_sums = norm_sums.reshape(6, 8, block).swapaxes(0, 1).reshape(8, 6 * block)
    norm_near, norm_far = disassemble(norm_sums, index)
    norm_own = norm_near[:, 0] + plane_move(norm_far[:, 0], 1, 0, 0)
    norm_total = norm_own[0]
    for spot, (y, x) in enumerate(((0, 1), (1, 0), (1, 1))):
        norm_total = norm_total + plane_move(norm_own[spot + 1], 0, y, x)
    norm_total = sum(z_gather(norm_total)).reshape(6, block)

    first = [unpack_heads(qkv_own[:, :640]), unpack_heads(qkv_own[:, 640:])]
    q_own, k_own, v_own = (jnp.concatenate([a, b], axis=1) for a, b in zip(*first))
    so_own = jnp.concatenate(
        [unpack_mixed(middle_sum[:, 384:640]), unpack_mixed(middle_sum[:, 640:896])], axis=1
    )
    return (
        out_frames,
        frame_grads,
        text_grad[:, None],
        norm_total[0],
        norm_total[1],
        norm_total[2],
        norm_total[3],
        norm_total[4],
        norm_total[5],
        q_own,
        k_own,
        v_own,
        so_own.T,
        middle_sum[:, :384],
        text_own_grad[:, :384],
        text_own_grad[:, 384:],
        middle_sum[:, 896:].T,
        feed_own[:, :ff],
        feed_own[:, ff:].T,
    )


def per_device(mesh):
    sizes = dict(mesh.shape)

    def dispatch(*args):
        frames, self_query, hidden_up = args[0], args[10], args[18]
        fits = (
            sizes[DATA] == 4
            and sizes[SIDES] == 2
            and frames.shape[1] == 1
            and frames.shape[2] % (16 * sizes[LEVELS]) == 0
            and self_query.shape[1] == 6 * HD
            and self_query.shape[0] * 8 == frames.shape[3]
        )
        return (shards if fits else general_shards)(*args)

    return dispatch


def solution(mesh):
    return jax.shard_map(
        per_device(mesh),
        mesh=mesh,
        in_specs=(
            P(None, DATA, SIDES, None),
            P(None, DATA, None, None),
            P(None, DATA, SIDES, None),
            P(None, DATA),
            P((DATA, SIDES)),
            P((DATA, SIDES)),
            P((DATA, SIDES)),
            P((DATA, SIDES)),
            P((DATA, SIDES)),
            P((DATA, SIDES)),
            P((DATA, SIDES), LEVELS),
            P((DATA, SIDES), LEVELS),
            P((DATA, SIDES), LEVELS),
            P(LEVELS, (DATA, SIDES)),
            P((DATA, SIDES), LEVELS),
            P((DATA, SIDES), LEVELS),
            P((DATA, SIDES), LEVELS),
            P(LEVELS, (DATA, SIDES)),
            P((DATA, SIDES), LEVELS),
            P(LEVELS, (DATA, SIDES)),
        ),
        out_specs=(
            P(None, DATA, SIDES, None),
            P(None, DATA, SIDES, None),
            P(None, DATA, SIDES, LEVELS),
            P((DATA, SIDES)),
            P((DATA, SIDES)),
            P((DATA, SIDES)),
            P((DATA, SIDES)),
            P((DATA, SIDES)),
            P((DATA, SIDES)),
            P((DATA, SIDES), LEVELS),
            P((DATA, SIDES), LEVELS),
            P((DATA, SIDES), LEVELS),
            P(LEVELS, (DATA, SIDES)),
            P((DATA, SIDES), LEVELS),
            P((DATA, SIDES), LEVELS),
            P((DATA, SIDES), LEVELS),
            P(LEVELS, (DATA, SIDES)),
            P((DATA, SIDES), LEVELS),
            P(LEVELS, (DATA, SIDES)),
        ),
        check_vma=False,
    )
```

```python
import functools

import jax
import jax.numpy as jnp
from jax import lax
from jax.experimental import pallas as pl
from jax.experimental.pallas import tpu as pltpu
from jax.sharding import PartitionSpec as P

HD = 64
PAIRS, MIXES, TURNED = "cihd,cjhd->chij", "chij,cjhd->cihd", "chij,cihd->cjhd"
DATA, SIDES, LEVELS = "dp", "context", "tensor"


epsilon = 1e-05
masked_score = -1e30


def layer_norm(values, norm_gain, norm_shift):
    centre = values - jnp.mean(values, axis=-1, keepdims=True)
    spread = jnp.mean(centre * centre, axis=-1, keepdims=True)
    return centre * lax.rsqrt(spread + epsilon) * norm_gain + norm_shift


def exact_gelu(values):
    return jax.nn.gelu(values, approximate=False)


def matmul(former, latter):
    return jnp.dot(former, latter, preferred_element_type=jnp.float32)


def against(former, latter):
    return lax.dot_general(
        former, latter, (((former.ndim - 1,), (1,)), ((), ())), preferred_element_type=jnp.float32
    )


def outer_sum(former, latter):
    flat_former = former.reshape(-1, former.shape[-1])
    flat_latter = latter.reshape(-1, latter.shape[-1])
    return lax.dot_general(
        flat_former, flat_latter, (((0,), (0,)), ((), ())), preferred_element_type=jnp.float32
    )


def split_heads(values):
    return values.reshape(values.shape[0], values.shape[1], values.shape[2] // HD, HD)


def join_heads(values):
    return values.reshape(values.shape[0], values.shape[1], values.shape[2] * values.shape[3])


def head_scores(queries, key_rows, offset, causal, key_offset=0):
    scores = jnp.einsum(
        PAIRS,
        split_heads(queries),
        split_heads(key_rows),
        preferred_element_type=jnp.float32,
    ) * HD ** (-0.5)
    if causal:
        shape_ij = (queries.shape[1], key_rows.shape[1])
        query_pos = offset + lax.broadcasted_iota(jnp.int32, shape_ij, 0)
        key_pos = key_offset + lax.broadcasted_iota(jnp.int32, shape_ij, 1)
        scores = jnp.where(key_pos <= query_pos, scores, masked_score)
    return scores


def softmax_parts(scores):
    top_score = jnp.max(scores, axis=-1, keepdims=True)
    scaled = jnp.exp(scores - top_score)
    row_total = jnp.sum(scaled, axis=-1, keepdims=True)
    return (scaled / row_total, top_score + jnp.log(row_total))


def mix_heads(weights, value_rows):
    return join_heads(
        jnp.einsum(
            MIXES, weights, split_heads(value_rows), preferred_element_type=jnp.float32
        )
    )


def attention_back(queries, key_rows, value_rows, grad_mixed, log_total, offset, causal):
    probability = jnp.exp(head_scores(queries, key_rows, offset, causal) - log_total)
    grad_probs = jnp.einsum(
        PAIRS,
        split_heads(grad_mixed),
        split_heads(value_rows),
        preferred_element_type=jnp.float32,
    )
    inner_sum = jnp.sum(grad_probs * probability, axis=-1, keepdims=True)
    grad_scores = (probability * (grad_probs - inner_sum)).astype(jnp.bfloat16)
    score_scale = HD ** (-0.5)
    grad_queries = join_heads(
        jnp.einsum(
            MIXES,
            grad_scores,
            split_heads(key_rows),
            preferred_element_type=jnp.float32,
        )
        * score_scale
    )
    grad_keys = join_heads(
        jnp.einsum(
            TURNED, grad_scores, split_heads(queries), preferred_element_type=jnp.float32
        )
        * score_scale
    )
    grad_values = join_heads(
        jnp.einsum(
            TURNED,
            probability.astype(jnp.bfloat16),
            split_heads(grad_mixed),
            preferred_element_type=jnp.float32,
        )
    )
    return (grad_queries.astype(jnp.bfloat16), inner_sum, grad_keys, grad_values)


def branch_sum(values):
    return lax.psum(values, LEVELS)


def back_sum(values):
    return lax.psum(values.astype(jnp.bfloat16), LEVELS).astype(jnp.float32)


def reduce_grads(row_terms, col_terms):
    row_sums = (
        lax.psum_scatter(
            row_terms[0].astype(jnp.bfloat16), (DATA, SIDES), scatter_dimension=0, tiled=True
        ).astype(jnp.float32),
        lax.psum_scatter(
            row_terms[1].astype(jnp.bfloat16), (DATA, SIDES), scatter_dimension=0, tiled=True
        ).astype(jnp.float32),
        lax.psum_scatter(
            row_terms[2].astype(jnp.bfloat16), (DATA, SIDES), scatter_dimension=0, tiled=True
        ).astype(jnp.float32),
        lax.psum_scatter(
            row_terms[3].astype(jnp.bfloat16), (DATA, SIDES), scatter_dimension=0, tiled=True
        ).astype(jnp.float32),
        lax.psum_scatter(
            row_terms[4].astype(jnp.bfloat16), (DATA, SIDES), scatter_dimension=0, tiled=True
        ).astype(jnp.float32),
        lax.psum_scatter(
            row_terms[5].astype(jnp.bfloat16), (DATA, SIDES), scatter_dimension=0, tiled=True
        ).astype(jnp.float32),
        lax.psum_scatter(
            row_terms[6].astype(jnp.bfloat16), (DATA, SIDES), scatter_dimension=0, tiled=True
        ).astype(jnp.float32),
        lax.psum_scatter(
            row_terms[7].astype(jnp.bfloat16), (DATA, SIDES), scatter_dimension=0, tiled=True
        ).astype(jnp.float32),
        lax.psum_scatter(
            row_terms[8].astype(jnp.bfloat16), (DATA, SIDES), scatter_dimension=0, tiled=True
        ).astype(jnp.float32),
        lax.psum_scatter(
            row_terms[9].astype(jnp.bfloat16), (DATA, SIDES), scatter_dimension=0, tiled=True
        ).astype(jnp.float32),
        lax.psum_scatter(
            row_terms[10].astype(jnp.bfloat16), (DATA, SIDES), scatter_dimension=0, tiled=True
        ).astype(jnp.float32),
        lax.psum_scatter(
            row_terms[11].astype(jnp.bfloat16), (DATA, SIDES), scatter_dimension=0, tiled=True
        ).astype(jnp.float32),
        lax.psum_scatter(
            row_terms[12].astype(jnp.bfloat16), (DATA, SIDES), scatter_dimension=0, tiled=True
        ).astype(jnp.float32),
    )
    col_sums = (
        lax.psum_scatter(
            col_terms[0].astype(jnp.bfloat16), (DATA, SIDES), scatter_dimension=1, tiled=True
        ).astype(jnp.float32),
        lax.psum_scatter(
            col_terms[1].astype(jnp.bfloat16), (DATA, SIDES), scatter_dimension=1, tiled=True
        ).astype(jnp.float32),
        lax.psum_scatter(
            col_terms[2].astype(jnp.bfloat16), (DATA, SIDES), scatter_dimension=1, tiled=True
        ).astype(jnp.float32),
    )
    return (row_sums, col_sums)


def general_shards(
    frames,
    text_states,
    cotangent,
    clip_live,
    first_gain,
    first_bias,
    second_gain,
    second_bias,
    third_gain,
    third_bias,
    self_query,
    self_key,
    self_value,
    self_output,
    cross_query,
    cross_key,
    cross_value,
    cross_output,
    hidden_up,
    hidden_down,
):
    row_weights = (
        lax.all_gather(first_gain, (DATA, SIDES), axis=0, tiled=True),
        lax.all_gather(first_bias, (DATA, SIDES), axis=0, tiled=True),
        lax.all_gather(second_gain, (DATA, SIDES), axis=0, tiled=True),
        lax.all_gather(second_bias, (DATA, SIDES), axis=0, tiled=True),
        lax.all_gather(third_gain, (DATA, SIDES), axis=0, tiled=True),
        lax.all_gather(third_bias, (DATA, SIDES), axis=0, tiled=True),
        lax.all_gather(self_query, (DATA, SIDES), axis=0, tiled=True),
        lax.all_gather(self_key, (DATA, SIDES), axis=0, tiled=True),
        lax.all_gather(self_value, (DATA, SIDES), axis=0, tiled=True),
        lax.all_gather(cross_query, (DATA, SIDES), axis=0, tiled=True),
        lax.all_gather(cross_key, (DATA, SIDES), axis=0, tiled=True),
        lax.all_gather(cross_value, (DATA, SIDES), axis=0, tiled=True),
        lax.all_gather(hidden_up, (DATA, SIDES), axis=0, tiled=True),
    )
    col_weights = (
        lax.all_gather(self_output, (DATA, SIDES), axis=1, tiled=True),
        lax.all_gather(cross_output, (DATA, SIDES), axis=1, tiled=True),
        lax.all_gather(hidden_down, (DATA, SIDES), axis=1, tiled=True),
    )
    norm_params = [member.astype(jnp.float32) for member in row_weights[:6]]
    query_full, key_full, value_full = (row_weights[6], row_weights[7], row_weights[8])
    cross_query_full, cross_key_full, cross_value_full = (
        row_weights[9],
        row_weights[10],
        row_weights[11],
    )
    up_full = row_weights[12]
    output_full, cross_output_full, down_full = col_weights
    context_index = lax.axis_index(SIDES)
    offset = context_index * frames.shape[2]
    text_share = text_states.shape[2] // lax.axis_size(SIDES)
    row_total = None
    col_total = None
    outputs = []
    input_grads = []
    text_grads = []
    for micro_batch in range(frames.shape[0]):
        block = frames[micro_batch]
        text_block = text_states[micro_batch]
        normed_first, first_back = jax.vjp(layer_norm, block, norm_params[0], norm_params[1])
        normed_one = normed_first.astype(jnp.bfloat16)
        queries = matmul(normed_one, query_full).astype(jnp.bfloat16)
        key_local = matmul(normed_one, key_full).astype(jnp.bfloat16)
        value_local = matmul(normed_one, value_full).astype(jnp.bfloat16)
        key_rows, value_rows = (
            lax.all_gather(key_local, SIDES, axis=1, tiled=True),
            lax.all_gather(value_local, SIDES, axis=1, tiled=True),
        )
        probability, log_total = softmax_parts(head_scores(queries, key_rows, offset, True))
        mixed = mix_heads(probability.astype(jnp.bfloat16), value_rows).astype(jnp.bfloat16)
        after_self = block + branch_sum(matmul(mixed, output_full))
        normed_second, second_back = jax.vjp(layer_norm, after_self, norm_params[2], norm_params[3])
        normed_two = normed_second.astype(jnp.bfloat16)
        cross_queries = matmul(normed_two, cross_query_full).astype(jnp.bfloat16)
        text_keys = matmul(text_block, cross_key_full).astype(jnp.bfloat16)
        text_values = matmul(text_block, cross_value_full).astype(jnp.bfloat16)
        cross_probs, cross_total = softmax_parts(head_scores(cross_queries, text_keys, 0, False))
        crossed = mix_heads(cross_probs.astype(jnp.bfloat16), text_values).astype(jnp.bfloat16)
        after_cross = after_self + branch_sum(matmul(crossed, cross_output_full))
        normed_third, third_back = jax.vjp(layer_norm, after_cross, norm_params[4], norm_params[5])
        normed_three = normed_third.astype(jnp.bfloat16)
        inner = matmul(normed_three, up_full)
        gelu_value, gelu_back = jax.vjp(exact_gelu, inner)
        activated = gelu_value.astype(jnp.bfloat16)
        outputs.append(after_cross + branch_sum(matmul(activated, down_full)))
        live_weight = clip_live[micro_batch].astype(jnp.float32)[:, None, None]
        grad_result = cotangent[micro_batch] * live_weight
        grad_branch = grad_result.astype(jnp.bfloat16)
        grad_down = outer_sum(activated, grad_branch)
        grad_inner = gelu_back(against(grad_branch, down_full))[0].astype(jnp.bfloat16)
        grad_up = outer_sum(normed_three, grad_inner)
        grad_cross_in, grad_gain_three, grad_bias_three = third_back(
            back_sum(against(grad_inner, up_full))
        )
        grad_after_cross = grad_result + grad_cross_in
        grad_branch = grad_after_cross.astype(jnp.bfloat16)
        grad_cross_output = outer_sum(crossed, grad_branch)
        grad_crossed = against(grad_branch, cross_output_full).astype(jnp.bfloat16)
        grad_cross_act, cross_inner, text_key_part, text_value_part = attention_back(
            cross_queries, text_keys, text_values, grad_crossed, cross_total, 0, False
        )
        text_key_sum, text_value_sum = (
            lax.psum_scatter(
                text_key_part.astype(jnp.bfloat16), SIDES, scatter_dimension=1, tiled=True
            ).astype(jnp.float32),
            lax.psum_scatter(
                text_value_part.astype(jnp.bfloat16), SIDES, scatter_dimension=1, tiled=True
            ).astype(jnp.float32),
        )
        text_key_grad = text_key_sum.astype(jnp.bfloat16)
        text_value_grad = text_value_sum.astype(jnp.bfloat16)
        text_slice = lax.dynamic_slice_in_dim(text_block, context_index * text_share, text_share, 1)
        grad_cross_query = outer_sum(normed_two, grad_cross_act)
        grad_cross_key = outer_sum(text_slice, text_key_grad)
        grad_cross_value = outer_sum(text_slice, text_value_grad)
        text_part = against(text_key_grad, cross_key_full) + against(
            text_value_grad, cross_value_full
        )
        text_grads.append(
            lax.psum_scatter(
                text_part.astype(jnp.bfloat16), LEVELS, scatter_dimension=2, tiled=True
            ).astype(jnp.float32)
        )
        grad_self_in, grad_gain_two, grad_bias_two = second_back(
            back_sum(against(grad_cross_act, cross_query_full))
        )
        grad_after_self = grad_after_cross + grad_self_in
        grad_branch = grad_after_self.astype(jnp.bfloat16)
        grad_self_output = outer_sum(mixed, grad_branch)
        grad_mixed = against(grad_branch, output_full).astype(jnp.bfloat16)
        back_keys, back_values = (key_rows, value_rows)
        grad_query_act, self_inner, key_part, value_part = attention_back(
            queries, back_keys, back_values, grad_mixed, log_total, offset, True
        )
        key_sum, value_sum = (
            lax.psum_scatter(
                key_part.astype(jnp.bfloat16), SIDES, scatter_dimension=1, tiled=True
            ).astype(jnp.float32),
            lax.psum_scatter(
                value_part.astype(jnp.bfloat16), SIDES, scatter_dimension=1, tiled=True
            ).astype(jnp.float32),
        )
        key_grad = key_sum.astype(jnp.bfloat16)
        value_grad = value_sum.astype(jnp.bfloat16)
        grad_self_query = outer_sum(normed_one, grad_query_act)
        grad_self_key = outer_sum(normed_one, key_grad)
        grad_self_value = outer_sum(normed_one, value_grad)
        normed_grad = back_sum(
            against(grad_query_act, query_full)
            + against(key_grad, key_full)
            + against(value_grad, value_full)
        )
        grad_frames_in, grad_gain_one, grad_bias_one = first_back(normed_grad)
        input_grads.append(grad_after_self + grad_frames_in)
        row_terms = (
            grad_gain_one,
            grad_bias_one,
            grad_gain_two,
            grad_bias_two,
            grad_gain_three,
            grad_bias_three,
            grad_self_query,
            grad_self_key,
            grad_self_value,
            grad_cross_query,
            grad_cross_key,
            grad_cross_value,
            grad_up,
        )
        col_terms = (grad_self_output, grad_cross_output, grad_down)
        if row_total is None:
            row_total, col_total = (row_terms, col_terms)
        else:
            row_total = jax.tree.map(jnp.add, row_total, row_terms)
            col_total = jax.tree.map(jnp.add, col_total, col_terms)
    row_total, col_total = reduce_grads(row_total, col_total)
    return (
        jnp.stack(outputs),
        jnp.stack(input_grads),
        jnp.stack(text_grads),
        row_total[0],
        row_total[1],
        row_total[2],
        row_total[3],
        row_total[4],
        row_total[5],
        row_total[6],
        row_total[7],
        row_total[8],
        col_total[0],
        row_total[9],
        row_total[10],
        row_total[11],
        col_total[1],
        row_total[12],
        col_total[2],
    )


def norm_stats(values):
    centre = values - jnp.mean(values, axis=-1, keepdims=True)
    rate = lax.rsqrt(jnp.mean(centre * centre, axis=-1, keepdims=True) + epsilon)
    return centre * rate, rate


def norm_back(grads, gain, normed, rate):
    scaled = grads * gain
    first = jnp.mean(scaled, axis=-1, keepdims=True)
    second = jnp.mean(scaled * normed, axis=-1, keepdims=True)
    return rate * (scaled - first - normed * second)


def low(values):
    return values.astype(jnp.bfloat16)


def wide(values):
    return values.astype(jnp.float32)


def plane_perm(sizes, core, row, col):
    dp, ctx = sizes
    return [
        (d * ctx + x, ((d ^ core) ^ (2 * row)) * ctx + (x ^ col)) for d in range(dp) for x in range(ctx)
    ]


def plane_move(values, core, row, col):
    sizes = (lax.axis_size(DATA), lax.axis_size(SIDES))
    return lax.ppermute(values, (DATA, SIDES), plane_perm(sizes, core, row, col))


def z_move(values, step):
    size = lax.axis_size(LEVELS)
    return lax.ppermute(values, LEVELS, [(k, (k + step) % size) for k in range(size)])


def side_swap(values):
    return lax.ppermute(values, SIDES, [(0, 1), (1, 0)])


OFFSETS = [(c, y, x) for c in range(2) for y in range(2) for x in range(2)]
BITS = [y * 4 + c * 2 + x for c, y, x in OFFSETS]


def after(values, *earlier):
    return lax.optimization_barrier((values, earlier))[0]


def near_gather(shard, *released):
    late = after(shard, *released) if released else shard
    return [shard, plane_move(late, 0, 0, 1), plane_move(shard, 0, 1, 0), plane_move(late, 0, 1, 1)]


def far_gather(near):
    return near + [plane_move(piece, 1, 0, 0) for piece in near]


def z_gather(piece):
    return [piece] + [z_move(piece, step) for step in range(1, lax.axis_size(LEVELS))]


def block_order(index):
    inverse = [0] * 8
    for place, bits in enumerate(BITS):
        inverse[bits] = place
    return jnp.asarray(inverse)[jnp.arange(8) ^ index]


def assemble(pieces, index):
    stacked = jnp.stack(pieces)[block_order(index)]
    return stacked.reshape(-1, stacked.shape[-1])


def disassemble(whole, index):
    blocks = whole.reshape(8, whole.shape[0] // 8, whole.shape[1])
    blocks = blocks[jnp.asarray(BITS) ^ index]
    return blocks[:4], blocks[4:]


def pack_heads(q, k, v):
    return jnp.concatenate(
        [q[:, :128], k[:, :128], v[:, :128], q[:, 128:], v[:, 128:], k[:, 128:], jnp.zeros_like(q[:, :64])],
        axis=1,
    )


def unpack_heads(packed):
    q = jnp.concatenate([packed[:, 0:128], packed[:, 384:448]], axis=1)
    k = jnp.concatenate([packed[:, 128:256], packed[:, 512:576]], axis=1)
    v = jnp.concatenate([packed[:, 256:384], packed[:, 448:512]], axis=1)
    return q, k, v


def pack_mixed(o):
    return jnp.concatenate([o[:, :128], jnp.zeros_like(o[:, :64]), o[:, 128:]], axis=1)


def unpack_mixed(packed):
    return jnp.concatenate([packed[:, :128], packed[:, 192:256]], axis=1)


def grid_exchange(rows):
    return lax.all_to_all(rows, (SIDES, LEVELS), 0, 0, tiled=True)


def level_gather(rows):
    return level_exchange(rows).reshape(-1, rows.shape[-1])


def by_distance(blocks, level):
    size = blocks.shape[0]
    return blocks[(level + size - jnp.arange(size)) % size]


def repeat_levels(rows, size):
    return jnp.broadcast_to(rows[None], (size, *rows.shape))


def level_exchange(rows):
    return lax.all_to_all(rows, LEVELS, 0, 0, tiled=True)


GRANT = 62 * 2**20
TEXT_LANE = 1280
LANES = 128


def any_spec():
    return pl.BlockSpec(memory_space=pl.ANY)


def full_spec(shape):
    return pl.BlockSpec(shape, lambda *_: (0,) * len(shape))


def run_kernel(kernel, name, grid, place, operands, in_specs, outs, out_specs, scratch, flops=0, moved=0):
    return pl.pallas_call(
        kernel,
        out_shape=outs,
        grid_spec=pltpu.PrefetchScalarGridSpec(
            num_scalar_prefetch=1,
            grid=grid,
            in_specs=in_specs,
            out_specs=out_specs,
            scratch_shapes=scratch,
        ),
        compiler_params=pltpu.CompilerParams(vmem_limit_bytes=GRANT),
        cost_estimate=pl.CostEstimate(flops=1, bytes_accessed=1, transcendentals=0),
        name=name,
    )(place, *operands)


def shape_of(shape, dtype=jnp.bfloat16):
    return jax.ShapeDtypeStruct(tuple(shape), dtype)


def piece_copies(pieces, weights, sems, index, rows, lane=0):
    copies = []
    for place, piece in enumerate(pieces):
        start = pl.multiple_of((index ^ BITS[place]) * rows, 64)
        copies.append(
            pltpu.make_async_copy(
                piece.at[pl.ds(0, rows), pl.ds(lane, weights.shape[1])],
                weights.at[pl.ds(start, rows), :],
                sems.at[place],
            )
        )
    return copies


def start_all(copies):
    for copy in copies:
        copy.start()


def wait_all(copies):
    for copy in copies:
        copy.wait()


def nn(former, latter):
    return lax.dot_general(former, latter, (((1,), (0,)), ((), ())), preferred_element_type=jnp.float32)


def nt(former, latter):
    return lax.dot_general(former, latter, (((1,), (1,)), ((), ())), preferred_element_type=jnp.float32)


def tn(former, latter):
    return lax.dot_general(former, latter, (((0,), (0,)), ((), ())), preferred_element_type=jnp.float32)


def low_half(shape):
    return lax.broadcasted_iota(jnp.int32, shape, len(shape) - 1) < HD


def masked_half(values, upper):
    mask = low_half(values.shape)
    zero = jnp.zeros_like(values)
    return jnp.where(mask, zero, values) if upper else jnp.where(mask, values, zero)


def project_kernel(place, x_ref, gains, *rest):
    pieces, (hidden, keep, send, weights, sems) = rest[:8], rest[8:]
    first = pl.program_id(0) == 0
    rows = weights.shape[0] // 8
    copies = piece_copies(pieces, weights, sems, place[2], rows)

    @pl.when(first)
    def _():
        start_all(copies)

    normed, _ = norm_stats(x_ref[0, 0])
    value = low(normed * gains[0:1] + gains[1:2])
    hidden[...] = value

    @pl.when(first)
    def _():
        wait_all(copies)

    both = low(nn(value, weights[...]))

    @pl.when(place[0] == 0)
    def _():
        keep[...] = both[:, :640]
        send[...] = both[:, 640:]

    @pl.when(place[0] != 0)
    def _():
        keep[...] = both[:, 640:]
        send[...] = both[:, :640]


def project(place, frames, batch, gains, pieces):
    rows, width = frames.shape[2:]
    tile = 256
    outs = (shape_of((rows, width)), shape_of((rows, 640)), shape_of((rows, 640)))
    return run_kernel(
        project_kernel,
        "project",
        (rows // tile,),
        place,
        (frames, gains, *pieces),
        [pl.BlockSpec((1, 1, tile, width), lambda i, _: (batch, 0, i, 0)), full_spec(gains.shape)]
        + [any_spec()] * 8,
        outs,
        [pl.BlockSpec((tile, out.shape[1]), lambda i, _: (i, 0)) for out in outs],
        [pltpu.VMEM((width, 1280), jnp.bfloat16), pltpu.SemaphoreType.DMA((8,))],
        2 * rows * width * 1280,
        rows * width * 6 + width * 2560 + rows * 2560,
    )


HEAD_TILES = ((0, 128, 256, False), (0, 128, 256, True))
QUERY_TILE = 256


def gather_rows(place, keep, recv, packed):
    count = keep.shape[0]
    own = pl.multiple_of(place[0] * count, 256)
    other = pl.multiple_of((1 - place[0]) * count, 256)
    packed[pl.ds(own, count), :] = keep[...]
    packed[pl.ds(other, count), :] = recv[...]


def level_start(place, share, step, size):
    return pl.multiple_of(((place[1] + size - step) % size) * share, 64)


def attend_kernel(place, keep, recv, *rest):
    mixed, packed = rest
    gather_rows(place, keep, recv, packed)
    total = packed.shape[0]
    scale = HD ** (-0.5)
    tile = QUERY_TILE
    causal = lax.broadcasted_iota(jnp.int32, (tile, tile), 1) <= lax.broadcasted_iota(
        jnp.int32, (tile, tile), 0
    )
    k01 = packed[:, 128:256]
    keys = (masked_half(k01, False), masked_half(k01, True), packed[:, 512:640])
    vals = (packed[:, 256:384], packed[:, 256:384], packed[:, 384:512])
    for part in range(total // tile):
        start, stop = part * tile, part * tile + tile
        results = []
        for head in range(3):
            lanes = slice(0, 128) if head < 2 else slice(384, 512)
            q = packed[start:stop, lanes] * scale
            key, val = keys[head], vals[head]
            edge = jnp.where(causal, nt(q, key[start:stop]), masked_score)
            top = jnp.max(edge, axis=-1, keepdims=True)
            if part > 0:
                body = nt(q, key[:start])
                top = jnp.maximum(top, jnp.max(body, axis=-1, keepdims=True))
                body = jnp.exp(body - top)
            edge = jnp.exp(edge - top)
            weight = jnp.sum(edge, axis=-1, keepdims=True)
            value = nn(low(edge), val[start:stop])
            if part > 0:
                weight = weight + jnp.sum(body, axis=-1, keepdims=True)
                value = value + nn(low(body), val[:start])
            results.append(value / weight)
        mask = low_half((tile, 128))
        mixed[start:stop, 0:128] = low(jnp.where(mask, results[0], results[1]))
        mixed[start:stop, 128:256] = low(jnp.where(mask, 0.0, results[2]))


def attend(place, keep, recv):
    count = keep.shape[0]
    out = shape_of((2 * count, 256))
    return run_kernel(
        attend_kernel,
        "attend",
        (1,),
        place,
        (keep, recv),
        [full_spec(keep.shape)] * 2,
        out,
        full_spec(out.shape),
        [pltpu.VMEM((2 * count, 640), jnp.bfloat16)],
        6e9,
        count * 8000,
    )


def attend_back_kernel(place, keep, recv, mixed, keep_out, send_out, packed, grads):
    gather_rows(place, keep, recv, packed)
    total = packed.shape[0]
    scale = HD ** (-0.5)
    tile = QUERY_TILE
    causal = lax.broadcasted_iota(jnp.int32, (tile, tile), 0) <= lax.broadcasted_iota(
        jnp.int32, (tile, tile), 1
    )
    for pair in range(2):
        heads = (0, 1) if pair == 0 else (2,)
        grads_q, grads_k, grads_v = [], None, None
        sums_k = [None] * (total // tile)
        sums_v = [None] * (total // tile)
        for part in range(total // tile):
            start, stop = part * tile, part * tile + tile
            sum_q = None
            for head in heads:
                if pair == 0:
                    upper = head == 1
                    q = masked_half(packed[start:stop, 0:128], upper) * scale
                    do = masked_half(mixed[start:stop, 0:128], upper)
                    key = packed[:stop, 128:256]
                    val = packed[:stop, 256:384]
                else:
                    q = masked_half(packed[start:stop, 384:512], False) * scale
                    do = mixed[start:stop, 128:256]
                    key = packed[:stop, 512:640]
                    val = packed[:stop, 384:512]
                scores = nt(key, q)
                edge = jnp.where(causal, scores[start:stop], masked_score)
                if part > 0:
                    scores = jnp.concatenate([scores[:start], edge], axis=0)
                else:
                    scores = edge
                scores = jnp.exp(scores - jnp.max(scores, axis=0, keepdims=True))
                p = scores * (1.0 / jnp.sum(scores, axis=0, keepdims=True))
                dp = nt(val, do)
                ds = low(p * (dp - jnp.sum(dp * p, axis=0, keepdims=True)))
                p = low(p)
                new_k = nn(ds, q)
                new_v = nn(p, do)
                if pair == 0:
                    key = masked_half(key, upper)
                new_q = tn(ds, key) * scale
                sum_q = new_q if sum_q is None else sum_q + new_q
                for spot in range(part + 1):
                    rows = slice(spot * tile, spot * tile + tile)
                    sums_k[spot] = new_k[rows] if sums_k[spot] is None else sums_k[spot] + new_k[rows]
                    sums_v[spot] = new_v[rows] if sums_v[spot] is None else sums_v[spot] + new_v[rows]
            grads_q.append(sum_q)
        for part in range(total // tile):
            rows = slice(part * tile, part * tile + tile)
            if pair == 0:
                grads[rows, 0:128] = low(grads_q[part])
                grads[rows, 128:256] = low(sums_k[part])
                grads[rows, 256:384] = low(sums_v[part])
            else:
                mask = low_half((tile, 128))
                grads[rows, 384:512] = low(jnp.where(mask, grads_q[part], sums_v[part]))
                grads[rows, 512:640] = low(sums_k[part])
    count = keep.shape[0]
    keep_out[...] = grads[pl.ds(pl.multiple_of(place[0] * count, 256), count), :]
    send_out[...] = grads[pl.ds(pl.multiple_of((1 - place[0]) * count, 256), count), :]


def attend_back(place, keep, recv, mixed):
    count = keep.shape[0]
    outs = [shape_of(keep.shape)] * 2
    return run_kernel(
        attend_back_kernel,
        "attend_back",
        (1,),
        place,
        (keep, recv, mixed),
        [full_spec(keep.shape)] * 2 + [full_spec(mixed.shape)],
        outs,
        [full_spec(keep.shape)] * 2,
        [
            pltpu.VMEM((2 * count, 640), jnp.bfloat16),
            pltpu.VMEM((2 * count, 640), jnp.bfloat16),
        ],
        12e9,
        count * 8000,
    )


def pair_keys(tile):
    return jnp.concatenate([masked_half(tile, False), masked_half(tile, True)], axis=0)


def pair_softmax(scores):
    mask = low_half(scores.shape)
    tops = [
        jnp.max(jnp.where(part, scores, masked_score), axis=-1, keepdims=True) for part in (mask, ~mask)
    ]
    scaled = jnp.exp(scores - jnp.where(mask, tops[0], tops[1]))
    sums = [jnp.sum(jnp.where(part, scaled, 0.0), axis=-1, keepdims=True) for part in (mask, ~mask)]
    return scaled * jnp.where(mask, 1.0 / sums[0], 1.0 / sums[1])


def middle_kernel(place, *rest):
    size = place_size(rest)
    mixed, x_ref, gains, text = rest[:4]
    pieces, rest = rest[4:12], rest[12:]
    mixed_row, after_self, hidden, queries, crossed, after_cross, third, weights, sems = rest
    copies = piece_copies(pieces, weights, sems, place[2], weights.shape[0] // 8)
    start_all(copies)
    share = mixed_row.shape[0]
    for step in range(size):
        for spot in range(2):
            lanes = slice((step * 2 + spot) * 256, (step * 2 + spot) * 256 + 256)
            start = spot * size * share + level_start(place, share, step, size)
            mixed_row[:, lanes] = mixed[pl.ds(pl.multiple_of(start, 64), share), :]
    wait_all(copies)
    first = jnp.zeros(x_ref.shape[2:], jnp.float32)
    for step in range(size):
        first = first + nt(
            mixed_row[:, step * 512 : step * 512 + 512], weights[:, step * 1280 + 384 : step * 1280 + 896]
        )
    first = x_ref[0, 0] + first
    after_self[...] = first
    normed, _ = norm_stats(first)
    value = low(normed * gains[2:3] + gains[3:4])
    hidden[...] = value
    scale = HD ** (-0.5)
    second = jnp.zeros_like(first)
    for step in range(size):
        q = low(nn(value, weights[:, step * 1280 : step * 1280 + 384]))
        queries[:, step * 384 : step * 384 + 384] = q
        for tile in range(3):
            lanes = slice(tile * 128, tile * 128 + 128)
            keys = pair_keys(text[step, :, lanes])
            vals = pair_keys(text[step, :, tile * 128 + 384 : tile * 128 + 512])
            p = low(pair_softmax(nt(q[:, lanes], keys) * scale))
            crossed[:, step * 384 + tile * 128 : step * 384 + tile * 128 + 128] = low(nn(p, vals))
    for step in range(size):
        second = second + nt(
            crossed[:, step * 384 : step * 384 + 384], weights[:, step * 1280 + 896 : step * 1280 + 1280]
        )
    second = after_self[...] + second
    after_cross[...] = second
    normed, _ = norm_stats(second)
    value = low(normed * gains[4:5] + gains[5:6])
    for step in range(size):
        third[step] = value


def place_size(refs):
    return 4


def middle_forward(place, mixed, frames, batch, gains, pieces, text):
    size = text.shape[0]
    share = mixed.shape[0] // (2 * size)
    width = frames.shape[3]
    outs = (
        shape_of((share, 512 * size)),
        shape_of((share, width), jnp.float32),
        shape_of((share, width)),
        shape_of((share, width)),
        shape_of((share, width)),
        shape_of((share, width), jnp.float32),
        shape_of((size, share, width)),
    )
    count = text.shape[2]
    return run_kernel(
        middle_kernel,
        "middle",
        (1,),
        place,
        (mixed, frames, gains, text, *pieces),
        [
            full_spec(mixed.shape),
            pl.BlockSpec((1, 1, share, width), lambda i, at: (batch, 0, at[1], 0)),
            full_spec(gains.shape),
            pl.BlockSpec((size, None, count, text.shape[3]), lambda i, at: (0, batch, 0, 0)),
        ]
        + [any_spec()] * 8,
        outs,
        [full_spec(out.shape) for out in outs],
        [pltpu.VMEM((width, 1280 * size), jnp.bfloat16), pltpu.SemaphoreType.DMA((8,))],
        2 * share * width * 1280 * size,
        width * 2560 * size,
    )


def feed_kernel(place, third, dy, live, *rest, batch):
    pieces, (activated, grad_inner, d3_out, y, e, weights, sems) = rest[:8], rest[8:]
    turn = pl.program_id(0)
    copies = piece_copies(pieces, weights, sems, place[2], weights.shape[0] // 8)

    @pl.when(turn == 0)
    def _():
        start_all(copies)
        wait_all(copies)

    half = weights.shape[1] // 2
    value = third[...]
    d3 = low(dy[0, 0] * live[batch])
    d3_out[...] = d3
    inner = nn(value, weights[:, :half])
    bell = (1.0 + lax.erf(inner * 0.5**0.5)) * 0.5
    act = low(inner * bell)
    activated[...] = act
    slope = bell + inner * jnp.exp(-0.5 * inner * inner) * (2.0 * jnp.pi) ** (-0.5)
    grad = low(nn(d3, weights[:, half:]) * slope)
    grad_inner[...] = grad
    e[...] = low(nt(grad, weights[:, :half]))
    y[...] = low(nt(act, weights[:, half:]))


def feed(place, third, cotangent, live, batch, size, pieces):
    rows, width = third.shape
    share = rows // size
    inner = pieces[0].shape[1] // 2
    outs = (
        shape_of((rows, inner)),
        shape_of((rows, inner)),
        *[shape_of((rows, width))] * 3,
    )
    return run_kernel(
        functools.partial(feed_kernel, batch=batch),
        "feed",
        (size // 2,),
        place,
        (third, cotangent, live, *pieces),
        [
            pl.BlockSpec((2 * share, width), lambda i, _: (i, 0)),
            pl.BlockSpec((1, 1, 2 * share, width), lambda i, _: (batch, 0, i, 0)),
            pl.BlockSpec(memory_space=pltpu.SMEM),
        ]
        + [any_spec()] * 8,
        outs,
        [pl.BlockSpec((2 * share, out.shape[1]), lambda i, _: (i, 0)) for out in outs],
        [pltpu.VMEM((width, 2 * inner), jnp.bfloat16), pltpu.SemaphoreType.DMA((8,))],
        8 * rows * width * inner,
        rows * width * 20,
    )


def middle_back_kernel(place, *rest, batch):
    size = place_size(rest)
    parts, rest = rest[0], rest[1:]
    dy_ref, live, gains, text = rest[:4]
    mixed_row, after_self_ref, hidden, queries, crossed, after_cross_ref = rest[4:10]
    pieces, rest = rest[10:18], rest[18:]
    blocks, rest = rest[0], rest[1:]
    d1_out, d2_out, dcq_out, grad_self_out, text_out, sums, weights, sems = rest
    copies = piece_copies(pieces, weights, sems, place[2], weights.shape[0] // 8)
    start_all(copies)
    third_grad = wide(parts[0])
    for step in range(1, size):
        third_grad = third_grad + wide(parts[step])
    after_cross = after_cross_ref[...]
    normed, rate = norm_stats(after_cross)
    sums[2:3] = jnp.sum(third_grad * normed, axis=0, keepdims=True)
    sums[3:4] = jnp.sum(third_grad, axis=0, keepdims=True)
    grad_cross = dy_ref[0, 0] * live[batch] + norm_back(third_grad, gains[4:5], normed, rate)
    d2 = low(grad_cross)
    d2_out[...] = d2
    wait_all(copies)
    scale = HD ** (-0.5)
    half_mask = low_half((text.shape[1], 128))
    for step in range(size):
        grad_crossed = low(nn(d2, weights[:, step * 1280 + 896 : step * 1280 + 1280]))
        for tile in range(3):
            lanes = slice(tile * 128, tile * 128 + 128)
            q = queries[:, step * 384 + tile * 128 : step * 384 + tile * 128 + 128]
            do = grad_crossed[:, lanes]
            keys = pair_keys(text[step, :, lanes])
            vals = pair_keys(text[step, :, tile * 128 + 384 : tile * 128 + 512])
            p = pair_softmax(nt(q, keys) * scale)
            dp = nt(do, vals)
            both = dp * p
            mask = low_half(both.shape)
            inner = jnp.where(
                mask,
                jnp.sum(jnp.where(mask, both, 0.0), axis=-1, keepdims=True),
                jnp.sum(jnp.where(mask, 0.0, both), axis=-1, keepdims=True),
            )
            ds = low(p * (dp - inner))
            dcq_out[:, step * 384 + tile * 128 : step * 384 + tile * 128 + 128] = low(nn(ds, keys) * scale)
            count = text.shape[1]
            dk = tn(ds, q) * scale
            dv = tn(low(p), do)
            base = step * 768 + tile * 128
            text_out[:, base : base + 128] = low(jnp.where(half_mask, dk[:count], dk[count:]))
            text_out[:, base + 384 : base + 512] = low(jnp.where(half_mask, dv[:count], dv[count:]))
    second_grad = jnp.zeros(d2.shape, jnp.float32)
    for step in range(size):
        second_grad = second_grad + nt(
            dcq_out[:, step * 384 : step * 384 + 384], weights[:, step * 1280 : step * 1280 + 384]
        )
    normed, rate = norm_stats(after_self_ref[...])
    sums[0:1] = jnp.sum(second_grad * normed, axis=0, keepdims=True)
    sums[1:2] = jnp.sum(second_grad, axis=0, keepdims=True)
    grad_self = grad_cross + norm_back(second_grad, gains[2:3], normed, rate)
    grad_self_out[...] = grad_self
    d1 = low(grad_self)
    d1_out[...] = d1
    for step in range(size):
        for spot in range(2):
            lanes = step * 1280 + 384 + spot * 256
            share = d1.shape[0]
            start = spot * size * share + level_start(place, share, step, size)
            blocks[pl.ds(pl.multiple_of(start, 64), share), :] = low(nn(d1, weights[:, lanes : lanes + 256]))


def middle_back(place, parts, cotangent, live, batch, kept, gains, pieces, text):
    size, share, width = parts.shape
    count = text.shape[2]
    outs = (
        shape_of((2 * size * share, 256)),
        shape_of((share, width)),
        shape_of((share, width)),
        shape_of((share, width)),
        shape_of((share, width), jnp.float32),
        shape_of((count, 768 * size)),
        shape_of((4, width), jnp.float32),
    )
    row_spec = pl.BlockSpec((1, 1, share, width), lambda i, at: (batch, 0, at[1], 0))
    return run_kernel(
        functools.partial(middle_back_kernel, batch=batch),
        "middle_back",
        (1,),
        place,
        (parts, cotangent, live, gains, text, *kept, *pieces),
        [
            full_spec(parts.shape),
            row_spec,
            pl.BlockSpec(memory_space=pltpu.SMEM),
            full_spec(gains.shape),
            pl.BlockSpec((size, None, count, text.shape[3]), lambda i, at: (0, batch, 0, 0)),
        ]
        + [full_spec(part.shape) for part in kept]
        + [any_spec()] * 8,
        outs,
        [full_spec(out.shape) for out in outs],
        [pltpu.VMEM((width, 1280 * size), jnp.bfloat16), pltpu.SemaphoreType.DMA((8,))],
        2 * share * width * 1280 * size,
        width * 2560 * size,
    )


def first_kernel(place, keep, recv, *rest):
    pieces, rest = rest[:8], rest[8:]
    result, weights, sems = rest
    copies = piece_copies(pieces, weights, sems, place[2], weights.shape[0] // 8)
    start_all(copies)
    wait_all(copies)

    @pl.when(place[0] == 0)
    def _():
        result[...] = low(nt(keep[...], weights[:, :640]) + nt(recv[...], weights[:, 640:]))

    @pl.when(place[0] != 0)
    def _():
        result[...] = low(nt(recv[...], weights[:, :640]) + nt(keep[...], weights[:, 640:]))


def first_part(place, keep, recv, pieces):
    rows = keep.shape[0]
    width = (pieces[0].shape[0] - 16) * 8
    out = shape_of((rows, width))
    return run_kernel(
        first_kernel,
        "first_part",
        (1,),
        place,
        (keep, recv, *pieces),
        [full_spec(keep.shape)] * 2 + [any_spec()] * 8,
        out,
        full_spec(out.shape),
        [pltpu.VMEM((width, 1280), jnp.bfloat16), pltpu.SemaphoreType.DMA((8,))],
        2 * rows * width * 1280,
        width * 2560 + rows * width * 2,
    )


def last_kernel(place, *rest, batch):
    parts, grad_self, x_ref, dy_ref, live, gains, branch, sums = rest
    total = wide(parts[0])
    for step in range(1, parts.shape[0]):
        total = total + wide(parts[step])
    normed, rate = norm_stats(x_ref[0, 0])
    sums[0:1] = jnp.sum(total * normed, axis=0, keepdims=True)
    sums[1:2] = jnp.sum(total, axis=0, keepdims=True)
    value = low(grad_self[...] + norm_back(total, gains[0:1], normed, rate) - dy_ref[0, 0] * live[batch])
    for step in range(parts.shape[0]):
        branch[step] = value


def last_part(place, parts, grad_self, frames, cotangent, live, batch, gains):
    size, share, width = parts.shape
    outs = (shape_of((size, share, width)), shape_of((2, width), jnp.float32))
    row_spec = pl.BlockSpec((1, 1, share, width), lambda i, at: (batch, 0, at[1], 0))
    return run_kernel(
        functools.partial(last_kernel, batch=batch),
        "last_part",
        (1,),
        place,
        (parts, grad_self, frames, cotangent, live, gains),
        [full_spec(parts.shape), full_spec((share, width))]
        + [row_spec, row_spec, pl.BlockSpec(memory_space=pltpu.SMEM), full_spec(gains.shape)],
        outs,
        [full_spec(out.shape) for out in outs],
        [],
        share * width * 30,
        share * width * 20,
    )


def place_kernel(place, base, live, first, second, out):
    batch = pl.program_id(0)
    grown = base[0, 0] * live[batch]

    @pl.when(batch == 0)
    def _():
        out[0, 0] = grown + wide(first[...])

    @pl.when(batch != 0)
    def _():
        out[0, 0] = grown + wide(second[...])


def place_rows(place, base, live, pieces):
    rows, width = pieces[0].shape
    tile = 256
    tiles = rows // tile
    spec = pl.BlockSpec((1, 1, tile, width), lambda m, i, at: (m, 0, i, 0))
    return run_kernel(
        place_kernel,
        "place_rows",
        (2, tiles),
        place,
        (base, live, *pieces),
        [
            spec,
            pl.BlockSpec(memory_space=pltpu.SMEM),
            pl.BlockSpec((tile, width), lambda m, i, at: (jnp.where(m == 0, i, tiles - 1), 0)),
            pl.BlockSpec((tile, width), lambda m, i, at: (jnp.where(m == 0, 0, i), 0)),
        ],
        shape_of(base.shape, jnp.float32),
        spec,
        [],
        base.size,
        base.size * 10,
    )


def outer_blocks(place, terms, width):
    operands, specs = [], []
    full = terms[0][0][0][0].shape[1]
    block = full // 8
    for pairs, _ in terms:
        for lhs, rhs in pairs:
            operands += [lhs, rhs]
            specs += [
                pl.BlockSpec((lhs.shape[0], 2 * block), lambda g, at: (0, at[3] ^ (g // 2) ^ (2 * (g % 2)))),
                full_spec(rhs.shape),
            ]

    def kernel(at, *refs):
        near, far = refs[-2:]
        turn = pl.program_id(0)
        spot = 0
        for pairs, segments in terms:
            chosen = refs[spot : spot + 2 * len(pairs)]
            spot += 2 * len(pairs)
            for start, target, count in segments:
                total = None
                for pair in range(len(pairs)):
                    value = tn(chosen[2 * pair][...], chosen[2 * pair + 1][:, start : start + count])
                    total = value if total is None else total + value
                total = low(total)
                target = pl.multiple_of(target(at), LANES) if callable(target) else target
                for col in range(2):
                    rows = total[col * block : col * block + block]

                    @pl.when(turn < 2)
                    def _():
                        near[at[0] ^ col, :, pl.ds(target, count)] = rows

                    @pl.when(turn >= 2)
                    def _():
                        far[at[0] ^ col, :, pl.ds(target, count)] = rows

    out = shape_of((4, block, width))
    rows = sum(lhs.shape[0] for pairs, _ in terms for lhs, _ in pairs)
    return run_kernel(
        kernel,
        "outer_blocks",
        (4,),
        place,
        operands,
        specs,
        (out, out),
        [
            pl.BlockSpec((2, block, width), lambda g, at: (jnp.minimum(g, 1), 0, 0)),
            pl.BlockSpec((2, block, width), lambda g, at: (jnp.maximum(g - 2, 0), 0, 0)),
        ],
        [],
        2 * rows * full * width / len(terms),
        full * width * 2 + rows * full * 4,
    )


def join_kernel(place, near, far, *outs):
    total = wide(near[...]) + wide(far[...])
    for spot, out in enumerate(outs):
        out[...] = low(total[spot])


def plane_join(place, near, far):
    count, block, width = near.shape
    tile = next(t for t in (640, 768, 1024) if width % t == 0)
    return run_kernel(
        join_kernel,
        "join",
        (width // tile,),
        place,
        (near, far),
        [pl.BlockSpec((count, block, tile), lambda i, _: (0, 0, i))] * 2,
        [shape_of((block, width))] * count,
        [pl.BlockSpec((block, tile), lambda i, _: (0, i))] * count,
        [],
        near.size,
        near.size * 6,
    )


def plane_spread(sums, *released):
    late = after(sums, *released) if released else sums
    return [sums[0], plane_move(late[1], 0, 0, 1), plane_move(sums[2], 0, 1, 0), plane_move(late[3], 0, 1, 1)]


def total_of(pieces):
    return sum(wide(piece) for piece in pieces)


def core_swap(values):
    return plane_move(values, 1, 0, 0)


def apply_kernel(place, rows, *rest, turned):
    pieces, (out, weights, sems) = rest[:8], rest[8:]
    copies = piece_copies(pieces, weights, sems, place[2], weights.shape[0] // 8, TEXT_LANE)
    start_all(copies)
    wait_all(copies)
    out[...] = low((nt if turned else nn)(rows[...], weights[...]))


def apply_pieces(place, rows, pieces, turned):
    block, width = pieces[0].shape[0] - 16, pieces[0].shape[1] - TEXT_LANE
    out = shape_of((rows.shape[0], 8 * block if turned else width))
    return run_kernel(
        functools.partial(apply_kernel, turned=turned),
        "apply",
        (1,),
        place,
        (rows, *pieces),
        [full_spec(rows.shape)] + [any_spec()] * 8,
        out,
        full_spec(out.shape),
        [pltpu.VMEM((8 * block, width), jnp.bfloat16), pltpu.SemaphoreType.DMA((8,))],
        2 * rows.shape[0] * 8 * block * width,
        8 * block * width * 2,
    )


def own_rows(rows, level, size):
    share = rows.shape[0] // size
    return lax.dynamic_slice_in_dim(rows, level * share, share, 0)


def shards(
    frames,
    text_states,
    cotangent,
    clip_live,
    first_gain,
    first_bias,
    second_gain,
    second_bias,
    third_gain,
    third_bias,
    self_query,
    self_key,
    self_value,
    self_output,
    cross_query,
    cross_key,
    cross_value,
    cross_output,
    hidden_up,
    hidden_down,
):
    side = lax.axis_index(SIDES)
    level = lax.axis_index(LEVELS)
    dp = lax.axis_index(DATA)
    index = dp * 2 + side
    place = jnp.stack([side, level, index, dp]).astype(jnp.int32)
    size = lax.axis_size(LEVELS)
    batches = frames.shape[0]
    live = clip_live.astype(jnp.float32)[:, 0]
    ones = jnp.ones_like(live)
    text = text_states[:, 0]
    text_rows = text.reshape(-1, text.shape[-1])
    count = text.shape[1]
    block = self_query.shape[0]

    half = self_query.shape[1] // 2
    norm_row = jnp.concatenate([first_gain, first_bias, second_gain, second_bias, third_gain, third_bias])
    norm_rows = jnp.zeros((16, TEXT_LANE + 2 * self_query.shape[1]), jnp.bfloat16).at[0, : 6 * block].set(norm_row)
    qkv_local = jnp.concatenate(
        [
            pack_heads(self_query[:, h], self_key[:, h], self_value[:, h])
            for h in (slice(0, half), slice(half, None))
        ]
        + [cross_key, cross_value],
        axis=1,
    )
    qkv_near = near_gather(jnp.concatenate([qkv_local, norm_rows], axis=0))
    so_turned = self_output.T
    middle_local = jnp.concatenate(
        [
            cross_query,
            pack_mixed(so_turned[:, :half]),
            pack_mixed(so_turned[:, half:]),
            cross_output.T,
        ],
        axis=1,
    )
    middle_levels = level_exchange(repeat_levels(middle_local, size))
    qkv_pieces = far_gather(qkv_near)
    norm_full = assemble([piece[block : block + 1] for piece in qkv_pieces], index)[:, : 6 * block]
    gains = wide(norm_full.reshape(8, 6, block).swapaxes(0, 1).reshape(6, -1))

    hidden, keeps, sends = [None] * 2, [None] * 2, [None] * 2
    hidden[0], keeps[0], sends[0] = project(place, frames, 0, gains, qkv_pieces)
    middle_row = by_distance(after(middle_levels, hidden[0]), level).swapaxes(0, 1)
    middle_row = middle_row.reshape(block, -1)
    hidden[1], keeps[1], sends[1] = project(place, frames, 1, after(gains, hidden[0]), qkv_pieces)
    recvs = [side_swap(send) for send in sends]
    middle_near = near_gather(after(middle_row, hidden[1]), recvs)
    text_part = apply_pieces(place, after(text_rows, hidden[1]), qkv_pieces, False)
    text_levels = level_exchange(repeat_levels(text_part, size))
    keep, recv = after((keeps[0], recvs[0]), text_part)
    mixed = [attend(place, keep, recv), None]
    blocks = [grid_exchange(mixed[0]), None]
    keep, recv = after((keeps[1], recvs[1]), mixed[0], text_levels)
    mixed[1] = attend(place, keep, recv)
    blocks[1] = grid_exchange(mixed[1])
    text_kv = by_distance(after(text_levels, mixed[1]), level)
    text_kv = text_kv.reshape(size, batches, count, text_kv.shape[-1])
    middle_pieces = far_gather(after(middle_near, mixed[1]))
    feed_near = near_gather(after(jnp.concatenate([hidden_up, hidden_down.T], axis=1), middle_near))
    kept, third = [None] * 2, [None] * 2
    kept[0] = middle_forward(place, after(blocks[0], mixed[1]), frames, 0, gains, middle_pieces, text_kv)
    third[0] = level_gather(kept[0][-1])
    kept[1] = middle_forward(
        place, after(blocks[1], kept[0][-1]), frames, 1, gains, middle_pieces, text_kv
    )
    third[1] = level_gather(kept[1][-1])
    feed_pieces = far_gather(after(feed_near, kept[1][-1]))
    third[0] = after(third[0], kept[1][-1])
    activated, grad_inner, d3, fed, parts = ([None] * 2 for _ in range(5))
    activated[0], grad_inner[0], d3[0], fed[0], parts[0] = feed(
        place, third[0], cotangent, live, 0, size, feed_pieces
    )
    third[1] = after(third[1], d3[0])
    activated[1], grad_inner[1], d3[1], fed[1], parts[1] = feed(
        place, third[1], cotangent, live, 1, size, feed_pieces
    )
    part_sums = [level_exchange(part.reshape(size, -1, part.shape[1])) for part in parts]
    out_branches = []
    for m in range(batches):
        fed_sum = lax.psum_scatter(
            after(fed[m], part_sums) if m == 0 else fed[m], LEVELS, scatter_dimension=0, tiled=True
        )
        rows = own_rows(frames[m, 0], level, size)
        out_branches.append(low(kept[m][5] - rows + wide(fed_sum)))
    branches = [lax.all_gather(rows, LEVELS, axis=0, tiled=True) for rows in out_branches]

    ff = hidden_up.shape[1]
    feed_grad, feed_far = outer_blocks(
        place,
        [
            ([(third[m], after(grad_inner[m], part_sums[0])) for m in range(batches)], [(0, 0, ff)]),
            ([(d3[m], activated[m]) for m in range(batches)], [(0, ff, ff)]),
        ],
        2 * ff,
    )
    feed_far = core_swap(feed_far)
    later = [None] * 2

    def swap_levels(rows):
        return level_exchange(rows.reshape(size, -1, rows.shape[1]))

    def back(m, sums):
        result = middle_back(
            place, sums, cotangent, live, m, kept[m][:-1], gains, middle_pieces, text_kv
        )
        return result

    later[0] = back(0, after(part_sums[0], feed_grad))
    back_blocks = [grid_exchange(later[0][0]), None]
    feed_sums = plane_join(place, after(feed_grad, later[0][1]), feed_far)
    feed_moved = plane_spread(feed_sums)
    later[1] = back(1, after(part_sums[1], feed_sums))
    back_blocks[1] = grid_exchange(later[1][0])
    middle_grad, middle_far = outer_blocks(
        place,
        [
            (
                [(kept[m][2], after(later[m][3], back_blocks[0])) for m in range(batches)],
                [(step * 384, step * 1280, 384) for step in range(size)],
            ),
            (
                [(later[m][1], kept[m][0]) for m in range(batches)],
                [(step * 512, step * 1280 + 384, 512) for step in range(size)],
            ),
            (
                [(later[m][2], kept[m][4]) for m in range(batches)],
                [(step * 384, step * 1280 + 896, 384) for step in range(size)],
            ),
        ],
        1280 * size,
    )
    middle_far = core_swap(middle_far)
    text_parts = jnp.concatenate([r[5] for r in later], axis=0)
    text_parts = text_parts.reshape(text_parts.shape[0], size, -1).swapaxes(0, 1)
    text_shares = level_exchange(by_distance(after(text_parts, back_blocks), level))
    grad_keep, grad_send = [None] * 2, [None] * 2
    grad_keep[0], grad_send[0] = attend_back(
        place, keeps[0], recvs[0], after(back_blocks[0], middle_grad, back_blocks[1])
    )
    grad_recv = [side_swap(grad_send[0]), None]
    text_sum = low(jnp.sum(wide(after(text_shares, grad_keep[0])), axis=0))
    text_swap = side_swap(text_sum)
    text_sum = low(wide(text_sum) + wide(text_swap))
    middle_sums = plane_join(place, after(middle_grad, text_sum, feed_moved), middle_far)
    grad_keep[1], grad_send[1] = attend_back(
        place, keeps[1], recvs[1], after(back_blocks[1], middle_sums)
    )
    grad_recv[1] = side_swap(grad_send[1])
    middle_moved = plane_spread(middle_sums, grad_recv)
    first = [None] * 2
    keep, recv = after((grad_keep[0], grad_recv[0]), grad_keep[1], out_branches[0])
    first[0] = first_part(place, keep, recv, qkv_pieces)
    first_moved = [swap_levels(first[0]), None]
    keep, recv = after((grad_keep[1], grad_recv[1]), first[0], out_branches[1])
    first[1] = first_part(place, keep, recv, qkv_pieces)
    first_moved[1] = swap_levels(first[1])
    text_side = lax.dynamic_slice_in_dim(text, side * (count // 2), count // 2, 1)
    sum_side = lax.dynamic_slice_in_dim(
        text_sum.reshape(batches, count, -1), side * (count // 2), count // 2, 1
    )
    qkv_grad, qkv_far = outer_blocks(
        place,
        [
            (
                [(hidden[m], after(grad_keep[m], first[1], first_moved[0])) for m in range(batches)],
                [(0, lambda at: at[0] * 640, 640)],
            ),
            (
                [(hidden[m], grad_recv[m]) for m in range(batches)],
                [(0, lambda at: (1 - at[0]) * 640, 640)],
            ),
            (
                [
                    (
                        text_side.reshape(-1, text.shape[-1]),
                        sum_side.reshape(-1, text_sum.shape[-1]),
                    )
                ],
                [(0, TEXT_LANE, text_sum.shape[-1])],
            ),
        ],
        TEXT_LANE + text_sum.shape[-1],
    )
    qkv_far = core_swap(qkv_far)
    qkv_sums = plane_join(place, after(qkv_grad, first_moved[0]), qkv_far)
    qkv_moved = plane_spread(qkv_sums)
    last = [None] * 2
    last[0] = last_part(
        place, after(first_moved[0], qkv_sums), later[0][4], frames, cotangent, live, 0, gains
    )
    frame_branches = [level_gather(last[0][0]), None]
    last[1] = last_part(
        place, after(first_moved[1], last[0][0]), later[1][4], frames, cotangent, live, 1, gains
    )
    frame_branches[1] = level_gather(last[1][0])
    text_back = apply_pieces(place, after(text_sum, last[1][0]), qkv_pieces, True)
    text_own = lax.dynamic_slice_in_dim(
        text_back.reshape(batches, count, -1), side * (count // 2), count // 2, 1
    )
    text_own = text_own.reshape(batches * count // 2, size, -1).swapaxes(0, 1)
    text_moved = level_exchange(text_own)
    feed_own = total_of(feed_moved)
    middle_own = total_of(after(middle_moved, last[1][0]))
    middle_own = low(middle_own).reshape(block, size, -1).swapaxes(0, 1)
    middle_sum = jnp.sum(wide(level_exchange(by_distance(middle_own, level))), axis=0)
    out_frames = place_rows(place, frames, ones, after(branches, last[1][0]))
    frame_grads = place_rows(place, cotangent, live, frame_branches)
    qkv_own = total_of(qkv_moved)
    text_own_grad = qkv_own[:, TEXT_LANE:]
    text_grad = jnp.sum(wide(text_moved), axis=0).reshape(batches, count // 2, -1)
    first_sums = [r[1] for r in last]

    norm_sums = jnp.concatenate([sum(first_sums), sum(r[6] for r in later)], axis=0)
    norm_sums = norm_sums.reshape(6, 8, block).swapaxes(0, 1).reshape(8, 6 * block)
    norm_near, norm_far = disassemble(norm_sums, index)
    norm_own = norm_near[:, 0] + plane_move(norm_far[:, 0], 1, 0, 0)
    norm_total = norm_own[0]
    for spot, (y, x) in enumerate(((0, 1), (1, 0), (1, 1))):
        norm_total = norm_total + plane_move(norm_own[spot + 1], 0, y, x)
    norm_total = sum(z_gather(norm_total)).reshape(6, block)

    first = [unpack_heads(qkv_own[:, :640]), unpack_heads(qkv_own[:, 640:TEXT_LANE])]
    q_own, k_own, v_own = (jnp.concatenate([a, b], axis=1) for a, b in zip(*first))
    so_own = jnp.concatenate(
        [unpack_mixed(middle_sum[:, 384:640]), unpack_mixed(middle_sum[:, 640:896])], axis=1
    )
    return (
        out_frames,
        frame_grads,
        text_grad[:, None],
        norm_total[0],
        norm_total[1],
        norm_total[2],
        norm_total[3],
        norm_total[4],
        norm_total[5],
        q_own,
        k_own,
        v_own,
        so_own.T,
        middle_sum[:, :384],
        text_own_grad[:, :384],
        text_own_grad[:, 384:],
        middle_sum[:, 896:].T,
        feed_own[:, :ff],
        feed_own[:, ff:].T,
    )


def per_device(mesh):
    sizes = dict(mesh.shape)

    def dispatch(*args):
        frames, self_query, hidden_up = args[0], args[10], args[18]
        fits = (
            sizes[DATA] == 4
            and sizes[SIDES] == 2
            and sizes[LEVELS] == 4
            and frames.shape[0] == 2
            and frames.shape[1] == 1
            and frames.shape[2] % (16 * sizes[LEVELS]) == 0
            and self_query.shape[1] == 6 * HD
            and self_query.shape[0] * 8 == frames.shape[3]
        )
        return (shards if fits else general_shards)(*args)

    return dispatch


def solution(mesh):
    return jax.shard_map(
        per_device(mesh),
        mesh=mesh,
        in_specs=(
            P(None, DATA, SIDES, None),
            P(None, DATA, None, None),
            P(None, DATA, SIDES, None),
            P(None, DATA),
            P((DATA, SIDES)),
            P((DATA, SIDES)),
            P((DATA, SIDES)),
            P((DATA, SIDES)),
            P((DATA, SIDES)),
            P((DATA, SIDES)),
            P((DATA, SIDES), LEVELS),
            P((DATA, SIDES), LEVELS),
            P((DATA, SIDES), LEVELS),
            P(LEVELS, (DATA, SIDES)),
            P((DATA, SIDES), LEVELS),
            P((DATA, SIDES), LEVELS),
            P((DATA, SIDES), LEVELS),
            P(LEVELS, (DATA, SIDES)),
            P((DATA, SIDES), LEVELS),
            P(LEVELS, (DATA, SIDES)),
        ),
        out_specs=(
            P(None, DATA, SIDES, None),
            P(None, DATA, SIDES, None),
            P(None, DATA, SIDES, LEVELS),
            P((DATA, SIDES)),
            P((DATA, SIDES)),
            P((DATA, SIDES)),
            P((DATA, SIDES)),
            P((DATA, SIDES)),
            P((DATA, SIDES)),
            P((DATA, SIDES), LEVELS),
            P((DATA, SIDES), LEVELS),
            P((DATA, SIDES), LEVELS),
            P(LEVELS, (DATA, SIDES)),
            P((DATA, SIDES), LEVELS),
            P((DATA, SIDES), LEVELS),
            P((DATA, SIDES), LEVELS),
            P(LEVELS, (DATA, SIDES)),
            P((DATA, SIDES), LEVELS),
            P(LEVELS, (DATA, SIDES)),
        ),
        check_vma=False,
    )
```

```python
import functools

import jax
import jax.numpy as jnp
from jax import lax
from jax.experimental import pallas as pl
from jax.experimental.pallas import tpu as pltpu
from jax.sharding import PartitionSpec as P

HD = 64
PAIRS, MIXES, TURNED = "cihd,cjhd->chij", "chij,cjhd->cihd", "chij,cihd->cjhd"
DATA, SIDES, LEVELS = "dp", "context", "tensor"


epsilon = 1e-05
masked_score = -1e30


def layer_norm(values, norm_gain, norm_shift):
    centre = values - jnp.mean(values, axis=-1, keepdims=True)
    spread = jnp.mean(centre * centre, axis=-1, keepdims=True)
    return centre * lax.rsqrt(spread + epsilon) * norm_gain + norm_shift


def exact_gelu(values):
    return jax.nn.gelu(values, approximate=False)


def matmul(former, latter):
    return jnp.dot(former, latter, preferred_element_type=jnp.float32)


def against(former, latter):
    return lax.dot_general(
        former, latter, (((former.ndim - 1,), (1,)), ((), ())), preferred_element_type=jnp.float32
    )


def outer_sum(former, latter):
    flat_former = former.reshape(-1, former.shape[-1])
    flat_latter = latter.reshape(-1, latter.shape[-1])
    return lax.dot_general(
        flat_former, flat_latter, (((0,), (0,)), ((), ())), preferred_element_type=jnp.float32
    )


def split_heads(values):
    return values.reshape(values.shape[0], values.shape[1], values.shape[2] // HD, HD)


def join_heads(values):
    return values.reshape(values.shape[0], values.shape[1], values.shape[2] * values.shape[3])


def head_scores(queries, key_rows, offset, causal, key_offset=0):
    scores = jnp.einsum(
        PAIRS,
        split_heads(queries),
        split_heads(key_rows),
        preferred_element_type=jnp.float32,
    ) * HD ** (-0.5)
    if causal:
        shape_ij = (queries.shape[1], key_rows.shape[1])
        query_pos = offset + lax.broadcasted_iota(jnp.int32, shape_ij, 0)
        key_pos = key_offset + lax.broadcasted_iota(jnp.int32, shape_ij, 1)
        scores = jnp.where(key_pos <= query_pos, scores, masked_score)
    return scores


def softmax_parts(scores):
    top_score = jnp.max(scores, axis=-1, keepdims=True)
    scaled = jnp.exp(scores - top_score)
    row_total = jnp.sum(scaled, axis=-1, keepdims=True)
    return (scaled / row_total, top_score + jnp.log(row_total))


def mix_heads(weights, value_rows):
    return join_heads(
        jnp.einsum(
            MIXES, weights, split_heads(value_rows), preferred_element_type=jnp.float32
        )
    )


def attention_back(queries, key_rows, value_rows, grad_mixed, log_total, offset, causal):
    probability = jnp.exp(head_scores(queries, key_rows, offset, causal) - log_total)
    grad_probs = jnp.einsum(
        PAIRS,
        split_heads(grad_mixed),
        split_heads(value_rows),
        preferred_element_type=jnp.float32,
    )
    inner_sum = jnp.sum(grad_probs * probability, axis=-1, keepdims=True)
    grad_scores = (probability * (grad_probs - inner_sum)).astype(jnp.bfloat16)
    score_scale = HD ** (-0.5)
    grad_queries = join_heads(
        jnp.einsum(
            MIXES,
            grad_scores,
            split_heads(key_rows),
            preferred_element_type=jnp.float32,
        )
        * score_scale
    )
    grad_keys = join_heads(
        jnp.einsum(
            TURNED, grad_scores, split_heads(queries), preferred_element_type=jnp.float32
        )
        * score_scale
    )
    grad_values = join_heads(
        jnp.einsum(
            TURNED,
            probability.astype(jnp.bfloat16),
            split_heads(grad_mixed),
            preferred_element_type=jnp.float32,
        )
    )
    return (grad_queries.astype(jnp.bfloat16), inner_sum, grad_keys, grad_values)


def branch_sum(values):
    return lax.psum(values, LEVELS)


def back_sum(values):
    return lax.psum(values.astype(jnp.bfloat16), LEVELS).astype(jnp.float32)


def reduce_grads(row_terms, col_terms):
    row_sums = (
        lax.psum_scatter(
            row_terms[0].astype(jnp.bfloat16), (DATA, SIDES), scatter_dimension=0, tiled=True
        ).astype(jnp.float32),
        lax.psum_scatter(
            row_terms[1].astype(jnp.bfloat16), (DATA, SIDES), scatter_dimension=0, tiled=True
        ).astype(jnp.float32),
        lax.psum_scatter(
            row_terms[2].astype(jnp.bfloat16), (DATA, SIDES), scatter_dimension=0, tiled=True
        ).astype(jnp.float32),
        lax.psum_scatter(
            row_terms[3].astype(jnp.bfloat16), (DATA, SIDES), scatter_dimension=0, tiled=True
        ).astype(jnp.float32),
        lax.psum_scatter(
            row_terms[4].astype(jnp.bfloat16), (DATA, SIDES), scatter_dimension=0, tiled=True
        ).astype(jnp.float32),
        lax.psum_scatter(
            row_terms[5].astype(jnp.bfloat16), (DATA, SIDES), scatter_dimension=0, tiled=True
        ).astype(jnp.float32),
        lax.psum_scatter(
            row_terms[6].astype(jnp.bfloat16), (DATA, SIDES), scatter_dimension=0, tiled=True
        ).astype(jnp.float32),
        lax.psum_scatter(
            row_terms[7].astype(jnp.bfloat16), (DATA, SIDES), scatter_dimension=0, tiled=True
        ).astype(jnp.float32),
        lax.psum_scatter(
            row_terms[8].astype(jnp.bfloat16), (DATA, SIDES), scatter_dimension=0, tiled=True
        ).astype(jnp.float32),
        lax.psum_scatter(
            row_terms[9].astype(jnp.bfloat16), (DATA, SIDES), scatter_dimension=0, tiled=True
        ).astype(jnp.float32),
        lax.psum_scatter(
            row_terms[10].astype(jnp.bfloat16), (DATA, SIDES), scatter_dimension=0, tiled=True
        ).astype(jnp.float32),
        lax.psum_scatter(
            row_terms[11].astype(jnp.bfloat16), (DATA, SIDES), scatter_dimension=0, tiled=True
        ).astype(jnp.float32),
        lax.psum_scatter(
            row_terms[12].astype(jnp.bfloat16), (DATA, SIDES), scatter_dimension=0, tiled=True
        ).astype(jnp.float32),
    )
    col_sums = (
        lax.psum_scatter(
            col_terms[0].astype(jnp.bfloat16), (DATA, SIDES), scatter_dimension=1, tiled=True
        ).astype(jnp.float32),
        lax.psum_scatter(
            col_terms[1].astype(jnp.bfloat16), (DATA, SIDES), scatter_dimension=1, tiled=True
        ).astype(jnp.float32),
        lax.psum_scatter(
            col_terms[2].astype(jnp.bfloat16), (DATA, SIDES), scatter_dimension=1, tiled=True
        ).astype(jnp.float32),
    )
    return (row_sums, col_sums)


def general_shards(
    frames,
    text_states,
    cotangent,
    clip_live,
    first_gain,
    first_bias,
    second_gain,
    second_bias,
    third_gain,
    third_bias,
    self_query,
    self_key,
    self_value,
    self_output,
    cross_query,
    cross_key,
    cross_value,
    cross_output,
    hidden_up,
    hidden_down,
):
    row_weights = (
        lax.all_gather(first_gain, (DATA, SIDES), axis=0, tiled=True),
        lax.all_gather(first_bias, (DATA, SIDES), axis=0, tiled=True),
        lax.all_gather(second_gain, (DATA, SIDES), axis=0, tiled=True),
        lax.all_gather(second_bias, (DATA, SIDES), axis=0, tiled=True),
        lax.all_gather(third_gain, (DATA, SIDES), axis=0, tiled=True),
        lax.all_gather(third_bias, (DATA, SIDES), axis=0, tiled=True),
        lax.all_gather(self_query, (DATA, SIDES), axis=0, tiled=True),
        lax.all_gather(self_key, (DATA, SIDES), axis=0, tiled=True),
        lax.all_gather(self_value, (DATA, SIDES), axis=0, tiled=True),
        lax.all_gather(cross_query, (DATA, SIDES), axis=0, tiled=True),
        lax.all_gather(cross_key, (DATA, SIDES), axis=0, tiled=True),
        lax.all_gather(cross_value, (DATA, SIDES), axis=0, tiled=True),
        lax.all_gather(hidden_up, (DATA, SIDES), axis=0, tiled=True),
    )
    col_weights = (
        lax.all_gather(self_output, (DATA, SIDES), axis=1, tiled=True),
        lax.all_gather(cross_output, (DATA, SIDES), axis=1, tiled=True),
        lax.all_gather(hidden_down, (DATA, SIDES), axis=1, tiled=True),
    )
    norm_params = [member.astype(jnp.float32) for member in row_weights[:6]]
    query_full, key_full, value_full = (row_weights[6], row_weights[7], row_weights[8])
    cross_query_full, cross_key_full, cross_value_full = (
        row_weights[9],
        row_weights[10],
        row_weights[11],
    )
    up_full = row_weights[12]
    output_full, cross_output_full, down_full = col_weights
    context_index = lax.axis_index(SIDES)
    offset = context_index * frames.shape[2]
    text_share = text_states.shape[2] // lax.axis_size(SIDES)
    row_total = None
    col_total = None
    outputs = []
    input_grads = []
    text_grads = []
    for micro_batch in range(frames.shape[0]):
        block = frames[micro_batch]
        text_block = text_states[micro_batch]
        normed_first, first_back = jax.vjp(layer_norm, block, norm_params[0], norm_params[1])
        normed_one = normed_first.astype(jnp.bfloat16)
        queries = matmul(normed_one, query_full).astype(jnp.bfloat16)
        key_local = matmul(normed_one, key_full).astype(jnp.bfloat16)
        value_local = matmul(normed_one, value_full).astype(jnp.bfloat16)
        key_rows, value_rows = (
            lax.all_gather(key_local, SIDES, axis=1, tiled=True),
            lax.all_gather(value_local, SIDES, axis=1, tiled=True),
        )
        probability, log_total = softmax_parts(head_scores(queries, key_rows, offset, True))
        mixed = mix_heads(probability.astype(jnp.bfloat16), value_rows).astype(jnp.bfloat16)
        after_self = block + branch_sum(matmul(mixed, output_full))
        normed_second, second_back = jax.vjp(layer_norm, after_self, norm_params[2], norm_params[3])
        normed_two = normed_second.astype(jnp.bfloat16)
        cross_queries = matmul(normed_two, cross_query_full).astype(jnp.bfloat16)
        text_keys = matmul(text_block, cross_key_full).astype(jnp.bfloat16)
        text_values = matmul(text_block, cross_value_full).astype(jnp.bfloat16)
        cross_probs, cross_total = softmax_parts(head_scores(cross_queries, text_keys, 0, False))
        crossed = mix_heads(cross_probs.astype(jnp.bfloat16), text_values).astype(jnp.bfloat16)
        after_cross = after_self + branch_sum(matmul(crossed, cross_output_full))
        normed_third, third_back = jax.vjp(layer_norm, after_cross, norm_params[4], norm_params[5])
        normed_three = normed_third.astype(jnp.bfloat16)
        inner = matmul(normed_three, up_full)
        gelu_value, gelu_back = jax.vjp(exact_gelu, inner)
        activated = gelu_value.astype(jnp.bfloat16)
        outputs.append(after_cross + branch_sum(matmul(activated, down_full)))
        live_weight = clip_live[micro_batch].astype(jnp.float32)[:, None, None]
        grad_result = cotangent[micro_batch] * live_weight
        grad_branch = grad_result.astype(jnp.bfloat16)
        grad_down = outer_sum(activated, grad_branch)
        grad_inner = gelu_back(against(grad_branch, down_full))[0].astype(jnp.bfloat16)
        grad_up = outer_sum(normed_three, grad_inner)
        grad_cross_in, grad_gain_three, grad_bias_three = third_back(
            back_sum(against(grad_inner, up_full))
        )
        grad_after_cross = grad_result + grad_cross_in
        grad_branch = grad_after_cross.astype(jnp.bfloat16)
        grad_cross_output = outer_sum(crossed, grad_branch)
        grad_crossed = against(grad_branch, cross_output_full).astype(jnp.bfloat16)
        grad_cross_act, cross_inner, text_key_part, text_value_part = attention_back(
            cross_queries, text_keys, text_values, grad_crossed, cross_total, 0, False
        )
        text_key_sum, text_value_sum = (
            lax.psum_scatter(
                text_key_part.astype(jnp.bfloat16), SIDES, scatter_dimension=1, tiled=True
            ).astype(jnp.float32),
            lax.psum_scatter(
                text_value_part.astype(jnp.bfloat16), SIDES, scatter_dimension=1, tiled=True
            ).astype(jnp.float32),
        )
        text_key_grad = text_key_sum.astype(jnp.bfloat16)
        text_value_grad = text_value_sum.astype(jnp.bfloat16)
        text_slice = lax.dynamic_slice_in_dim(text_block, context_index * text_share, text_share, 1)
        grad_cross_query = outer_sum(normed_two, grad_cross_act)
        grad_cross_key = outer_sum(text_slice, text_key_grad)
        grad_cross_value = outer_sum(text_slice, text_value_grad)
        text_part = against(text_key_grad, cross_key_full) + against(
            text_value_grad, cross_value_full
        )
        text_grads.append(
            lax.psum_scatter(
                text_part.astype(jnp.bfloat16), LEVELS, scatter_dimension=2, tiled=True
            ).astype(jnp.float32)
        )
        grad_self_in, grad_gain_two, grad_bias_two = second_back(
            back_sum(against(grad_cross_act, cross_query_full))
        )
        grad_after_self = grad_after_cross + grad_self_in
        grad_branch = grad_after_self.astype(jnp.bfloat16)
        grad_self_output = outer_sum(mixed, grad_branch)
        grad_mixed = against(grad_branch, output_full).astype(jnp.bfloat16)
        back_keys, back_values = (key_rows, value_rows)
        grad_query_act, self_inner, key_part, value_part = attention_back(
            queries, back_keys, back_values, grad_mixed, log_total, offset, True
        )
        key_sum, value_sum = (
            lax.psum_scatter(
                key_part.astype(jnp.bfloat16), SIDES, scatter_dimension=1, tiled=True
            ).astype(jnp.float32),
            lax.psum_scatter(
                value_part.astype(jnp.bfloat16), SIDES, scatter_dimension=1, tiled=True
            ).astype(jnp.float32),
        )
        key_grad = key_sum.astype(jnp.bfloat16)
        value_grad = value_sum.astype(jnp.bfloat16)
        grad_self_query = outer_sum(normed_one, grad_query_act)
        grad_self_key = outer_sum(normed_one, key_grad)
        grad_self_value = outer_sum(normed_one, value_grad)
        normed_grad = back_sum(
            against(grad_query_act, query_full)
            + against(key_grad, key_full)
            + against(value_grad, value_full)
        )
        grad_frames_in, grad_gain_one, grad_bias_one = first_back(normed_grad)
        input_grads.append(grad_after_self + grad_frames_in)
        row_terms = (
            grad_gain_one,
            grad_bias_one,
            grad_gain_two,
            grad_bias_two,
            grad_gain_three,
            grad_bias_three,
            grad_self_query,
            grad_self_key,
            grad_self_value,
            grad_cross_query,
            grad_cross_key,
            grad_cross_value,
            grad_up,
        )
        col_terms = (grad_self_output, grad_cross_output, grad_down)
        if row_total is None:
            row_total, col_total = (row_terms, col_terms)
        else:
            row_total = jax.tree.map(jnp.add, row_total, row_terms)
            col_total = jax.tree.map(jnp.add, col_total, col_terms)
    row_total, col_total = reduce_grads(row_total, col_total)
    return (
        jnp.stack(outputs),
        jnp.stack(input_grads),
        jnp.stack(text_grads),
        row_total[0],
        row_total[1],
        row_total[2],
        row_total[3],
        row_total[4],
        row_total[5],
        row_total[6],
        row_total[7],
        row_total[8],
        col_total[0],
        row_total[9],
        row_total[10],
        row_total[11],
        col_total[1],
        row_total[12],
        col_total[2],
    )


def norm_stats(values):
    centre = values - jnp.mean(values, axis=-1, keepdims=True)
    rate = lax.rsqrt(jnp.mean(centre * centre, axis=-1, keepdims=True) + epsilon)
    return centre * rate, rate


def norm_back(grads, gain, normed, rate):
    scaled = grads * gain
    first = jnp.mean(scaled, axis=-1, keepdims=True)
    second = jnp.mean(scaled * normed, axis=-1, keepdims=True)
    return rate * (scaled - first - normed * second)


def low(values):
    return values.astype(jnp.bfloat16)


def wide(values):
    return values.astype(jnp.float32)


def plane_perm(sizes, core, row, col):
    dp, ctx = sizes
    return [
        (d * ctx + x, ((d ^ core) ^ (2 * row)) * ctx + (x ^ col)) for d in range(dp) for x in range(ctx)
    ]


def plane_move(values, core, row, col):
    sizes = (lax.axis_size(DATA), lax.axis_size(SIDES))
    return lax.ppermute(values, (DATA, SIDES), plane_perm(sizes, core, row, col))


def z_move(values, step):
    size = lax.axis_size(LEVELS)
    return lax.ppermute(values, LEVELS, [(k, (k + step) % size) for k in range(size)])


def side_swap(values):
    return lax.ppermute(values, SIDES, [(0, 1), (1, 0)])


OFFSETS = [(c, y, x) for c in range(2) for y in range(2) for x in range(2)]
BITS = [y * 4 + c * 2 + x for c, y, x in OFFSETS]


def after(values, *earlier):
    return lax.optimization_barrier((values, earlier))[0]


def near_gather(shard, *released):
    late = after(shard, *released) if released else shard
    return [shard, plane_move(late, 0, 0, 1), plane_move(shard, 0, 1, 0), plane_move(late, 0, 1, 1)]


def far_gather(near):
    return near + [plane_move(piece, 1, 0, 0) for piece in near]


def z_gather(piece):
    return [piece] + [z_move(piece, step) for step in range(1, lax.axis_size(LEVELS))]


def block_order(index):
    inverse = [0] * 8
    for place, bits in enumerate(BITS):
        inverse[bits] = place
    return jnp.asarray(inverse)[jnp.arange(8) ^ index]


def assemble(pieces, index):
    stacked = jnp.stack(pieces)[block_order(index)]
    return stacked.reshape(-1, stacked.shape[-1])


def disassemble(whole, index):
    blocks = whole.reshape(8, whole.shape[0] // 8, whole.shape[1])
    blocks = blocks[jnp.asarray(BITS) ^ index]
    return blocks[:4], blocks[4:]


def pack_heads(q, k, v):
    return jnp.concatenate(
        [q[:, :128], k[:, :128], v[:, :128], q[:, 128:], v[:, 128:], k[:, 128:], jnp.zeros_like(q[:, :64])],
        axis=1,
    )


def unpack_heads(packed):
    q = jnp.concatenate([packed[:, 0:128], packed[:, 384:448]], axis=1)
    k = jnp.concatenate([packed[:, 128:256], packed[:, 512:576]], axis=1)
    v = jnp.concatenate([packed[:, 256:384], packed[:, 448:512]], axis=1)
    return q, k, v


def pack_mixed(o):
    return jnp.concatenate([o[:, :128], jnp.zeros_like(o[:, :64]), o[:, 128:]], axis=1)


def unpack_mixed(packed):
    return jnp.concatenate([packed[:, :128], packed[:, 192:256]], axis=1)


def grid_exchange(rows):
    return lax.all_to_all(rows, (SIDES, LEVELS), 0, 0, tiled=True)


def level_gather(rows):
    return level_exchange(rows).reshape(-1, rows.shape[-1])


def by_distance(blocks, level):
    size = blocks.shape[0]
    return blocks[(level + size - jnp.arange(size)) % size]


def repeat_levels(rows, size):
    return jnp.broadcast_to(rows[None], (size, *rows.shape))


def level_exchange(rows):
    return lax.all_to_all(rows, LEVELS, 0, 0, tiled=True)


GRANT = 62 * 2**20
TEXT_LANE = 1280
LANES = 128


def any_spec():
    return pl.BlockSpec(memory_space=pl.ANY)


def full_spec(shape):
    return pl.BlockSpec(shape, lambda *_: (0,) * len(shape))


def run_kernel(kernel, name, grid, place, operands, in_specs, outs, out_specs, scratch, flops=0, moved=0):
    return pl.pallas_call(
        kernel,
        out_shape=outs,
        grid_spec=pltpu.PrefetchScalarGridSpec(
            num_scalar_prefetch=1,
            grid=grid,
            in_specs=in_specs,
            out_specs=out_specs,
            scratch_shapes=scratch,
        ),
        compiler_params=pltpu.CompilerParams(vmem_limit_bytes=GRANT),
        cost_estimate=pl.CostEstimate(flops=1, bytes_accessed=1, transcendentals=0),
        name=name,
    )(place, *operands)


def shape_of(shape, dtype=jnp.bfloat16):
    return jax.ShapeDtypeStruct(tuple(shape), dtype)


def piece_copies(pieces, weights, sems, index, rows, lane=0):
    copies = []
    for place, piece in enumerate(pieces):
        start = pl.multiple_of((index ^ BITS[place]) * rows, 64)
        copies.append(
            pltpu.make_async_copy(
                piece.at[pl.ds(0, rows), pl.ds(lane, weights.shape[1])],
                weights.at[pl.ds(start, rows), :],
                sems.at[place],
            )
        )
    return copies


def start_all(copies):
    for copy in copies:
        copy.start()


def wait_all(copies):
    for copy in copies:
        copy.wait()


def nn(former, latter):
    return lax.dot_general(former, latter, (((1,), (0,)), ((), ())), preferred_element_type=jnp.float32)


def nt(former, latter):
    return lax.dot_general(former, latter, (((1,), (1,)), ((), ())), preferred_element_type=jnp.float32)


def tn(former, latter):
    return lax.dot_general(former, latter, (((0,), (0,)), ((), ())), preferred_element_type=jnp.float32)


def low_half(shape):
    return lax.broadcasted_iota(jnp.int32, shape, len(shape) - 1) < HD


def masked_half(values, upper):
    mask = low_half(values.shape)
    zero = jnp.zeros_like(values)
    return jnp.where(mask, zero, values) if upper else jnp.where(mask, values, zero)


def project_kernel(place, x_ref, gains, *rest):
    pieces, (hidden, keep, send, weights, sems) = rest[:8], rest[8:]
    first = pl.program_id(0) == 0
    rows = weights.shape[0] // 8
    copies = piece_copies(pieces, weights, sems, place[2], rows)

    @pl.when(first)
    def _():
        start_all(copies)

    normed, _ = norm_stats(x_ref[0, 0])
    value = low(normed * gains[0:1] + gains[1:2])
    hidden[...] = value

    @pl.when(first)
    def _():
        wait_all(copies)

    both = low(nn(value, weights[...]))

    @pl.when(place[0] == 0)
    def _():
        keep[...] = both[:, :640]
        send[...] = both[:, 640:]

    @pl.when(place[0] != 0)
    def _():
        keep[...] = both[:, 640:]
        send[...] = both[:, :640]


def project(place, frames, batch, gains, pieces):
    rows, width = frames.shape[2:]
    tile = 256
    outs = (shape_of((rows, width)), shape_of((rows, 640)), shape_of((rows, 640)))
    return run_kernel(
        project_kernel,
        "project",
        (rows // tile,),
        place,
        (frames, gains, *pieces),
        [pl.BlockSpec((1, 1, tile, width), lambda i, _: (batch, 0, i, 0)), full_spec(gains.shape)]
        + [any_spec()] * 8,
        outs,
        [pl.BlockSpec((tile, out.shape[1]), lambda i, _: (i, 0)) for out in outs],
        [pltpu.VMEM((width, 1280), jnp.bfloat16), pltpu.SemaphoreType.DMA((8,))],
        2 * rows * width * 1280,
        rows * width * 6 + width * 2560 + rows * 2560,
    )


HEAD_TILES = ((0, 128, 256, False), (0, 128, 256, True))
QUERY_TILE = 256


def gather_rows(place, keep, recv, packed):
    count = keep.shape[0]
    own = pl.multiple_of(place[0] * count, 256)
    other = pl.multiple_of((1 - place[0]) * count, 256)
    packed[pl.ds(own, count), :] = keep[...]
    packed[pl.ds(other, count), :] = recv[...]


def level_start(place, share, step, size):
    return pl.multiple_of(((place[1] + size - step) % size) * share, 64)


def attend_kernel(place, keep, recv, *rest):
    mixed, packed = rest
    gather_rows(place, keep, recv, packed)
    total = packed.shape[0]
    scale = HD ** (-0.5)
    tile = QUERY_TILE
    causal = lax.broadcasted_iota(jnp.int32, (tile, tile), 1) <= lax.broadcasted_iota(
        jnp.int32, (tile, tile), 0
    )
    k01 = packed[:, 128:256]
    keys = (masked_half(k01, False), masked_half(k01, True), packed[:, 512:640])
    vals = (packed[:, 256:384], packed[:, 256:384], packed[:, 384:512])
    for part in range(total // tile):
        start, stop = part * tile, part * tile + tile
        results = []
        for head in range(3):
            lanes = slice(0, 128) if head < 2 else slice(384, 512)
            q = packed[start:stop, lanes] * scale
            key, val = keys[head], vals[head]
            edge = jnp.where(causal, nt(q, key[start:stop]), masked_score)
            top = jnp.max(edge, axis=-1, keepdims=True)
            if part > 0:
                body = nt(q, key[:start])
                top = jnp.maximum(top, jnp.max(body, axis=-1, keepdims=True))
                body = jnp.exp(body - top)
            edge = jnp.exp(edge - top)
            weight = jnp.sum(edge, axis=-1, keepdims=True)
            value = nn(low(edge), val[start:stop])
            if part > 0:
                weight = weight + jnp.sum(body, axis=-1, keepdims=True)
                value = value + nn(low(body), val[:start])
            results.append(value / weight)
        mask = low_half((tile, 128))
        mixed[start:stop, 0:128] = low(jnp.where(mask, results[0], results[1]))
        mixed[start:stop, 128:256] = low(jnp.where(mask, 0.0, results[2]))


def attend(place, keep, recv):
    count = keep.shape[0]
    out = shape_of((2 * count, 256))
    return run_kernel(
        attend_kernel,
        "attend",
        (1,),
        place,
        (keep, recv),
        [full_spec(keep.shape)] * 2,
        out,
        full_spec(out.shape),
        [pltpu.VMEM((2 * count, 640), jnp.bfloat16)],
        6e9,
        count * 8000,
    )


def attend_back_kernel(place, keep, recv, mixed, keep_out, send_out, packed, grads):
    gather_rows(place, keep, recv, packed)
    total = packed.shape[0]
    scale = HD ** (-0.5)
    tile = QUERY_TILE
    causal = lax.broadcasted_iota(jnp.int32, (tile, tile), 0) <= lax.broadcasted_iota(
        jnp.int32, (tile, tile), 1
    )
    for pair in range(2):
        heads = (0, 1) if pair == 0 else (2,)
        grads_q, grads_k, grads_v = [], None, None
        sums_k = [None] * (total // tile)
        sums_v = [None] * (total // tile)
        for part in range(total // tile):
            start, stop = part * tile, part * tile + tile
            sum_q = None
            for head in heads:
                if pair == 0:
                    upper = head == 1
                    q = masked_half(packed[start:stop, 0:128], upper) * scale
                    do = masked_half(mixed[start:stop, 0:128], upper)
                    key = packed[:stop, 128:256]
                    val = packed[:stop, 256:384]
                else:
                    q = masked_half(packed[start:stop, 384:512], False) * scale
                    do = mixed[start:stop, 128:256]
                    key = packed[:stop, 512:640]
                    val = packed[:stop, 384:512]
                scores = nt(key, q)
                edge = jnp.where(causal, scores[start:stop], masked_score)
                if part > 0:
                    scores = jnp.concatenate([scores[:start], edge], axis=0)
                else:
                    scores = edge
                scores = jnp.exp(scores - jnp.max(scores, axis=0, keepdims=True))
                p = scores * (1.0 / jnp.sum(scores, axis=0, keepdims=True))
                dp = nt(val, do)
                ds = low(p * (dp - jnp.sum(dp * p, axis=0, keepdims=True)))
                p = low(p)
                new_k = nn(ds, q)
                new_v = nn(p, do)
                if pair == 0:
                    key = masked_half(key, upper)
                new_q = tn(ds, key) * scale
                sum_q = new_q if sum_q is None else sum_q + new_q
                for spot in range(part + 1):
                    rows = slice(spot * tile, spot * tile + tile)
                    sums_k[spot] = new_k[rows] if sums_k[spot] is None else sums_k[spot] + new_k[rows]
                    sums_v[spot] = new_v[rows] if sums_v[spot] is None else sums_v[spot] + new_v[rows]
            grads_q.append(sum_q)
        for part in range(total // tile):
            rows = slice(part * tile, part * tile + tile)
            if pair == 0:
                grads[rows, 0:128] = low(grads_q[part])
                grads[rows, 128:256] = low(sums_k[part])
                grads[rows, 256:384] = low(sums_v[part])
            else:
                mask = low_half((tile, 128))
                grads[rows, 384:512] = low(jnp.where(mask, grads_q[part], sums_v[part]))
                grads[rows, 512:640] = low(sums_k[part])
    count = keep.shape[0]
    keep_out[...] = grads[pl.ds(pl.multiple_of(place[0] * count, 256), count), :]
    send_out[...] = grads[pl.ds(pl.multiple_of((1 - place[0]) * count, 256), count), :]


def attend_back(place, keep, recv, mixed):
    count = keep.shape[0]
    outs = [shape_of(keep.shape)] * 2
    return run_kernel(
        attend_back_kernel,
        "attend_back",
        (1,),
        place,
        (keep, recv, mixed),
        [full_spec(keep.shape)] * 2 + [full_spec(mixed.shape)],
        outs,
        [full_spec(keep.shape)] * 2,
        [
            pltpu.VMEM((2 * count, 640), jnp.bfloat16),
            pltpu.VMEM((2 * count, 640), jnp.bfloat16),
        ],
        12e9,
        count * 8000,
    )


def pair_keys(tile):
    return jnp.concatenate([masked_half(tile, False), masked_half(tile, True)], axis=0)


def pair_softmax(scores):
    mask = low_half(scores.shape)
    tops = [
        jnp.max(jnp.where(part, scores, masked_score), axis=-1, keepdims=True) for part in (mask, ~mask)
    ]
    scaled = jnp.exp(scores - jnp.where(mask, tops[0], tops[1]))
    sums = [jnp.sum(jnp.where(part, scaled, 0.0), axis=-1, keepdims=True) for part in (mask, ~mask)]
    return scaled * jnp.where(mask, 1.0 / sums[0], 1.0 / sums[1])


def middle_kernel(place, *rest):
    size = place_size(rest)
    mixed, x_ref, gains, text = rest[:4]
    pieces, rest = rest[4:12], rest[12:]
    mixed_row, after_self, hidden, queries, crossed, after_cross, third, weights, sems = rest
    copies = piece_copies(pieces, weights, sems, place[2], weights.shape[0] // 8)
    start_all(copies)
    share = mixed_row.shape[0]
    for step in range(size):
        for spot in range(2):
            lanes = slice((step * 2 + spot) * 256, (step * 2 + spot) * 256 + 256)
            start = spot * size * share + level_start(place, share, step, size)
            mixed_row[:, lanes] = mixed[pl.ds(pl.multiple_of(start, 64), share), :]
    wait_all(copies)
    first = jnp.zeros(x_ref.shape[2:], jnp.float32)
    for step in range(size):
        first = first + nt(
            mixed_row[:, step * 512 : step * 512 + 512], weights[:, step * 1280 + 384 : step * 1280 + 896]
        )
    first = x_ref[0, 0] + first
    after_self[...] = first
    normed, _ = norm_stats(first)
    value = low(normed * gains[2:3] + gains[3:4])
    hidden[...] = value
    scale = HD ** (-0.5)
    second = jnp.zeros_like(first)
    for step in range(size):
        q = low(nn(value, weights[:, step * 1280 : step * 1280 + 384]))
        queries[:, step * 384 : step * 384 + 384] = q
        for tile in range(3):
            lanes = slice(tile * 128, tile * 128 + 128)
            keys = pair_keys(text[step, :, lanes])
            vals = pair_keys(text[step, :, tile * 128 + 384 : tile * 128 + 512])
            p = low(pair_softmax(nt(q[:, lanes], keys) * scale))
            crossed[:, step * 384 + tile * 128 : step * 384 + tile * 128 + 128] = low(nn(p, vals))
    for step in range(size):
        second = second + nt(
            crossed[:, step * 384 : step * 384 + 384], weights[:, step * 1280 + 896 : step * 1280 + 1280]
        )
    second = after_self[...] + second
    after_cross[...] = second
    normed, _ = norm_stats(second)
    value = low(normed * gains[4:5] + gains[5:6])
    for step in range(size):
        third[step] = value


def place_size(refs):
    return 4


def middle_forward(place, mixed, frames, batch, gains, pieces, text):
    size = text.shape[0]
    share = mixed.shape[0] // (2 * size)
    width = frames.shape[3]
    outs = (
        shape_of((share, 512 * size)),
        shape_of((share, width), jnp.float32),
        shape_of((share, width)),
        shape_of((share, width)),
        shape_of((share, width)),
        shape_of((share, width), jnp.float32),
        shape_of((size, share, width)),
    )
    count = text.shape[2]
    return run_kernel(
        middle_kernel,
        "middle",
        (1,),
        place,
        (mixed, frames, gains, text, *pieces),
        [
            full_spec(mixed.shape),
            pl.BlockSpec((1, 1, share, width), lambda i, at: (batch, 0, at[1], 0)),
            full_spec(gains.shape),
            pl.BlockSpec((size, None, count, text.shape[3]), lambda i, at: (0, batch, 0, 0)),
        ]
        + [any_spec()] * 8,
        outs,
        [full_spec(out.shape) for out in outs],
        [pltpu.VMEM((width, 1280 * size), jnp.bfloat16), pltpu.SemaphoreType.DMA((8,))],
        2 * share * width * 1280 * size,
        width * 2560 * size,
    )


def feed_kernel(place, third, dy, live, *rest, batch):
    pieces, (activated, grad_inner, d3_out, y, e, weights, sems) = rest[:8], rest[8:]
    turn = pl.program_id(0)
    copies = piece_copies(pieces, weights, sems, place[2], weights.shape[0] // 8)

    @pl.when(turn == 0)
    def _():
        start_all(copies)
        wait_all(copies)

    half = weights.shape[1] // 2
    value = third[...]
    d3 = low(dy[0, 0] * live[batch])
    d3_out[...] = d3
    inner = nn(value, weights[:, :half])
    bell = (1.0 + lax.erf(inner * 0.5**0.5)) * 0.5
    act = low(inner * bell)
    activated[...] = act
    slope = bell + inner * jnp.exp(-0.5 * inner * inner) * (2.0 * jnp.pi) ** (-0.5)
    grad = low(nn(d3, weights[:, half:]) * slope)
    grad_inner[...] = grad
    e[...] = low(nt(grad, weights[:, :half]))
    y[...] = low(nt(act, weights[:, half:]))


def feed(place, third, cotangent, live, batch, size, pieces):
    rows, width = third.shape
    share = rows // size
    inner = pieces[0].shape[1] // 2
    outs = (
        shape_of((rows, inner)),
        shape_of((rows, inner)),
        *[shape_of((rows, width))] * 3,
    )
    return run_kernel(
        functools.partial(feed_kernel, batch=batch),
        "feed",
        (size // 2,),
        place,
        (third, cotangent, live, *pieces),
        [
            pl.BlockSpec((2 * share, width), lambda i, _: (i, 0)),
            pl.BlockSpec((1, 1, 2 * share, width), lambda i, _: (batch, 0, i, 0)),
            pl.BlockSpec(memory_space=pltpu.SMEM),
        ]
        + [any_spec()] * 8,
        outs,
        [pl.BlockSpec((2 * share, out.shape[1]), lambda i, _: (i, 0)) for out in outs],
        [pltpu.VMEM((width, 2 * inner), jnp.bfloat16), pltpu.SemaphoreType.DMA((8,))],
        8 * rows * width * inner,
        rows * width * 20,
    )


def middle_back_kernel(place, *rest, batch):
    size = place_size(rest)
    parts, rest = rest[0], rest[1:]
    dy_ref, live, gains, text = rest[:4]
    mixed_row, after_self_ref, hidden, queries, crossed, after_cross_ref = rest[4:10]
    pieces, rest = rest[10:18], rest[18:]
    blocks, rest = rest[0], rest[1:]
    d1_out, d2_out, dcq_out, grad_self_out, text_out, sums, weights, sems = rest
    copies = piece_copies(pieces, weights, sems, place[2], weights.shape[0] // 8)
    start_all(copies)
    third_grad = wide(parts[0])
    for step in range(1, size):
        third_grad = third_grad + wide(parts[step])
    after_cross = after_cross_ref[...]
    normed, rate = norm_stats(after_cross)
    sums[2:3] = jnp.sum(third_grad * normed, axis=0, keepdims=True)
    sums[3:4] = jnp.sum(third_grad, axis=0, keepdims=True)
    grad_cross = dy_ref[0, 0] * live[batch] + norm_back(third_grad, gains[4:5], normed, rate)
    d2 = low(grad_cross)
    d2_out[...] = d2
    wait_all(copies)
    scale = HD ** (-0.5)
    half_mask = low_half((text.shape[1], 128))
    for step in range(size):
        grad_crossed = low(nn(d2, weights[:, step * 1280 + 896 : step * 1280 + 1280]))
        for tile in range(3):
            lanes = slice(tile * 128, tile * 128 + 128)
            q = queries[:, step * 384 + tile * 128 : step * 384 + tile * 128 + 128]
            do = grad_crossed[:, lanes]
            keys = pair_keys(text[step, :, lanes])
            vals = pair_keys(text[step, :, tile * 128 + 384 : tile * 128 + 512])
            p = pair_softmax(nt(q, keys) * scale)
            dp = nt(do, vals)
            both = dp * p
            mask = low_half(both.shape)
            inner = jnp.where(
                mask,
                jnp.sum(jnp.where(mask, both, 0.0), axis=-1, keepdims=True),
                jnp.sum(jnp.where(mask, 0.0, both), axis=-1, keepdims=True),
            )
            ds = low(p * (dp - inner))
            dcq_out[:, step * 384 + tile * 128 : step * 384 + tile * 128 + 128] = low(nn(ds, keys) * scale)
            count = text.shape[1]
            dk = tn(ds, q) * scale
            dv = tn(low(p), do)
            base = step * 768 + tile * 128
            text_out[:, base : base + 128] = low(jnp.where(half_mask, dk[:count], dk[count:]))
            text_out[:, base + 384 : base + 512] = low(jnp.where(half_mask, dv[:count], dv[count:]))
    second_grad = jnp.zeros(d2.shape, jnp.float32)
    for step in range(size):
        second_grad = second_grad + nt(
            dcq_out[:, step * 384 : step * 384 + 384], weights[:, step * 1280 : step * 1280 + 384]
        )
    normed, rate = norm_stats(after_self_ref[...])
    sums[0:1] = jnp.sum(second_grad * normed, axis=0, keepdims=True)
    sums[1:2] = jnp.sum(second_grad, axis=0, keepdims=True)
    grad_self = grad_cross + norm_back(second_grad, gains[2:3], normed, rate)
    grad_self_out[...] = grad_self
    d1 = low(grad_self)
    d1_out[...] = d1
    for step in range(size):
        for spot in range(2):
            lanes = step * 1280 + 384 + spot * 256
            share = d1.shape[0]
            start = spot * size * share + level_start(place, share, step, size)
            blocks[pl.ds(pl.multiple_of(start, 64), share), :] = low(nn(d1, weights[:, lanes : lanes + 256]))


def middle_back(place, parts, cotangent, live, batch, kept, gains, pieces, text):
    size, share, width = parts.shape
    count = text.shape[2]
    outs = (
        shape_of((2 * size * share, 256)),
        shape_of((share, width)),
        shape_of((share, width)),
        shape_of((share, width)),
        shape_of((share, width), jnp.float32),
        shape_of((count, 768 * size)),
        shape_of((4, width), jnp.float32),
    )
    row_spec = pl.BlockSpec((1, 1, share, width), lambda i, at: (batch, 0, at[1], 0))
    return run_kernel(
        functools.partial(middle_back_kernel, batch=batch),
        "middle_back",
        (1,),
        place,
        (parts, cotangent, live, gains, text, *kept, *pieces),
        [
            full_spec(parts.shape),
            row_spec,
            pl.BlockSpec(memory_space=pltpu.SMEM),
            full_spec(gains.shape),
            pl.BlockSpec((size, None, count, text.shape[3]), lambda i, at: (0, batch, 0, 0)),
        ]
        + [full_spec(part.shape) for part in kept]
        + [any_spec()] * 8,
        outs,
        [full_spec(out.shape) for out in outs],
        [pltpu.VMEM((width, 1280 * size), jnp.bfloat16), pltpu.SemaphoreType.DMA((8,))],
        2 * share * width * 1280 * size,
        width * 2560 * size,
    )


def first_kernel(place, keep, recv, *rest):
    pieces, rest = rest[:8], rest[8:]
    result, weights, sems = rest
    copies = piece_copies(pieces, weights, sems, place[2], weights.shape[0] // 8)
    start_all(copies)
    wait_all(copies)

    @pl.when(place[0] == 0)
    def _():
        result[...] = low(nt(keep[...], weights[:, :640]) + nt(recv[...], weights[:, 640:]))

    @pl.when(place[0] != 0)
    def _():
        result[...] = low(nt(recv[...], weights[:, :640]) + nt(keep[...], weights[:, 640:]))


def first_part(place, keep, recv, pieces):
    rows = keep.shape[0]
    width = (pieces[0].shape[0] - 16) * 8
    out = shape_of((rows, width))
    return run_kernel(
        first_kernel,
        "first_part",
        (1,),
        place,
        (keep, recv, *pieces),
        [full_spec(keep.shape)] * 2 + [any_spec()] * 8,
        out,
        full_spec(out.shape),
        [pltpu.VMEM((width, 1280), jnp.bfloat16), pltpu.SemaphoreType.DMA((8,))],
        2 * rows * width * 1280,
        width * 2560 + rows * width * 2,
    )


def last_kernel(place, *rest, batch):
    parts, grad_self, x_ref, dy_ref, live, gains, branch, sums = rest
    total = wide(parts[0])
    for step in range(1, parts.shape[0]):
        total = total + wide(parts[step])
    normed, rate = norm_stats(x_ref[0, 0])
    sums[0:1] = jnp.sum(total * normed, axis=0, keepdims=True)
    sums[1:2] = jnp.sum(total, axis=0, keepdims=True)
    value = low(grad_self[...] + norm_back(total, gains[0:1], normed, rate) - dy_ref[0, 0] * live[batch])
    for step in range(parts.shape[0]):
        branch[step] = value


def last_part(place, parts, grad_self, frames, cotangent, live, batch, gains):
    size, share, width = parts.shape
    outs = (shape_of((size, share, width)), shape_of((2, width), jnp.float32))
    row_spec = pl.BlockSpec((1, 1, share, width), lambda i, at: (batch, 0, at[1], 0))
    return run_kernel(
        functools.partial(last_kernel, batch=batch),
        "last_part",
        (1,),
        place,
        (parts, grad_self, frames, cotangent, live, gains),
        [full_spec(parts.shape), full_spec((share, width))]
        + [row_spec, row_spec, pl.BlockSpec(memory_space=pltpu.SMEM), full_spec(gains.shape)],
        outs,
        [full_spec(out.shape) for out in outs],
        [],
        share * width * 30,
        share * width * 20,
    )


def place_kernel(place, base, live, first, second, out):
    batch = pl.program_id(0)
    grown = base[0, 0] * live[batch]

    @pl.when(batch == 0)
    def _():
        out[0, 0] = grown + wide(first[...])

    @pl.when(batch != 0)
    def _():
        out[0, 0] = grown + wide(second[...])


def place_rows(place, base, live, pieces):
    rows, width = pieces[0].shape
    tile = 256
    tiles = rows // tile
    spec = pl.BlockSpec((1, 1, tile, width), lambda m, i, at: (m, 0, i, 0))
    return run_kernel(
        place_kernel,
        "place_rows",
        (2, tiles),
        place,
        (base, live, *pieces),
        [
            spec,
            pl.BlockSpec(memory_space=pltpu.SMEM),
            pl.BlockSpec((tile, width), lambda m, i, at: (jnp.where(m == 0, i, tiles - 1), 0)),
            pl.BlockSpec((tile, width), lambda m, i, at: (jnp.where(m == 0, 0, i), 0)),
        ],
        shape_of(base.shape, jnp.float32),
        spec,
        [],
        base.size,
        base.size * 10,
    )


def outer_blocks(place, terms, width):
    operands, specs = [], []
    full = terms[0][0][0][0].shape[1]
    block = full // 8
    for pairs, _ in terms:
        for lhs, rhs in pairs:
            operands += [lhs, rhs]
            specs += [
                pl.BlockSpec((lhs.shape[0], 2 * block), lambda g, at: (0, at[3] ^ (g // 2) ^ (2 * (g % 2)))),
                full_spec(rhs.shape),
            ]

    def kernel(at, *refs):
        near, far = refs[-2:]
        turn = pl.program_id(0)
        spot = 0
        for pairs, segments in terms:
            chosen = refs[spot : spot + 2 * len(pairs)]
            spot += 2 * len(pairs)
            for start, target, count in segments:
                total = None
                for pair in range(len(pairs)):
                    value = tn(chosen[2 * pair][...], chosen[2 * pair + 1][:, start : start + count])
                    total = value if total is None else total + value
                total = low(total)
                target = pl.multiple_of(target(at), LANES) if callable(target) else target
                for col in range(2):
                    rows = total[col * block : col * block + block]

                    @pl.when(turn < 2)
                    def _():
                        near[at[0] ^ col, :, pl.ds(target, count)] = rows

                    @pl.when(turn >= 2)
                    def _():
                        far[at[0] ^ col, :, pl.ds(target, count)] = rows

    out = shape_of((4, block, width))
    rows = sum(lhs.shape[0] for pairs, _ in terms for lhs, _ in pairs)
    return run_kernel(
        kernel,
        "outer_blocks",
        (4,),
        place,
        operands,
        specs,
        (out, out),
        [
            pl.BlockSpec((2, block, width), lambda g, at: (jnp.minimum(g, 1), 0, 0)),
            pl.BlockSpec((2, block, width), lambda g, at: (jnp.maximum(g - 2, 0), 0, 0)),
        ],
        [],
        2 * rows * full * width / len(terms),
        full * width * 2 + rows * full * 4,
    )


def join_kernel(place, near, far, *outs):
    total = wide(near[...]) + wide(far[...])
    for spot, out in enumerate(outs):
        out[...] = low(total[spot])


def plane_join(place, near, far):
    count, block, width = near.shape
    tile = next(t for t in (640, 768, 1024) if width % t == 0)
    return run_kernel(
        join_kernel,
        "join",
        (width // tile,),
        place,
        (near, far),
        [pl.BlockSpec((count, block, tile), lambda i, _: (0, 0, i))] * 2,
        [shape_of((block, width))] * count,
        [pl.BlockSpec((block, tile), lambda i, _: (0, i))] * count,
        [],
        near.size,
        near.size * 6,
    )


def plane_spread(sums, *released):
    late = after(sums, *released) if released else sums
    return [sums[0], plane_move(late[1], 0, 0, 1), plane_move(sums[2], 0, 1, 0), plane_move(late[3], 0, 1, 1)]


def total_of(pieces):
    return sum(wide(piece) for piece in pieces)


def core_swap(values):
    return plane_move(values, 1, 0, 0)


def apply_kernel(place, rows, *rest, turned):
    pieces, (out, weights, sems) = rest[:8], rest[8:]
    copies = piece_copies(pieces, weights, sems, place[2], weights.shape[0] // 8, TEXT_LANE)
    start_all(copies)
    wait_all(copies)
    out[...] = low((nt if turned else nn)(rows[...], weights[...]))


def apply_pieces(place, rows, pieces, turned):
    block, width = pieces[0].shape[0] - 16, pieces[0].shape[1] - TEXT_LANE
    out = shape_of((rows.shape[0], 8 * block if turned else width))
    return run_kernel(
        functools.partial(apply_kernel, turned=turned),
        "apply",
        (1,),
        place,
        (rows, *pieces),
        [full_spec(rows.shape)] + [any_spec()] * 8,
        out,
        full_spec(out.shape),
        [pltpu.VMEM((8 * block, width), jnp.bfloat16), pltpu.SemaphoreType.DMA((8,))],
        2 * rows.shape[0] * 8 * block * width,
        8 * block * width * 2,
    )


def own_rows(rows, level, size):
    share = rows.shape[0] // size
    return lax.dynamic_slice_in_dim(rows, level * share, share, 0)


def shards(
    frames,
    text_states,
    cotangent,
    clip_live,
    first_gain,
    first_bias,
    second_gain,
    second_bias,
    third_gain,
    third_bias,
    self_query,
    self_key,
    self_value,
    self_output,
    cross_query,
    cross_key,
    cross_value,
    cross_output,
    hidden_up,
    hidden_down,
):
    side = lax.axis_index(SIDES)
    level = lax.axis_index(LEVELS)
    dp = lax.axis_index(DATA)
    index = dp * 2 + side
    place = jnp.stack([side, level, index, dp]).astype(jnp.int32)
    size = lax.axis_size(LEVELS)
    batches = frames.shape[0]
    live = clip_live.astype(jnp.float32)[:, 0]
    ones = jnp.ones_like(live)
    text = text_states[:, 0]
    text_rows = text.reshape(-1, text.shape[-1])
    count = text.shape[1]
    block = self_query.shape[0]

    half = self_query.shape[1] // 2
    norm_row = jnp.concatenate([first_gain, first_bias, second_gain, second_bias, third_gain, third_bias])
    norm_rows = jnp.zeros((16, TEXT_LANE + 2 * self_query.shape[1]), jnp.bfloat16).at[0, : 6 * block].set(norm_row)
    qkv_local = jnp.concatenate(
        [
            pack_heads(self_query[:, h], self_key[:, h], self_value[:, h])
            for h in (slice(0, half), slice(half, None))
        ]
        + [cross_key, cross_value],
        axis=1,
    )
    qkv_near = near_gather(jnp.concatenate([qkv_local, norm_rows], axis=0))
    so_turned = self_output.T
    middle_local = jnp.concatenate(
        [
            cross_query,
            pack_mixed(so_turned[:, :half]),
            pack_mixed(so_turned[:, half:]),
            cross_output.T,
        ],
        axis=1,
    )
    middle_levels = level_exchange(repeat_levels(middle_local, size))
    qkv_pieces = far_gather(qkv_near)
    norm_full = assemble([piece[block : block + 1] for piece in qkv_pieces], index)[:, : 6 * block]
    gains = wide(norm_full.reshape(8, 6, block).swapaxes(0, 1).reshape(6, -1))

    hidden, keeps, sends = [None] * 2, [None] * 2, [None] * 2
    hidden[0], keeps[0], sends[0] = project(place, frames, 0, gains, qkv_pieces)
    middle_row = by_distance(after(middle_levels, hidden[0]), level).swapaxes(0, 1)
    middle_row = middle_row.reshape(block, -1)
    hidden[1], keeps[1], sends[1] = project(place, frames, 1, after(gains, hidden[0]), qkv_pieces)
    recvs = [side_swap(send) for send in sends]
    middle_near = near_gather(after(middle_row, hidden[1]), recvs)
    text_part = apply_pieces(place, after(text_rows, hidden[1]), qkv_pieces, False)
    text_levels = level_exchange(repeat_levels(text_part, size))
    keep, recv = after((keeps[0], recvs[0]), text_part)
    mixed = [attend(place, keep, recv), None]
    blocks = [grid_exchange(mixed[0]), None]
    keep, recv = after((keeps[1], recvs[1]), mixed[0], text_levels)
    mixed[1] = attend(place, keep, recv)
    blocks[1] = grid_exchange(mixed[1])
    text_kv = by_distance(after(text_levels, mixed[1]), level)
    text_kv = text_kv.reshape(size, batches, count, text_kv.shape[-1])
    middle_pieces = far_gather(after(middle_near, mixed[1], blocks[0]))
    feed_near = near_gather(after(jnp.concatenate([hidden_up, hidden_down.T], axis=1), middle_near))
    kept, third = [None] * 2, [None] * 2
    kept[0] = middle_forward(place, after(blocks[0], mixed[1]), frames, 0, gains, middle_pieces, text_kv)
    third[0] = level_gather(kept[0][-1])
    kept[1] = middle_forward(
        place, after(blocks[1], kept[0][-1]), frames, 1, gains, middle_pieces, text_kv
    )
    third[1] = level_gather(kept[1][-1])
    feed_pieces = far_gather(after(feed_near, kept[1][-1]))
    third[0] = after(third[0], kept[1][-1])
    activated, grad_inner, d3, fed, parts = ([None] * 2 for _ in range(5))
    activated[0], grad_inner[0], d3[0], fed[0], parts[0] = feed(
        place, third[0], cotangent, live, 0, size, feed_pieces
    )
    third[1] = after(third[1], d3[0])
    activated[1], grad_inner[1], d3[1], fed[1], parts[1] = feed(
        place, third[1], cotangent, live, 1, size, feed_pieces
    )
    part_sums = [level_exchange(part.reshape(size, -1, part.shape[1])) for part in parts]
    out_branches = []
    for m in range(batches):
        fed_sum = lax.psum_scatter(
            after(fed[m], part_sums) if m == 0 else fed[m], LEVELS, scatter_dimension=0, tiled=True
        )
        rows = own_rows(frames[m, 0], level, size)
        out_branches.append(low(kept[m][5] - rows + wide(fed_sum)))
    branches = [lax.all_gather(rows, LEVELS, axis=0, tiled=True) for rows in out_branches]

    ff = hidden_up.shape[1]
    feed_grad, feed_far = outer_blocks(
        place,
        [
            ([(third[m], after(grad_inner[m], part_sums[0])) for m in range(batches)], [(0, 0, ff)]),
            ([(d3[m], activated[m]) for m in range(batches)], [(0, ff, ff)]),
        ],
        2 * ff,
    )
    feed_far = core_swap(feed_far)
    later = [None] * 2

    def swap_levels(rows):
        return level_exchange(rows.reshape(size, -1, rows.shape[1]))

    def back(m, sums):
        result = middle_back(
            place, sums, cotangent, live, m, kept[m][:-1], gains, middle_pieces, text_kv
        )
        return result

    later[0] = back(0, after(part_sums[0], feed_grad))
    back_blocks = [grid_exchange(after(later[0][0], part_sums[1])), None]
    feed_sums = plane_join(place, after(feed_grad, later[0][1]), feed_far)
    feed_moved = plane_spread(feed_sums)
    later[1] = back(1, after(part_sums[1], feed_sums))
    back_blocks[1] = grid_exchange(later[1][0])
    middle_grad, middle_far = outer_blocks(
        place,
        [
            (
                [(kept[m][2], after(later[m][3], back_blocks[0])) for m in range(batches)],
                [(step * 384, step * 1280, 384) for step in range(size)],
            ),
            (
                [(later[m][1], kept[m][0]) for m in range(batches)],
                [(step * 512, step * 1280 + 384, 512) for step in range(size)],
            ),
            (
                [(later[m][2], kept[m][4]) for m in range(batches)],
                [(step * 384, step * 1280 + 896, 384) for step in range(size)],
            ),
        ],
        1280 * size,
    )
    middle_far = core_swap(middle_far)
    text_parts = jnp.concatenate([r[5] for r in later], axis=0)
    text_parts = text_parts.reshape(text_parts.shape[0], size, -1).swapaxes(0, 1)
    text_shares = level_exchange(by_distance(after(text_parts, back_blocks), level))
    grad_keep, grad_send = [None] * 2, [None] * 2
    grad_keep[0], grad_send[0] = attend_back(
        place, keeps[0], recvs[0], after(back_blocks[0], middle_grad, back_blocks[1], feed_moved)
    )
    grad_recv = [side_swap(grad_send[0]), None]
    text_sum = low(jnp.sum(wide(after(text_shares, grad_keep[0])), axis=0))
    text_swap = side_swap(text_sum)
    text_sum = low(wide(text_sum) + wide(text_swap))
    middle_sums = plane_join(place, after(middle_grad, text_sum, feed_moved), middle_far)
    grad_keep[1], grad_send[1] = attend_back(
        place, keeps[1], recvs[1], after(back_blocks[1], middle_sums)
    )
    grad_recv[1] = side_swap(grad_send[1])
    middle_moved = plane_spread(middle_sums, grad_recv)
    first = [None] * 2
    keep, recv = after((grad_keep[0], grad_recv[0]), grad_keep[1], out_branches[0])
    first[0] = first_part(place, keep, recv, qkv_pieces)
    first_moved = [swap_levels(first[0]), None]
    keep, recv = after((grad_keep[1], grad_recv[1]), first[0], out_branches[1])
    first[1] = first_part(place, keep, recv, qkv_pieces)
    first_moved[1] = swap_levels(first[1])
    text_side = lax.dynamic_slice_in_dim(text, side * (count // 2), count // 2, 1)
    sum_side = lax.dynamic_slice_in_dim(
        text_sum.reshape(batches, count, -1), side * (count // 2), count // 2, 1
    )
    qkv_grad, qkv_far = outer_blocks(
        place,
        [
            (
                [(hidden[m], after(grad_keep[m], first[1], first_moved[0])) for m in range(batches)],
                [(0, lambda at: at[0] * 640, 640)],
            ),
            (
                [(hidden[m], grad_recv[m]) for m in range(batches)],
                [(0, lambda at: (1 - at[0]) * 640, 640)],
            ),
            (
                [
                    (
                        text_side.reshape(-1, text.shape[-1]),
                        sum_side.reshape(-1, text_sum.shape[-1]),
                    )
                ],
                [(0, TEXT_LANE, text_sum.shape[-1])],
            ),
        ],
        TEXT_LANE + text_sum.shape[-1],
    )
    qkv_far = core_swap(qkv_far)
    qkv_sums = plane_join(place, after(qkv_grad, first_moved[0]), qkv_far)
    qkv_moved = plane_spread(qkv_sums)
    last = [None] * 2
    last[0] = last_part(
        place, after(first_moved[0], qkv_sums, branches[0]), later[0][4], frames, cotangent, live, 0, gains
    )
    frame_branches = [level_gather(last[0][0]), None]
    last[1] = last_part(
        place, after(first_moved[1], last[0][0]), later[1][4], frames, cotangent, live, 1, gains
    )
    frame_branches[1] = level_gather(last[1][0])
    text_back = apply_pieces(place, after(text_sum, last[1][0]), qkv_pieces, True)
    text_own = lax.dynamic_slice_in_dim(
        text_back.reshape(batches, count, -1), side * (count // 2), count // 2, 1
    )
    text_own = text_own.reshape(batches * count // 2, size, -1).swapaxes(0, 1)
    text_moved = level_exchange(after(text_own, frame_branches[0]))
    feed_own = total_of(feed_moved)
    middle_own = total_of(after(middle_moved, last[1][0]))
    middle_own = low(middle_own).reshape(block, size, -1).swapaxes(0, 1)
    middle_sum = jnp.sum(wide(level_exchange(by_distance(middle_own, level))), axis=0)
    out_frames = place_rows(place, frames, ones, after(branches, last[1][0]))
    frame_grads = place_rows(place, cotangent, live, frame_branches)
    qkv_own = total_of(qkv_moved)
    text_own_grad = qkv_own[:, TEXT_LANE:]
    text_grad = jnp.sum(wide(text_moved), axis=0).reshape(batches, count // 2, -1)
    first_sums = [r[1] for r in last]

    norm_sums = jnp.concatenate([sum(first_sums), sum(r[6] for r in later)], axis=0)
    norm_sums = norm_sums.reshape(6, 8, block).swapaxes(0, 1).reshape(8, 6 * block)
    norm_near, norm_far = disassemble(norm_sums, index)
    norm_own = norm_near[:, 0] + plane_move(norm_far[:, 0], 1, 0, 0)
    norm_total = norm_own[0]
    for spot, (y, x) in enumerate(((0, 1), (1, 0), (1, 1))):
        norm_total = norm_total + plane_move(norm_own[spot + 1], 0, y, x)
    norm_total = sum(z_gather(norm_total)).reshape(6, block)

    first = [unpack_heads(qkv_own[:, :640]), unpack_heads(qkv_own[:, 640:TEXT_LANE])]
    q_own, k_own, v_own = (jnp.concatenate([a, b], axis=1) for a, b in zip(*first))
    so_own = jnp.concatenate(
        [unpack_mixed(middle_sum[:, 384:640]), unpack_mixed(middle_sum[:, 640:896])], axis=1
    )
    return (
        out_frames,
        frame_grads,
        text_grad[:, None],
        norm_total[0],
        norm_total[1],
        norm_total[2],
        norm_total[3],
        norm_total[4],
        norm_total[5],
        q_own,
        k_own,
        v_own,
        so_own.T,
        middle_sum[:, :384],
        text_own_grad[:, :384],
        text_own_grad[:, 384:],
        middle_sum[:, 896:].T,
        feed_own[:, :ff],
        feed_own[:, ff:].T,
    )


def per_device(mesh):
    sizes = dict(mesh.shape)

    def dispatch(*args):
        frames, self_query, hidden_up = args[0], args[10], args[18]
        fits = (
            sizes[DATA] == 4
            and sizes[SIDES] == 2
            and sizes[LEVELS] == 4
            and frames.shape[0] == 2
            and frames.shape[1] == 1
            and frames.shape[2] % (16 * sizes[LEVELS]) == 0
            and self_query.shape[1] == 6 * HD
            and self_query.shape[0] * 8 == frames.shape[3]
        )
        return (shards if fits else general_shards)(*args)

    return dispatch


def solution(mesh):
    return jax.shard_map(
        per_device(mesh),
        mesh=mesh,
        in_specs=(
            P(None, DATA, SIDES, None),
            P(None, DATA, None, None),
            P(None, DATA, SIDES, None),
            P(None, DATA),
            P((DATA, SIDES)),
            P((DATA, SIDES)),
            P((DATA, SIDES)),
            P((DATA, SIDES)),
            P((DATA, SIDES)),
            P((DATA, SIDES)),
            P((DATA, SIDES), LEVELS),
            P((DATA, SIDES), LEVELS),
            P((DATA, SIDES), LEVELS),
            P(LEVELS, (DATA, SIDES)),
            P((DATA, SIDES), LEVELS),
            P((DATA, SIDES), LEVELS),
            P((DATA, SIDES), LEVELS),
            P(LEVELS, (DATA, SIDES)),
            P((DATA, SIDES), LEVELS),
            P(LEVELS, (DATA, SIDES)),
        ),
        out_specs=(
            P(None, DATA, SIDES, None),
            P(None, DATA, SIDES, None),
            P(None, DATA, SIDES, LEVELS),
            P((DATA, SIDES)),
            P((DATA, SIDES)),
            P((DATA, SIDES)),
            P((DATA, SIDES)),
            P((DATA, SIDES)),
            P((DATA, SIDES)),
            P((DATA, SIDES), LEVELS),
            P((DATA, SIDES), LEVELS),
            P((DATA, SIDES), LEVELS),
            P(LEVELS, (DATA, SIDES)),
            P((DATA, SIDES), LEVELS),
            P((DATA, SIDES), LEVELS),
            P((DATA, SIDES), LEVELS),
            P(LEVELS, (DATA, SIDES)),
            P((DATA, SIDES), LEVELS),
            P(LEVELS, (DATA, SIDES)),
        ),
        check_vma=False,
    )
```
